32 devices in a mesh: row: 16 (over z, y, x), col: 2 (over core).
Axes of the slice: x: 2, y: 2, z: 4, core: 2. Of those that a mesh axis runs over, the one named last changes fastest.
Arguments:
- block_input: bfloat16 [16384, 1024], P(('row', 'col')), may hold values from -6 to 6
- teacher: bfloat16 [16384, 1024], P(('row', 'col')), may hold values from -6 to 6
- lengths: int32 [16], P('row'), may hold values from 256 to 1024, as said below
- head_routes: int32 [16384, 4, 2], P(('row', 'col')), may hold values from 0 to 4, all different within a row
- expert_routes: int32 [16384, 16], P('row'), may hold values from 0 to 31, all different within a row; in each aligned block of 1024 rows (0 to 1023, 1024 to 2047, ...) at most 768 rows name the same one
- first_gain: bfloat16 [1024], P(('row', 'col')), may hold values from 0.5 to 1.5
- query_weight: bfloat16 [1024, 512], P(('row', 'col')), may hold values from -0.1875 to 0.1875
- key_weight: bfloat16 [1024, 512], P(('row', 'col')), may hold values from -0.1875 to 0.1875
- value_weight: bfloat16 [1024, 2560], P(('row', 'col')), may hold values from -0.1875 to 0.1875
- head_router: bfloat16 [1024, 40], P(('row', 'col')), may hold values from -0.3125 to 0.3125
- output_weight: bfloat16 [2560, 1024], P(None, ('row', 'col')), may hold values from -4 to 4
- second_gain: bfloat16 [1024], P(('row', 'col')), may hold values from 0.5 to 1.5
- expert_router: bfloat16 [1024, 32], P('row', 'col'), may hold values from -0.21875 to 0.21875
- expert_up: bfloat16 [32, 1024, 128], P('col', 'row'), may hold values from -0.1875 to 0.1875
- expert_down: bfloat16 [32, 128, 1024], P('col', None, 'row'), may hold values from -0.5 to 0.5
Outputs:
- block_output: bfloat16 [16384, 1024], P(('row', 'col'))
- input_grad: float32 [16384, 1024], P(('row', 'col'))
- first_gain_grad: float32 [1024], P(('row', 'col'))
- query_weight_grad: float32 [1024, 512], P(('row', 'col'))
- key_weight_grad: float32 [1024, 512], P(('row', 'col'))
- value_weight_grad: float32 [1024, 2560], P(('row', 'col'))
- head_router_grad: float32 [1024, 40], P(('row', 'col'))
- output_weight_grad: float32 [2560, 1024], P(None, ('row', 'col'))
- second_gain_grad: float32 [1024], P(('row', 'col'))
- expert_router_grad: float32 [1024, 32], P('row', 'col')
- expert_up_grad: float32 [32, 1024, 128], P('col', 'row')
- expert_down_grad: float32 [32, 128, 1024], P('col', None, 'row')
The draws below stay inside these ranges and needn't reach their ends.
Inputs may be any that keep to these rules, and one draw needn't show every extreme that they name: `lengths`: every sequence is at most 1024 long and some sequence is exactly 1024 long; some is 256 long. `head_routes`: the 2 experts of one token in one head are different. `expert_routes`: the 16 experts of one token are different. In each aligned block of 1024 rows (the tokens of one index of row), no expert is named by more than 768 rows, a bound that some block reaches.
All inputs are finite; a program needn't handle non-finite values.
Results may differ from the reference program's by a relative error of at most 0.025.
The reference program's roundings to bfloat16 on the way count: a program that leaves them out, or rounds other values in their place, can miss the bound.
Values may be sent and summed in bfloat16 or wider, within the bound.
A program may use at most 384 MiB of HBM per device.

```python
import math
import jax
import jax.numpy as jnp
import numpy as np
from jax import lax

D = 1024
H = 4
DH = 128
AEXP = 5
AK = 2
G = 128
TOPK = 16
GROUP_TOK = 1024
SEQ_LEN = 1024
SEQS = 16
TOKENS = 16384
EXPERTS = 32
CAP = 768


def draw_lengths(key, part):
    drawn = jax.random.randint(key, (SEQS,), SEQ_LEN // 4, SEQ_LEN + 1, dtype=jnp.int32)
    drawn = drawn.at[0].set(SEQ_LEN)
    return drawn.at[SEQS - 1].set(SEQ_LEN // 4).astype(jnp.int32)


def shard_levels(rng, extent, shards, smallest, top_value):
    level, own = 1.0, jax.random.fold_in(rng, 6)
    for dim, blocks in shards:
        draws = jnp.exp(jax.random.uniform(jax.random.fold_in(own, dim), (blocks,), jnp.float32, smallest / len(shards), top_value / len(shards)))
        level = level * jnp.repeat(draws, extent[dim] // blocks).reshape([-1 if axis == dim else 1 for axis in range(len(extent))])
    return level


def different_ones(rng, rows, number_of, top, lift):
    sequence = jax.random.permutation(jax.random.fold_in(rng, 1), number_of)
    pull = sequence
    for power in range(3):
        pull = pull * pull // number_of
    pull = pull * lift // number_of
    tickets = jax.random.randint(jax.random.fold_in(rng, 2), (rows, number_of), 0, 4096) + pull
    holders = jax.random.permutation(jax.random.fold_in(rng, 3), rows)[jnp.arange(number_of) % rows]
    tickets = jnp.where(jnp.arange(rows)[:, None] == holders[None, :], 1 << 14, tickets)
    merit = tickets * number_of + jnp.arange(number_of)
    return lax.top_k(merit.astype(jnp.int32), top)[1].astype(jnp.int32)


def deal_out(own_key, own, number, rows, number_of, top, limit, lean):
    sequence = jax.random.permutation(own_key, number_of)
    packed, common = shares(number_of, rows * top, limit, lean, True), shares(number_of, rows * top, limit, lean, False)
    places = jnp.arange(number_of)

    def named(sizes, turn):
        used = int((sizes > 0).sum())
        fixed = max(1, used // 4)
        passed = fixed + (places - fixed + turn * (used - fixed)) % max(1, number_of - fixed)
        return jnp.zeros((number_of,), jnp.int32).at[sequence[jnp.where(places < fixed, places, passed)]].set(jnp.asarray(sizes, jnp.int32))

    sizes = jnp.where(number % 4 == 0, named(packed, number // 4), named(common, number - number // 4 - 1))
    mixed = jax.random.permutation(jax.random.fold_in(own, 3), number_of)
    donor, taker = mixed[0:number_of // 2 * 2:2], mixed[1:number_of // 2 * 2:2]
    margin = jnp.minimum(sizes[donor] - 1, limit - sizes[taker]) // 2
    margin = jnp.where((donor == sequence[0]) | (taker == sequence[0]) | (sizes[taker] == 0), 0, jnp.maximum(margin, 0))
    passed = jax.random.randint(jax.random.fold_in(own, 4), (number_of // 2,), 0, 1 << 20) % (margin + 1)
    sizes = sizes.at[donor].add(-passed).at[taker].add(passed)
    members = jnp.searchsorted(jnp.cumsum(sizes), jnp.arange(rows * top), side="right").astype(jnp.int32)
    listing = members.reshape(top, rows).T
    listing = listing[jax.random.permutation(jax.random.fold_in(own, 1), rows)]
    turn = jax.random.randint(jax.random.fold_in(own, 2), (rows, 1), 0, top)
    return jnp.take_along_axis(listing, (jnp.arange(top)[None, :] + turn) % top, axis=1)


def shares(count, total, bound, lean, full):
    weights = [(1 << 20) // math.isqrt(rank ** lean) + 1 for rank in range(1, count + 1)]
    largest = bound if full else min(bound, max(-(-total // count), total * weights[0] // sum(weights)))
    least = 1 if total - largest >= count - 1 else 0
    given, surplus = [largest] + [least] * (count - 1), total - largest - least * (count - 1)
    while surplus > 0:
        candidates = [i for i in range(1, count) if given[i] < largest] or [i for i in range(1, count) if given[i] < bound]
        whole, remaining = sum([weights[i] for i in candidates]), surplus
        for i in candidates:
            extra = min(bound - given[i], max(1, remaining * weights[i] // whole), surplus)
            given[i] = given[i] + extra
            surplus = surplus - extra
    return np.array(given)


def scatter_about(rng, extent, deviation, reach, pieces=(), held_as=jnp.bfloat16):
    values = deviation * jax.random.normal(rng, extent, jnp.float32)
    if pieces:
        values = values * shard_levels(rng, extent, pieces, -0.22, 0.18)
    return jnp.clip(values, -reach, reach).astype(held_as)


def setup_inputs(seed: int = 0) -> dict:
    key_of = jax.random.split(jax.random.key(seed), 16)
    block_input = scatter_about(key_of[0], (TOKENS, D), 1.0, 6.0, ((0, 32),))
    teacher = scatter_about(key_of[1], (TOKENS, D), 1.0, 6.0, ((0, 32),))
    lengths = draw_lengths(jax.random.fold_in(key_of[15], 71), 0)
    head_routes = different_ones(key_of[3], TOKENS * H, AEXP, AK, 0).reshape((TOKENS, H, AK))
    expert_routes_keys = jax.random.split(jax.random.fold_in(key_of[4], 1), TOKENS // GROUP_TOK)
    expert_routes_turns = jax.random.permutation(jax.random.fold_in(key_of[4], 3), TOKENS // GROUP_TOK)
    expert_routes = jax.vmap(lambda own, number: deal_out(jax.random.fold_in(key_of[4], 2), own, number, GROUP_TOK, EXPERTS, TOPK, CAP, 1))(expert_routes_keys, expert_routes_turns).reshape((TOKENS, TOPK))
    first_gain = jnp.clip(1.0 + 0.1 * jax.random.normal(key_of[5], (D,), jnp.float32), 0.5, 1.5).astype(jnp.bfloat16)
    query_weight = scatter_about(key_of[6], (D, H * DH), D ** -0.5, 0.1875, ((0, 32),))
    key_weight = scatter_about(key_of[7], (D, H * DH), D ** -0.5, 0.1875, ((0, 32),))
    value_weight = scatter_about(key_of[8], (D, H * AEXP * DH), D ** -0.5, 0.1875, ((0, 32),))
    head_router = scatter_about(key_of[9], (D, 2 * H * AEXP), 0.022, 0.3125, ((0, 32),))
    output_weight = scatter_about(key_of[10], (H * AEXP * DH, D), 2 ** -0.5, 4.0, ((1, 32),))
    second_gain = jnp.clip(1.0 + 0.1 * jax.random.normal(key_of[11], (D,), jnp.float32), 0.5, 1.5).astype(jnp.bfloat16)
    expert_router = scatter_about(key_of[12], (D, EXPERTS), 0.0156, 0.21875, ((0, 16), (1, 2)))
    expert_up = scatter_about(key_of[13], (EXPERTS, D, G), D ** -0.5, 0.1875, ((0, 2), (1, 16)))
    expert_down = scatter_about(key_of[14], (EXPERTS, G, D), G ** -0.5, 0.5, ((0, 2), (2, 16)))
    return {"block_input": block_input, "teacher": teacher, "lengths": lengths, "head_routes": head_routes, "expert_routes": expert_routes, "first_gain": first_gain, "query_weight": query_weight, "key_weight": key_weight, "value_weight": value_weight, "head_router": head_router, "output_weight": output_weight, "second_gain": second_gain, "expert_router": expert_router, "expert_up": expert_up, "expert_down": expert_down}


@jax.custom_vjp
def low(v):
    return lax.optimization_barrier(v.astype(jnp.bfloat16)).astype(jnp.float32)

@jax.custom_vjp
def low_back(v):
    return v

def low_keep(v):
    return (low(v), None)

def low_pass(kept, grad):
    return (grad,)

def back_keep(v):
    return (v, None)

def back_low(kept, grad):
    return (low(grad),)
low.defvjp(low_keep, low_pass)
low_back.defvjp(back_keep, back_low)
EPS = 1e-05
MASKED = -1e+30
pair_block = 256

def exact_dot(left, right):
    return jnp.dot(left, right, precision=lax.Precision.HIGHEST, preferred_element_type=jnp.float32)

def norm_rows(values, gain):
    average = lax.optimization_barrier(jnp.mean(values, axis=-1, keepdims=True))
    centred = values - average
    spread = lax.optimization_barrier(jnp.mean(centred * centred, axis=-1, keepdims=True))
    return centred * lax.rsqrt(spread + EPS) * gain

def rope_tables(positions, width):
    half_width = width // 2
    freq = jnp.exp(jnp.arange(half_width).astype(jnp.float32) * (-2.0 * math.log(10000.0) / width))
    angle = positions.astype(jnp.float32)[:, None] * freq[None, :]
    return (jnp.cos(angle), jnp.sin(angle))

def rotate(values, cosine, sines):
    half_width = values.shape[-1] // 2
    front_half = values[..., :half_width]
    back_half = values[..., half_width:]
    cos_part = cosine[:, None, :]
    sin_part = sines[:, None, :]
    return jnp.concatenate([front_half * cos_part - back_half * sin_part, back_half * cos_part + front_half * sin_part], axis=-1)

def attend_one(parts):
    queries, keys, values, seq_length = parts
    positions = jnp.arange(SEQ_LEN, dtype=jnp.int32)
    allowed = (positions[None, :] <= positions[:, None]) & (positions[None, :] < seq_length)
    scores = low_back(jnp.einsum('qhd,khd->hqk', queries, keys, precision=lax.Precision.HIGHEST))
    scores = jnp.where(allowed[None], scores, MASKED)
    row_top = lax.optimization_barrier(jnp.max(scores, axis=2, keepdims=True))
    exponent = jnp.exp(scores - row_top)
    probs = low(exponent / lax.optimization_barrier(jnp.sum(exponent, axis=2, keepdims=True)))
    return jnp.einsum('hqk,khd->qhd', probs, values, precision=lax.Precision.HIGHEST)

def expert_mix(resid_low, gates, expert_up, expert_down, routes):
    row_total = resid_low.shape[0]
    pair_count = row_total * TOPK
    flat_experts = routes.reshape(-1).astype(jnp.int32)
    pair_rows = jnp.arange(pair_count, dtype=jnp.int32) // TOPK
    loads = jnp.zeros((EXPERTS,), jnp.int32).at[flat_experts].add(1)
    blocks = (loads + pair_block - 1) // pair_block
    block_end = jnp.cumsum(blocks)
    block_begin = block_end - blocks
    load_begin = jnp.cumsum(loads) - loads
    order = jnp.argsort(flat_experts, stable=True).astype(jnp.int32)
    sorted_experts = flat_experts[order]
    ranks = jnp.arange(pair_count, dtype=jnp.int32) - load_begin[sorted_experts]
    slots = block_begin[sorted_experts] * pair_block + ranks
    block_total = (pair_count + pair_block - 1) // pair_block + EXPERTS
    slot_total = block_total * pair_block
    slot_rows = jnp.zeros((slot_total,), jnp.int32).at[slots].set(pair_rows[order])
    slot_live = jnp.zeros((slot_total,), jnp.float32).at[slots].set(1.0)
    block_ids = jnp.arange(block_total, dtype=jnp.int32)
    block_expert = jnp.minimum(lax.optimization_barrier(jnp.sum((block_end[None, :] <= block_ids[:, None]).astype(jnp.int32), axis=1)), EXPERTS - 1).astype(jnp.int32)
    slot_expert = jnp.repeat(block_expert, pair_block)
    slot_gate = gates[slot_rows, slot_expert] * slot_live
    rows_in = resid_low[slot_rows].reshape(block_total, pair_block, resid_low.shape[1])

    def one_block(parts):
        rows, expert_id, gate_rows = parts
        inner = low_back(exact_dot(rows, expert_up[expert_id]))
        active = low(jnp.where(inner > 0, inner, 0.0))
        return low_back(exact_dot(active, expert_down[expert_id])) * gate_rows[:, None]
    results = lax.map(jax.checkpoint(one_block), (rows_in, block_expert, slot_gate.reshape(block_total, pair_block)))
    return jnp.zeros_like(resid_low).at[slot_rows].add(results.reshape(slot_total, resid_low.shape[1]))

def block_loss(inputs, first_gain, query_weight, key_weight, value_weight, head_router, output_weight, second_gain, expert_router, expert_up, expert_down, teacher, lengths, head_routes, expert_routes):
    row_total = inputs.shape[0]
    row_ids = jnp.arange(row_total, dtype=jnp.int32)
    seq_pos = row_ids % SEQ_LEN
    seq_ids = row_ids // SEQ_LEN
    valid = (seq_pos < lengths[seq_ids]).astype(jnp.float32)
    normed_one = low(norm_rows(inputs, first_gain))
    query_raw = low_back(exact_dot(normed_one, query_weight))
    key_raw = low_back(exact_dot(normed_one, key_weight))
    cosine, sines = rope_tables(seq_pos, DH)
    queries = low(rotate(query_raw.reshape(row_total, H, DH), cosine, sines) * DH ** (-0.5))
    keys = low(rotate(key_raw.reshape(row_total, H, DH), cosine, sines))
    route_logits = low_back(exact_dot(normed_one, head_router))
    chosen = jnp.any(head_routes[:, :, :, None] == jnp.arange(AEXP, dtype=jnp.int32)[None, None, None, :], axis=2).astype(jnp.float32)
    value_gates = jax.nn.sigmoid(route_logits[:, :H * AEXP]).reshape(row_total, H, AEXP) * chosen
    output_gates = jax.nn.sigmoid(route_logits[:, H * AEXP:]).reshape(row_total, H, AEXP) * chosen
    value_all = low_back(exact_dot(inputs, value_weight)).reshape(row_total, H, AEXP, DH)
    values = low(lax.optimization_barrier(jnp.sum(value_all * value_gates[..., None], axis=2)))
    attended = lax.map(jax.checkpoint(attend_one), (queries.reshape(SEQS, SEQ_LEN, H, DH), keys.reshape(SEQS, SEQ_LEN, H, DH), values.reshape(SEQS, SEQ_LEN, H, DH), lengths))
    attended = low_back(attended.reshape(row_total, H, DH))
    mixed = low_back(low(attended[:, :, None, :] * output_gates[..., None])).reshape(row_total, H * AEXP * DH)
    resid = inputs + low_back(exact_dot(mixed, output_weight))
    resid_low = low(resid)
    normed_two = low(norm_rows(resid_low, second_gain))
    expert_gates = jax.nn.sigmoid(low_back(exact_dot(normed_two, expert_router)))
    output_full = resid + low_back(expert_mix(resid_low, expert_gates, expert_up, expert_down, expert_routes))
    ratio = TOKENS / jnp.sum(lengths).astype(jnp.float32)
    error = (output_full - teacher) * valid[:, None]
    return (0.5 * ratio * jnp.sum(error * error), output_full)

def reference(block_input, teacher, lengths, head_routes, expert_routes, first_gain, query_weight, key_weight, value_weight, head_router, output_weight, second_gain, expert_router, expert_up, expert_down):
    teacher_full = teacher.astype(jnp.float32)

    def loss_of(inputs, gain_one, w_query, w_key, w_value, router_head, w_output, gain_two, router_expert, up_experts, down_experts):
        return block_loss(inputs, gain_one, w_query, w_key, w_value, router_head, w_output, gain_two, router_expert, up_experts, down_experts, teacher_full, lengths, head_routes, expert_routes)
    loss, pullback, output_full = jax.vjp(loss_of, block_input.astype(jnp.float32), first_gain.astype(jnp.float32), query_weight.astype(jnp.float32), key_weight.astype(jnp.float32), value_weight.astype(jnp.float32), head_router.astype(jnp.float32), output_weight.astype(jnp.float32), second_gain.astype(jnp.float32), expert_router.astype(jnp.float32), expert_up.astype(jnp.float32), expert_down.astype(jnp.float32), has_aux=True)
    grads = pullback(jnp.ones((), jnp.float32))
    return (output_full.astype(jnp.bfloat16), grads[0], grads[1], grads[2], grads[3], grads[4], grads[5], grads[6], grads[7], grads[8], grads[9], grads[10])
```

```python
import math

import jax
import jax.numpy as jnp
from jax import lax
from jax.sharding import PartitionSpec as P

H = 4
DH = 128
AEXP = 5
MAXLEN = 2048


EPS = 1e-05
MASKED = -1e30


def shifted(value, axis, steps):
    count = lax.axis_size(axis)
    leading, last = (max(0, -steps), min(count, count - steps))
    return lax.ppermute(value, axis, [(source, source + steps) for source in range(leading, last)])


def contract_last(left, right):
    return lax.dot_general(
        left, right, (((1,), (1,)), ((), ())), preferred_element_type=jnp.float32
    )


def contract_first(left, right):
    return lax.dot_general(
        left, right, (((0,), (0,)), ((), ())), preferred_element_type=jnp.float32
    )


GRID = (4, 2, 2)
ORDER_A, ORDER_B, ORDER_C = ((0, 1, 2), (1, 2, 0), (2, 0, 1))


def by_grid():
    return lax.axis_size("row") == math.prod(GRID) and lax.axis_size("col") == 2


def grid_place(dim):
    row = lax.axis_index("row")
    return (row // 4, (row // 2) % 2, row % 2)[dim]


def grid_pairs(dim, steps):
    pairs = []
    for row in range(math.prod(GRID)):
        place = [row // 4, (row // 2) % 2, row % 2]
        place[dim] = (place[dim] + steps) % GRID[dim]
        pairs.append((row, (place[0] * 2 + place[1]) * 2 + place[2]))
    return pairs


def sibling(value):
    return lax.ppermute(value, "col", [(0, 1), (1, 0)])


def gather_row(part, order):
    if not by_grid():
        return lax.all_gather(part, "row", axis=0, tiled=True)
    held = part.reshape((1, 1, 1) + part.shape)
    for dim in order:
        size, place = (GRID[dim], grid_place(dim))
        came = [lax.ppermute(held, "row", grid_pairs(dim, k)) for k in range(1, size)]
        shape = list(held.shape)
        shape[dim] = size
        whole = lax.dynamic_update_slice_in_dim(jnp.zeros(shape, held.dtype), held, place, dim)
        for k, block in zip(range(1, size), came):
            whole = lax.dynamic_update_slice_in_dim(whole, block, (place - k) % size, dim)
        held = whole
    return held.reshape((-1,) + part.shape[1:])


def gather_all(part, order):
    if not by_grid():
        return lax.all_gather(part, ("row", "col"), axis=0, tiled=True)
    rows, wide = part.shape
    mine = gather_row(part, order).reshape(-1, 1, rows, wide)
    other = sibling(mine)
    core = lax.axis_index("col")
    whole = lax.dynamic_update_slice_in_dim(
        jnp.zeros((mine.shape[0], 2, rows, wide), part.dtype), mine, core, 1
    )
    whole = lax.dynamic_update_slice_in_dim(whole, other, 1 - core, 1)
    return whole.reshape(-1, wide)


def scatter_row(total, order):
    if not by_grid():
        return lax.psum_scatter(total, "row", scatter_dimension=0, tiled=True)
    rows = total.shape[0] // math.prod(GRID)
    held = total.reshape(GRID + (rows, total.shape[1]))
    for dim in order[::-1]:
        size, place = (GRID[dim], grid_place(dim))
        own = lax.dynamic_slice_in_dim(held, place, 1, dim).astype(jnp.float32)
        for k in range(1, size):
            leaving = lax.dynamic_slice_in_dim(held, (place + k) % size, 1, dim)
            came = lax.ppermute(leaving.astype(jnp.bfloat16), "row", grid_pairs(dim, k))
            own = own + came.astype(jnp.float32)
        held = own
    return held.reshape(rows, total.shape[1])


def scatter_all(total, order):
    if not by_grid():
        return lax.psum_scatter(total, ("row", "col"), scatter_dimension=0, tiled=True)
    rows = total.shape[0] // (2 * math.prod(GRID))
    core = lax.axis_index("col")
    split = total.reshape(-1, 2, rows, total.shape[1])
    mine = lax.dynamic_slice_in_dim(split, core, 1, 1)
    leaving = lax.dynamic_slice_in_dim(split, 1 - core, 1, 1).astype(jnp.bfloat16)
    summed = mine + sibling(leaving).astype(jnp.float32)
    return scatter_row(summed.reshape(-1, total.shape[1]), order)


def gather_col(value):
    if lax.axis_size("col") != 2:
        return lax.all_gather(value, "col", axis=0, tiled=True)
    core = lax.axis_index("col")
    rows = value.shape[0]
    whole = jnp.zeros((2 * rows,) + value.shape[1:], value.dtype)
    whole = lax.dynamic_update_slice_in_dim(whole, value, core * rows, 0)
    return lax.dynamic_update_slice_in_dim(whole, sibling(value), (1 - core) * rows, 0)


def scatter_col(total):
    if lax.axis_size("col") != 2:
        return lax.psum_scatter(total, "col", scatter_dimension=0, tiled=True)
    core = lax.axis_index("col")
    rows = total.shape[0] // 2
    leaving = lax.dynamic_slice_in_dim(total, (1 - core) * rows, rows, 0).astype(jnp.bfloat16)
    mine = lax.dynamic_slice_in_dim(total, core * rows, rows, 0)
    return mine + sibling(leaving).astype(jnp.float32)


def padded(value, wide):
    return jnp.pad(value, ((0, 0), (0, wide - value.shape[1])))


def norm_parts(values, gain):
    average = jnp.mean(values, axis=-1, keepdims=True)
    centred = values - average
    inv_std = lax.rsqrt(jnp.mean(centred * centred, axis=-1, keepdims=True) + EPS)
    normed = centred * inv_std
    return (normed * gain, normed, inv_std)


def norm_back(grad_in, gain, normed, inv_std):
    grad_hat = grad_in * gain
    mean_one = jnp.mean(grad_hat, axis=-1, keepdims=True)
    mean_two = jnp.mean(grad_hat * normed, axis=-1, keepdims=True)
    return inv_std * (grad_hat - mean_one - normed * mean_two)


def rope_tables(positions, width):
    half_width = width // 2
    freq = jnp.exp(jnp.arange(half_width).astype(jnp.float32) * (-2.0 * math.log(10000.0) / width))
    angle = positions.astype(jnp.float32)[:, None] * freq[None, :]
    return (jnp.cos(angle), jnp.sin(angle))


def rotate(values, cosine, sines):
    half_width = values.shape[-1] // 2
    front_half = values[..., :half_width]
    back_half = values[..., half_width:]
    cos_part = cosine[:, None, :]
    sin_part = sines[:, None, :]
    return jnp.concatenate(
        [
            front_half * cos_part - back_half * sin_part,
            back_half * cos_part + front_half * sin_part,
        ],
        axis=-1,
    )


def unrotate(values, cosine, sines):
    half_width = values.shape[-1] // 2
    front_half = values[..., :half_width]
    back_half = values[..., half_width:]
    cos_part = cosine[:, None, :]
    sin_part = sines[:, None, :]
    return jnp.concatenate(
        [
            front_half * cos_part + back_half * sin_part,
            back_half * cos_part - front_half * sin_part,
        ],
        axis=-1,
    )


def shards(
    block_input,
    teacher,
    lengths,
    head_routes,
    expert_routes,
    first_gain,
    query_weight,
    key_weight,
    value_weight,
    head_router,
    output_weight,
    second_gain,
    expert_router,
    expert_up,
    expert_down,
):
    tok_rows = block_input.shape[0]
    width = block_input.shape[1]
    col_count = lax.axis_size("col")
    col_index = lax.axis_index("col")
    total_rows = tok_rows * lax.axis_size("row") * col_count
    group_size = tok_rows * col_count
    seq_length = min(MAXLEN, group_size)
    key_span = seq_length // tok_rows
    gated = H * AEXP
    half_heads = gated * DH // 2
    local_experts = expert_up.shape[0]
    hidden_local = expert_up.shape[2]
    hidden = local_experts * hidden_local
    length_sum = jnp.sum(lengths)
    small_parts = [
        query_weight,
        key_weight,
        head_router,
        first_gain[:, None],
        second_gain[:, None],
    ]
    for digits in (length_sum // 64, length_sum % 64):
        small_parts.append(
            jnp.broadcast_to(digits.astype(jnp.bfloat16)[None, None], (first_gain.shape[0], 1))
        )
    lead_local = padded(jnp.concatenate(small_parts, axis=1), 2 * H * DH + 128)
    lead_full = gather_all(lead_local, ORDER_B)
    value_one = gather_all(value_weight[:, :half_heads], ORDER_A)
    value_two = gather_all(value_weight[:, half_heads:], ORDER_C)
    up_local = jnp.concatenate(
        [
            jnp.transpose(expert_up, (1, 0, 2)).reshape(-1, hidden),
            padded(expert_router, 128),
        ],
        axis=1,
    )
    down_local = jnp.transpose(expert_down, (2, 0, 1)).reshape(-1, hidden)
    output_turned = gather_all(output_weight.T, ORDER_B)
    up_wide = gather_row(up_local, ORDER_A)
    down_turned = gather_row(down_local, ORDER_C)
    up_full = up_wide[:, :hidden]
    router_cols = up_wide[:, hidden : hidden + local_experts]
    query_full = lead_full[:, : H * DH]
    key_full = lead_full[:, H * DH : 2 * H * DH]
    router_full = lead_full[:, 2 * H * DH : 2 * H * DH + 2 * gated]
    extra = lead_full[:, 2 * H * DH + 2 * gated :].astype(jnp.float32)
    gain_one = extra[:, 0]
    gain_two = extra[:, 1]
    stride = first_gain.shape[0] * col_count
    token_count = jnp.sum(extra[::stride, 2]) * 64.0 + jnp.sum(extra[::stride, 3])
    local_ids = jnp.arange(tok_rows, dtype=jnp.int32)
    group_ids = col_index * tok_rows + local_ids
    seq_pos = group_ids % seq_length
    seq_ids = group_ids // seq_length
    seq_slots = jnp.arange(lengths.shape[0], dtype=jnp.int32)
    tok_length = jnp.sum(
        jnp.where(seq_ids[:, None] == seq_slots[None, :], lengths[None, :], 0), axis=1
    )
    valid = (seq_pos < tok_length).astype(jnp.float32)
    inputs_full = block_input.astype(jnp.float32)
    normed_one, hat_one, inv_one = norm_parts(inputs_full, gain_one)
    normed_low = normed_one.astype(jnp.bfloat16)
    query_raw = jnp.dot(normed_low, query_full, preferred_element_type=jnp.float32)
    key_raw = jnp.dot(normed_low, key_full, preferred_element_type=jnp.float32)
    cosine, sines = rope_tables(seq_pos, DH)
    query_scale = DH ** (-0.5)
    query_rot = (rotate(query_raw.reshape(tok_rows, H, DH), cosine, sines) * query_scale).astype(
        jnp.bfloat16
    )
    key_rot = rotate(key_raw.reshape(tok_rows, H, DH), cosine, sines).astype(jnp.bfloat16)
    route_logits = jnp.dot(normed_low, router_full, preferred_element_type=jnp.float32)
    chosen = jnp.any(
        head_routes[:, :, :, None] == jnp.arange(AEXP, dtype=jnp.int32)[None, None, None, :], axis=2
    ).astype(jnp.float32)
    value_sig = jax.nn.sigmoid(route_logits[:, :gated]).reshape(tok_rows, H, AEXP)
    output_sig = jax.nn.sigmoid(route_logits[:, gated:]).reshape(tok_rows, H, AEXP)
    value_gates = value_sig * chosen
    output_gates = output_sig * chosen
    value_all = jnp.concatenate(
        [
            jnp.dot(block_input, value_one, preferred_element_type=jnp.float32),
            jnp.dot(block_input, value_two, preferred_element_type=jnp.float32),
        ],
        axis=1,
    ).reshape(tok_rows, H, AEXP, DH)
    values_low = jnp.sum(value_all * value_gates[..., None], axis=2).astype(jnp.bfloat16)
    key_parts = [key_rot]
    value_parts = [values_low]
    id_parts = [group_ids]
    for offset in range(1, key_span):
        came_keys, came_values = shifted((key_rot, values_low), "col", offset)
        key_parts.append(came_keys)
        value_parts.append(came_values)
        id_parts.append(group_ids - offset * tok_rows)
    keys_all = jnp.concatenate(key_parts, axis=0)
    values_all = jnp.concatenate(value_parts, axis=0)
    key_ids = jnp.concatenate(id_parts, axis=0)
    allowed = (
        (key_ids[None, :] // seq_length == seq_ids[:, None])
        & (key_ids[None, :] <= group_ids[:, None])
        & (key_ids[None, :] % seq_length < tok_length[:, None])
    )

    def head_scores(head_idx):
        raw_scores = jnp.einsum(
            "qd,kd->qk",
            query_rot[:, head_idx],
            keys_all[:, head_idx],
            preferred_element_type=jnp.float32,
        )
        return jnp.where(allowed, raw_scores, MASKED)

    attended_list = []
    lse_list = []
    for head_idx in range(H):
        scores = head_scores(head_idx)
        row_top = jnp.max(scores, axis=1, keepdims=True)
        exponent = jnp.exp(scores - row_top)
        row_total = jnp.sum(exponent, axis=1, keepdims=True)
        probs_low = (exponent / row_total).astype(jnp.bfloat16)
        attended_list.append(
            jnp.dot(probs_low, values_all[:, head_idx], preferred_element_type=jnp.float32)
        )
        lse_list.append(row_top + jnp.log(row_total))
    attended = jnp.stack(attended_list, axis=1)
    mixed_low = (
        (attended[:, :, None, :] * output_gates[..., None])
        .astype(jnp.bfloat16)
        .reshape(tok_rows, gated * DH)
    )
    resid = inputs_full + contract_last(mixed_low, output_turned)
    resid_low = resid.astype(jnp.bfloat16)
    group_in = gather_col(resid_low)
    normed_two, hat_two, inv_two = norm_parts(group_in.astype(jnp.float32), gain_two)
    normed_two_low = normed_two.astype(jnp.bfloat16)
    gates = jax.nn.sigmoid(jnp.dot(normed_two_low, router_cols, preferred_element_type=jnp.float32))
    expert_ids = col_index * local_experts + jnp.arange(local_experts, dtype=jnp.int32)
    member = jnp.any(expert_routes[:, :, None] == expert_ids[None, None, :], axis=1)
    used_gates = gates * member.astype(jnp.float32)

    def spread(columns):
        return jnp.repeat(columns, hidden_local, axis=1)

    inner = jnp.dot(group_in, up_full, preferred_element_type=jnp.float32)
    active = jnp.maximum(inner, 0.0).astype(jnp.bfloat16)
    gated_active = (active.astype(jnp.float32) * spread(used_gates)).astype(jnp.bfloat16)
    expert_sum = scatter_col(contract_last(gated_active, down_turned))
    output_full_rows = resid + expert_sum
    block_output = output_full_rows.astype(jnp.bfloat16)
    ratio = total_rows / token_count
    grad_output = ratio * (output_full_rows - teacher.astype(jnp.float32)) * valid[:, None]
    grad_output_low = grad_output.astype(jnp.bfloat16)
    group_grad = gather_col(grad_output_low)
    grad_hidden = jnp.dot(group_grad, down_turned, preferred_element_type=jnp.float32)
    gate_grad = jnp.sum(
        (active.astype(jnp.float32) * grad_hidden).reshape(group_size, local_experts, hidden_local),
        axis=2,
    )
    grad_inner = jnp.where(active > 0, grad_hidden * spread(used_gates), 0.0).astype(jnp.bfloat16)
    down_grad = contract_first(group_grad, gated_active)
    up_grad = contract_first(group_in, grad_inner)
    slot_back = contract_last(grad_inner, up_full)
    logit_low = (gate_grad * used_gates * (1.0 - gates)).astype(jnp.bfloat16)
    router_grad = contract_first(normed_two_low, logit_low)
    grad_norm_two = contract_last(logit_low, router_cols)
    second_gain_part = jnp.sum(grad_norm_two * hat_two, axis=0)
    grad_rows = slot_back + norm_back(grad_norm_two, gain_two, hat_two, inv_two)
    moe_grad = scatter_col(grad_rows)
    up_sum = scatter_row(jnp.concatenate([up_grad, padded(router_grad, 128)], axis=1), ORDER_A)
    down_sum = scatter_row(down_grad, ORDER_C)
    router_sum = up_sum[:, hidden : hidden + local_experts]
    up_out = jnp.transpose(
        up_sum[:, :hidden].reshape(-1, local_experts, hidden_local), (1, 0, 2)
    )
    down_out = jnp.transpose(down_sum.reshape(-1, local_experts, hidden_local), (1, 2, 0))
    grad_resid = grad_output + moe_grad
    grad_branch = grad_resid.astype(jnp.bfloat16)
    output_grad = contract_first(grad_branch, mixed_low)
    output_sum = scatter_all(output_grad, ORDER_B).T
    grad_mixed = (
        jnp.dot(grad_branch, output_turned, preferred_element_type=jnp.float32)
        .astype(jnp.bfloat16)
        .astype(jnp.float32)
        .reshape(tok_rows, H, AEXP, DH)
    )
    grad_attended = jnp.sum(grad_mixed * output_gates[..., None], axis=2).astype(jnp.bfloat16)
    grad_output_gates = jnp.sum(grad_mixed * attended[:, :, None, :], axis=3)
    query_grads = []
    key_grads = []
    value_grads = []
    for head_idx in range(H):
        scores = head_scores(head_idx)
        probs_full = jnp.exp(scores - lse_list[head_idx])
        probs_low = probs_full.astype(jnp.bfloat16)
        grad_probs = jnp.einsum(
            "qd,kd->qk",
            grad_attended[:, head_idx],
            values_all[:, head_idx],
            preferred_element_type=jnp.float32,
        )
        grad_scores = (
            probs_full * (grad_probs - jnp.sum(probs_full * grad_probs, axis=1, keepdims=True))
        ).astype(jnp.bfloat16)
        query_grads.append(
            jnp.dot(grad_scores, keys_all[:, head_idx], preferred_element_type=jnp.float32)
        )
        key_grads.append(contract_first(grad_scores, query_rot[:, head_idx]))
        value_grads.append(contract_first(probs_low, grad_attended[:, head_idx]))
    grad_queries = jnp.stack(query_grads, axis=1)
    key_grads_all = jnp.stack(key_grads, axis=1)
    value_grads_all = jnp.stack(value_grads, axis=1)
    grad_key_rot = key_grads_all[:tok_rows]
    grad_values = value_grads_all[:tok_rows]
    for offset in range(1, key_span):
        back_keys, back_values = (
            shifted(
                key_grads_all[offset * tok_rows : (offset + 1) * tok_rows].astype(jnp.bfloat16),
                "col",
                -offset,
            ).astype(jnp.float32),
            shifted(
                value_grads_all[offset * tok_rows : (offset + 1) * tok_rows].astype(jnp.bfloat16),
                "col",
                -offset,
            ).astype(jnp.float32),
        )
        grad_key_rot = grad_key_rot + back_keys
        grad_values = grad_values + back_values
    grad_value_all = (
        (grad_values[:, :, None, :] * value_gates[..., None])
        .astype(jnp.bfloat16)
        .reshape(tok_rows, gated * DH)
    )
    grad_value_gates = jnp.sum(value_all * grad_values[:, :, None, :], axis=3)
    grad_query_raw = (
        unrotate(grad_queries * query_scale, cosine, sines)
        .astype(jnp.bfloat16)
        .reshape(tok_rows, H * DH)
    )
    grad_key_raw = (
        unrotate(grad_key_rot, cosine, sines).astype(jnp.bfloat16).reshape(tok_rows, H * DH)
    )
    grad_route = jnp.concatenate(
        [
            (grad_value_gates * chosen * value_sig * (1.0 - value_sig)).reshape(tok_rows, gated),
            (grad_output_gates * chosen * output_sig * (1.0 - output_sig)).reshape(tok_rows, gated),
        ],
        axis=1,
    ).astype(jnp.bfloat16)
    query_grad = contract_first(normed_low, grad_query_raw)
    key_grad = contract_first(normed_low, grad_key_raw)
    router_head_grad = contract_first(normed_low, grad_route)
    value_grad_one = contract_first(block_input, grad_value_all[:, :half_heads])
    value_grad_two = contract_first(block_input, grad_value_all[:, half_heads:])
    grad_norm_one = (
        contract_last(grad_query_raw, query_full)
        + contract_last(grad_key_raw, key_full)
        + contract_last(grad_route, router_full)
    )
    first_gain_part = jnp.sum(grad_norm_one * hat_one, axis=0)
    input_grad = (
        grad_resid
        + norm_back(grad_norm_one, gain_one, hat_one, inv_one)
        + contract_last(grad_value_all[:, :half_heads], value_one)
        + contract_last(grad_value_all[:, half_heads:], value_two)
    )
    lead_grad = padded(
        jnp.concatenate(
            [
                query_grad,
                key_grad,
                router_head_grad,
                first_gain_part[:, None],
                second_gain_part[:, None],
            ],
            axis=1,
        ),
        2 * H * DH + 128,
    )
    lead_sum = scatter_all(lead_grad, ORDER_B)
    value_sum = jnp.concatenate(
        [scatter_all(value_grad_one, ORDER_A), scatter_all(value_grad_two, ORDER_C)], axis=1
    )
    query_sum = lead_sum[:, : H * DH]
    key_sum = lead_sum[:, H * DH : 2 * H * DH]
    extra_at = 2 * H * DH + 2 * gated
    router_head_sum = lead_sum[:, 2 * H * DH : extra_at]
    first_sum = lead_sum[:, extra_at]
    second_sum = lead_sum[:, extra_at + 1]
    return (
        block_output,
        input_grad,
        first_sum,
        query_sum,
        key_sum,
        value_sum,
        router_head_sum,
        output_sum,
        second_sum,
        router_sum,
        up_out,
        down_out,
    )


def solution(mesh):
    return jax.shard_map(
        shards,
        mesh=mesh,
        in_specs=(
            P(("row", "col"), None),
            P(("row", "col"), None),
            P("row"),
            P(("row", "col"), None, None),
            P("row", None),
            P(("row", "col")),
            P(("row", "col"), None),
            P(("row", "col"), None),
            P(("row", "col"), None),
            P(("row", "col"), None),
            P(None, ("row", "col")),
            P(("row", "col")),
            P("row", "col"),
            P("col", "row", None),
            P("col", None, "row"),
        ),
        out_specs=(
            P(("row", "col"), None),
            P(("row", "col"), None),
            P(("row", "col")),
            P(("row", "col"), None),
            P(("row", "col"), None),
            P(("row", "col"), None),
            P(("row", "col"), None),
            P(None, ("row", "col")),
            P(("row", "col")),
            P("row", "col"),
            P("col", "row", None),
            P("col", None, "row"),
        ),
        check_vma=False,
    )
```

```python
import functools
import math

import jax
import jax.numpy as jnp
from jax import lax
from jax.experimental import pallas as pl
from jax.experimental.pallas import tpu as pltpu
from jax.sharding import PartitionSpec as P

H = 4
DH = 128
AEXP = 5
MAXLEN = 2048


EPS = 1e-05
MASKED = -1e30


def shifted(value, axis, steps):
    count = lax.axis_size(axis)
    leading, last = (max(0, -steps), min(count, count - steps))
    return lax.ppermute(value, axis, [(source, source + steps) for source in range(leading, last)])


def contract_last(left, right):
    return lax.dot_general(
        left, right, (((1,), (1,)), ((), ())), preferred_element_type=jnp.float32
    )


def contract_first(left, right):
    return lax.dot_general(
        left, right, (((0,), (0,)), ((), ())), preferred_element_type=jnp.float32
    )


GRID = (4, 2, 2)
MESH = pl.DeviceIdType.MESH
GATHER_PLAN = (
    (
        (3, 0, 1152, (2, 0, 1)),
        (4, 0, 768, (2, 1, 0)),
        (1, 0, 1280, (0, 1, 2)),
        (2, 0, 768, (0, 2, 1)),
        (3, 1152, 1024, (0, 1, 2)),
        (1, 1280, 1280, (0, 2, 1)),
        (2, 768, 1792, (0, 1, 2)),
        (0, 0, 1152, (0, 2, 1)),
        (4, 768, 1280, (0, 1, 2)),
    ),
    (
        (0, 0),
        (1, 0),
        (2, 0),
        (3, 0),
        (4, 0),
        (5, 0),
        (6, 0),
        (7, 0),
        (8, 0),
        (0, 1),
        (1, 1),
        (2, 1),
        (3, 1),
        (1, 2),
        (3, 2),
        (2, 2),
        (4, 1),
        (3, 3),
        (5, 1),
        (2, 3),
        (4, 2),
        (6, 1),
        (5, 2),
        (7, 1),
        (6, 2),
        (8, 1),
        (5, 3),
        (7, 2),
        (8, 2),
        (0, 2),
        (6, 3),
        (7, 3),
    ),
)
SCATTER_PLAN = (
    (
        (2, 0, 1664, (1, 2, 0)),
        (2, 1664, 896, (2, 0, 1)),
        (5, 0, 1152, (2, 0, 1)),
        (1, 0, 896, (2, 1, 0)),
        (4, 0, 128, (2, 0, 1)),
        (1, 896, 1664, (1, 2, 0)),
        (5, 1152, 896, (1, 2, 0)),
        (3, 0, 1408, (1, 2, 0)),
        (0, 0, 1152, (1, 2, 0)),
        (3, 1408, 640, (0, 1, 2)),
    ),
    (
        (2, 0),
        (4, 0),
        (6, 0),
        (7, 0),
        (9, 0),
        (0, 0),
        (1, 0),
        (3, 0),
        (5, 0),
        (8, 0),
        (6, 1),
        (2, 1),
        (4, 1),
        (9, 1),
        (1, 1),
        (3, 1),
        (7, 1),
        (2, 2),
        (4, 2),
        (6, 2),
        (1, 2),
        (0, 1),
        (7, 2),
        (0, 2),
        (5, 1),
        (5, 2),
        (8, 1),
        (9, 2),
        (3, 2),
        (8, 2),
    ),
)


def by_grid():
    return lax.axis_size("row") == math.prod(GRID) and lax.axis_size("col") == 2


def places():
    row = lax.axis_index("row")
    return (row // 4, (row // 2) % 2, row % 2)


def row_of(place):
    return (place[0] * 2 + place[1]) * 2 + place[2]


def moved(place, dim, steps):
    there = list(place)
    there[dim] = lax.rem(place[dim] + steps, GRID[dim])
    return row_of(there)


def greet(place, core):
    barrier = pltpu.get_barrier_semaphore()
    partners = [(moved(place, dim, k), core) for dim in range(3) for k in range(1, GRID[dim])]
    partners.append((row_of(place), 1 - core))
    for row, col in partners:
        pl.semaphore_signal(barrier, inc=1, device_id={"row": row, "col": col}, device_id_type=MESH)
    pl.semaphore_wait(barrier, len(partners))


def push(source, target, send, recv, row, core):
    copy = pltpu.make_async_remote_copy(
        source, target, send, recv, device_id={"row": row, "col": core}, device_id_type=MESH
    )
    copy.start()
    return copy


def gather_kernel(chunks, events, shared, *refs):
    count = len(shared)
    ins, outs = (refs[:count], refs[count : 2 * count])
    send, recv, local = refs[2 * count :]
    place, core = (places(), lax.axis_index("col"))
    greet(place, core)
    owns = []
    for n in range(count):
        at = tuple(place) + ((core,) if shared[n] else ())
        owns.append(pltpu.make_async_copy(ins[n], outs[n].at[at], local.at[n]))
        owns[-1].start()
    sent, flying = ([], {})
    waited = False
    for i, phase in events:
        which, start, wide, order = chunks[i]
        if phase == 1 and not waited:
            for copy in owns:
                copy.wait()
            waited = True
        for copy in flying.pop(i, []):
            copy.wait_recv()
        held = order[:phase]
        at = [slice(None) if dim in held else place[dim] for dim in range(3)]
        at += [core] if shared[which] else []
        block = outs[which].at[tuple(at) + (slice(None), pl.ds(start, wide))]
        if phase == 3:
            flying[i] = [push(block, block, send.at[i, 5], recv.at[i, 5], row_of(place), 1 - core)]
        else:
            dim = order[phase]
            source = ins[which].at[:, pl.ds(start, wide)] if phase == 0 else block
            slot = (0, 3, 4)[dim]
            flying[i] = [
                push(
                    source,
                    block,
                    send.at[i, slot + k - 1],
                    recv.at[i, slot + k - 1],
                    moved(place, dim, k),
                    core,
                )
                for k in range(1, GRID[dim])
            ]
        sent += flying[i]
    for copies in flying.values():
        for copy in copies:
            copy.wait_recv()
    for copy in sent:
        copy.wait_send()


def gather_parts(parts, shared, plan, collective_id):
    if not by_grid():
        return [
            lax.all_gather(part, ("row", "col") if both else "row", axis=0, tiled=True)
            for part, both in zip(parts, shared)
        ]
    chunks, events = plan
    count = len(parts)
    outs = pl.pallas_call(
        functools.partial(gather_kernel, chunks, events, shared),
        out_shape=[
            jax.ShapeDtypeStruct(GRID + ((2,) if both else ()) + part.shape, part.dtype)
            for part, both in zip(parts, shared)
        ],
        in_specs=[pl.BlockSpec(memory_space=pltpu.VMEM)] * count,
        out_specs=[pl.BlockSpec(memory_space=pl.ANY)] * count,
        scratch_shapes=[
            pltpu.SemaphoreType.DMA((len(chunks), 6)),
            pltpu.SemaphoreType.DMA((len(chunks), 6)),
            pltpu.SemaphoreType.DMA((count,)),
        ],
        compiler_params=pltpu.CompilerParams(collective_id=collective_id, has_side_effects=True),
    )(*parts)
    return [out.reshape(-1, part.shape[1]) for out, part in zip(outs, parts)]


def add_blocks(target, terms, lead, rows):
    steps = rows // 16

    def body(step, carry):
        block, part = (step // steps, (step % steps) * 16)
        at = []
        for size in lead[::-1]:
            at.insert(0, block % size)
            block = block // size
        at = tuple(at) + (pl.ds(pl.multiple_of(part, 16), 16),)
        total = terms[0][at].astype(jnp.float32)
        for term in terms[1:]:
            total = total + term[at].astype(jnp.float32)
        target[at] = total.astype(target.dtype)
        return carry

    lax.fori_loop(0, math.prod(lead) * steps, body, 0)


def scatter_kernel(chunks, events, shared, *refs):
    count = len(shared)
    ins, outs = (refs[:count], refs[count : 2 * count])
    send, recv, local = refs[2 * count : 2 * count + 3]
    slots = list(refs[2 * count + 3 :])
    place, core = (places(), lax.axis_index("col"))
    held = {}
    for i in range(len(chunks)):
        held[i] = [slots.pop(0) for _ in range(5 if shared[chunks[i][0]] else 4)]
    greet(place, core)
    sent, flying, owns = ([], {}, {})

    def lead_of(order, phase):
        return [GRID[dim] for dim in range(3) if dim not in order[: phase + 1]]

    for i in dict.fromkeys(i for i, _ in events):
        which, start, wide, order = chunks[i]
        cols = pl.ds(start, wide)
        if shared[which]:
            own = ins[which].at[:, :, :, core, :, cols]
            other = ins[which].at[:, :, :, 1 - core, :, cols]
            flying[i] = [push(other, held[i][1], send.at[i, 5], recv.at[i, 5], row_of(place), 1 - core)]
            sent += flying[i]
        else:
            at = [slice(None)] * 3
            at[order[0]] = place[order[0]]
            own = ins[which].at[tuple(at) + (slice(None), cols)]
        owns[i] = pltpu.make_async_copy(own, held[i][0], local.at[i])
        owns[i].start()

    def source_of(i, phase):
        which, start, wide, order = chunks[i]
        if phase == 0:
            return held[i][1] if shared[which] else ins[which].at[:, :, :, :, pl.ds(start, wide)]
        return held[i][-3 + phase - 1].at[0]

    def landed(i, phase):
        which, start, wide, order = chunks[i]
        rows = outs[which].shape[0]
        for copy in flying.pop(i):
            copy.wait_recv()
        if phase < 0:
            owns[i].wait()
            add_blocks(held[i][1], [held[i][0], held[i][1]], list(GRID), rows)
            return
        dim = order[phase]
        came = held[i][-3 + phase]
        if phase == 0 and not shared[which]:
            owns[i].wait()
            own = held[i][0]
        else:
            left = [d for d in range(3) if d not in order[:phase]]
            at = tuple(place[dim] if d == dim else slice(None) for d in left)
            own = source_of(i, phase).at[at]
        target = outs[which].at[:, pl.ds(start, wide)] if phase == 2 else came.at[0]
        terms = [own] + [came.at[k] for k in range(GRID[dim] - 1)]
        add_blocks(target, terms, lead_of(order, phase), rows)

    for i, phase in events:
        which, start, wide, order = chunks[i]
        if phase > 0 or shared[which]:
            landed(i, phase - 1)
        dim = order[phase]
        left = [d for d in range(3) if d not in order[:phase]]
        slot = (0, 3, 4)[dim]
        flying[i] = []
        for k in range(1, GRID[dim]):
            there = lax.rem(place[dim] + k, GRID[dim])
            at = tuple(there if d == dim else slice(None) for d in left)
            flying[i].append(
                push(
                    source_of(i, phase).at[at],
                    held[i][-3 + phase].at[k - 1],
                    send.at[i, slot + k - 1],
                    recv.at[i, slot + k - 1],
                    moved(place, dim, k),
                    core,
                )
            )
        sent += flying[i]
    for i in list(flying):
        landed(i, 2)
    for copy in sent:
        copy.wait_send()


def scatter_parts(parts, shared, plan, collective_id):
    if not by_grid():
        return [
            lax.psum_scatter(
                part.astype(jnp.float32),
                ("row", "col") if both else "row",
                scatter_dimension=0,
                tiled=True,
            )
            for part, both in zip(parts, shared)
        ]
    chunks, events = plan
    count = len(parts)
    views = []
    for part, both in zip(parts, shared):
        rows = part.shape[0] // (math.prod(GRID) * (2 if both else 1))
        views.append(part.reshape(GRID + ((2,) if both else ()) + (rows, part.shape[1])))
    scratch = []
    for which, _, wide, order in chunks:
        rows = views[which].shape[-2]
        if shared[which]:
            scratch += [pltpu.VMEM(GRID + (rows, wide), jnp.bfloat16)] * 2
        else:
            lead = tuple(GRID[dim] for dim in range(3) if dim != order[0])
            scratch.append(pltpu.VMEM(lead + (rows, wide), jnp.bfloat16))
        for phase in range(3):
            lead = tuple(GRID[dim] for dim in range(3) if dim not in order[: phase + 1])
            scratch.append(
                pltpu.VMEM((GRID[order[phase]] - 1,) + lead + (rows, wide), jnp.bfloat16)
            )
    return pl.pallas_call(
        functools.partial(scatter_kernel, chunks, events, shared),
        out_shape=[jax.ShapeDtypeStruct(view.shape[-2:], jnp.float32) for view in views],
        in_specs=[pl.BlockSpec(memory_space=pl.ANY)] * count,
        out_specs=[pl.BlockSpec(memory_space=pltpu.VMEM)] * count,
        scratch_shapes=[
            pltpu.SemaphoreType.DMA((len(chunks), 6)),
            pltpu.SemaphoreType.DMA((len(chunks), 6)),
            pltpu.SemaphoreType.DMA((len(chunks),)),
        ]
        + scratch,
        compiler_params=pltpu.CompilerParams(
            collective_id=collective_id, has_side_effects=True, vmem_limit_bytes=60 * 1024 * 1024
        ),
    )(*views)


def sibling(value):
    return lax.ppermute(value, "col", [(0, 1), (1, 0)])


def gather_col(value):
    if lax.axis_size("col") != 2:
        return lax.all_gather(value, "col", axis=0, tiled=True)
    core = lax.axis_index("col")
    rows = value.shape[0]
    whole = jnp.zeros((2 * rows,) + value.shape[1:], value.dtype)
    whole = lax.dynamic_update_slice_in_dim(whole, value, core * rows, 0)
    return lax.dynamic_update_slice_in_dim(whole, sibling(value), (1 - core) * rows, 0)


def scatter_col(total):
    if lax.axis_size("col") != 2:
        return lax.psum_scatter(total, "col", scatter_dimension=0, tiled=True)
    core = lax.axis_index("col")
    rows = total.shape[0] // 2
    leaving = lax.dynamic_slice_in_dim(total, (1 - core) * rows, rows, 0).astype(jnp.bfloat16)
    mine = lax.dynamic_slice_in_dim(total, core * rows, rows, 0)
    return mine + sibling(leaving).astype(jnp.float32)


def padded(value, wide):
    return jnp.pad(value, ((0, 0), (0, wide - value.shape[1])))


def norm_parts(values, gain):
    average = jnp.mean(values, axis=-1, keepdims=True)
    centred = values - average
    inv_std = lax.rsqrt(jnp.mean(centred * centred, axis=-1, keepdims=True) + EPS)
    normed = centred * inv_std
    return (normed * gain, normed, inv_std)


def norm_back(grad_in, gain, normed, inv_std):
    grad_hat = grad_in * gain
    mean_one = jnp.mean(grad_hat, axis=-1, keepdims=True)
    mean_two = jnp.mean(grad_hat * normed, axis=-1, keepdims=True)
    return inv_std * (grad_hat - mean_one - normed * mean_two)


def rope_tables(positions, width):
    half_width = width // 2
    freq = jnp.exp(jnp.arange(half_width).astype(jnp.float32) * (-2.0 * math.log(10000.0) / width))
    angle = positions.astype(jnp.float32)[:, None] * freq[None, :]
    return (jnp.cos(angle), jnp.sin(angle))


def rotate(values, cosine, sines):
    half_width = values.shape[-1] // 2
    front_half = values[..., :half_width]
    back_half = values[..., half_width:]
    cos_part = cosine[:, None, :]
    sin_part = sines[:, None, :]
    return jnp.concatenate(
        [
            front_half * cos_part - back_half * sin_part,
            back_half * cos_part + front_half * sin_part,
        ],
        axis=-1,
    )


def unrotate(values, cosine, sines):
    half_width = values.shape[-1] // 2
    front_half = values[..., :half_width]
    back_half = values[..., half_width:]
    cos_part = cosine[:, None, :]
    sin_part = sines[:, None, :]
    return jnp.concatenate(
        [
            front_half * cos_part + back_half * sin_part,
            back_half * cos_part - front_half * sin_part,
        ],
        axis=-1,
    )


def shards(
    block_input,
    teacher,
    lengths,
    head_routes,
    expert_routes,
    first_gain,
    query_weight,
    key_weight,
    value_weight,
    head_router,
    output_weight,
    second_gain,
    expert_router,
    expert_up,
    expert_down,
):
    tok_rows = block_input.shape[0]
    width = block_input.shape[1]
    col_count = lax.axis_size("col")
    col_index = lax.axis_index("col")
    total_rows = tok_rows * lax.axis_size("row") * col_count
    group_size = tok_rows * col_count
    seq_length = min(MAXLEN, group_size)
    key_span = seq_length // tok_rows
    gated = H * AEXP
    local_experts = expert_up.shape[0]
    hidden_local = expert_up.shape[2]
    hidden = local_experts * hidden_local
    length_sum = jnp.sum(lengths)
    small_parts = [
        query_weight,
        key_weight,
        head_router,
        first_gain[:, None],
        second_gain[:, None],
    ]
    for digits in (length_sum // 64, length_sum % 64):
        small_parts.append(
            jnp.broadcast_to(digits.astype(jnp.bfloat16)[None, None], (first_gain.shape[0], 1))
        )
    lead_local = padded(jnp.concatenate(small_parts, axis=1), 2 * H * DH + 128)
    up_local = jnp.concatenate(
        [
            jnp.transpose(expert_up, (1, 0, 2)).reshape(-1, hidden),
            padded(expert_router, 128),
        ],
        axis=1,
    )
    down_local = jnp.transpose(expert_down, (2, 0, 1)).reshape(-1, hidden)
    lead_full, value_full, output_turned, up_wide, down_turned = gather_parts(
        [lead_local, value_weight, output_weight.T, up_local, down_local],
        [True, True, True, False, False],
        GATHER_PLAN,
        1,
    )
    up_full = up_wide[:, :hidden]
    router_cols = up_wide[:, hidden : hidden + local_experts]
    extra_at = 2 * H * DH + 2 * gated
    extra = lead_full[:, extra_at : extra_at + 4].astype(jnp.float32)
    gain_one = extra[:, 0]
    gain_two = extra[:, 1]
    stride = first_gain.shape[0] * col_count
    token_count = jnp.sum(extra[::stride, 2]) * 64.0 + jnp.sum(extra[::stride, 3])
    local_ids = jnp.arange(tok_rows, dtype=jnp.int32)
    group_ids = col_index * tok_rows + local_ids
    seq_pos = group_ids % seq_length
    seq_ids = group_ids // seq_length
    seq_slots = jnp.arange(lengths.shape[0], dtype=jnp.int32)
    tok_length = jnp.sum(
        jnp.where(seq_ids[:, None] == seq_slots[None, :], lengths[None, :], 0), axis=1
    )
    valid = (seq_pos < tok_length).astype(jnp.float32)
    inputs_full = block_input.astype(jnp.float32)
    normed_one, hat_one, inv_one = norm_parts(inputs_full, gain_one)
    normed_low = normed_one.astype(jnp.bfloat16)
    lead_raw = jnp.dot(normed_low, lead_full, preferred_element_type=jnp.float32)
    query_raw = lead_raw[:, : H * DH]
    key_raw = lead_raw[:, H * DH : 2 * H * DH]
    route_logits = lead_raw[:, 2 * H * DH : extra_at]
    cosine, sines = rope_tables(seq_pos, DH)
    query_scale = DH ** (-0.5)
    query_rot = (rotate(query_raw.reshape(tok_rows, H, DH), cosine, sines) * query_scale).astype(
        jnp.bfloat16
    )
    key_rot = rotate(key_raw.reshape(tok_rows, H, DH), cosine, sines).astype(jnp.bfloat16)
    chosen = jnp.any(
        head_routes[:, :, :, None] == jnp.arange(AEXP, dtype=jnp.int32)[None, None, None, :], axis=2
    ).astype(jnp.float32)
    value_sig = jax.nn.sigmoid(route_logits[:, :gated]).reshape(tok_rows, H, AEXP)
    output_sig = jax.nn.sigmoid(route_logits[:, gated:]).reshape(tok_rows, H, AEXP)
    value_gates = value_sig * chosen
    output_gates = output_sig * chosen
    value_all = jnp.dot(block_input, value_full, preferred_element_type=jnp.float32).reshape(
        tok_rows, H, AEXP, DH
    )
    values_low = jnp.sum(value_all * value_gates[..., None], axis=2).astype(jnp.bfloat16)
    key_parts = [key_rot]
    value_parts = [values_low]
    id_parts = [group_ids]
    for offset in range(1, key_span):
        came_keys, came_values = shifted((key_rot, values_low), "col", offset)
        key_parts.append(came_keys)
        value_parts.append(came_values)
        id_parts.append(group_ids - offset * tok_rows)
    keys_all = jnp.concatenate(key_parts, axis=0)
    values_all = jnp.concatenate(value_parts, axis=0)
    key_ids = jnp.concatenate(id_parts, axis=0)
    allowed = (
        (key_ids[None, :] // seq_length == seq_ids[:, None])
        & (key_ids[None, :] <= group_ids[:, None])
        & (key_ids[None, :] % seq_length < tok_length[:, None])
    )

    def head_scores(head_idx):
        raw_scores = jnp.einsum(
            "qd,kd->qk",
            query_rot[:, head_idx],
            keys_all[:, head_idx],
            preferred_element_type=jnp.float32,
        )
        return jnp.where(allowed, raw_scores, MASKED)

    attended_list = []
    lse_list = []
    for head_idx in range(H):
        scores = head_scores(head_idx)
        row_top = jnp.max(scores, axis=1, keepdims=True)
        exponent = jnp.exp(scores - row_top)
        row_total = jnp.sum(exponent, axis=1, keepdims=True)
        probs_low = (exponent / row_total).astype(jnp.bfloat16)
        attended_list.append(
            jnp.dot(probs_low, values_all[:, head_idx], preferred_element_type=jnp.float32)
        )
        lse_list.append(row_top + jnp.log(row_total))
    attended = jnp.stack(attended_list, axis=1)
    mixed_low = (
        (attended[:, :, None, :] * output_gates[..., None])
        .astype(jnp.bfloat16)
        .reshape(tok_rows, gated * DH)
    )
    resid = inputs_full + contract_last(mixed_low, output_turned)
    resid_low = resid.astype(jnp.bfloat16)
    group_in = gather_col(resid_low)
    normed_two, hat_two, inv_two = norm_parts(group_in.astype(jnp.float32), gain_two)
    normed_two_low = normed_two.astype(jnp.bfloat16)
    gates = jax.nn.sigmoid(jnp.dot(normed_two_low, router_cols, preferred_element_type=jnp.float32))
    expert_ids = col_index * local_experts + jnp.arange(local_experts, dtype=jnp.int32)
    member = jnp.any(expert_routes[:, :, None] == expert_ids[None, None, :], axis=1)
    used_gates = gates * member.astype(jnp.float32)

    def spread(columns):
        return jnp.repeat(columns, hidden_local, axis=1)

    inner = jnp.dot(group_in, up_full, preferred_element_type=jnp.float32)
    active = jnp.maximum(inner, 0.0).astype(jnp.bfloat16)
    gated_active = (active.astype(jnp.float32) * spread(used_gates)).astype(jnp.bfloat16)
    expert_sum = scatter_col(contract_last(gated_active, down_turned))
    output_full_rows = resid + expert_sum
    block_output = output_full_rows.astype(jnp.bfloat16)
    ratio = total_rows / token_count
    grad_output = ratio * (output_full_rows - teacher.astype(jnp.float32)) * valid[:, None]
    grad_output_low = grad_output.astype(jnp.bfloat16)
    group_grad = gather_col(grad_output_low)
    grad_hidden = jnp.dot(group_grad, down_turned, preferred_element_type=jnp.float32)
    gate_grad = jnp.sum(
        (active.astype(jnp.float32) * grad_hidden).reshape(group_size, local_experts, hidden_local),
        axis=2,
    )
    grad_inner = jnp.where(active > 0, grad_hidden * spread(used_gates), 0.0).astype(jnp.bfloat16)
    down_grad = contract_first(group_grad, gated_active).astype(jnp.bfloat16)
    up_grad = contract_first(group_in, grad_inner).astype(jnp.bfloat16)
    slot_back = contract_last(grad_inner, up_full)
    logit_low = (gate_grad * used_gates * (1.0 - gates)).astype(jnp.bfloat16)
    router_grad = contract_first(normed_two_low, padded(logit_low, 128)).astype(jnp.bfloat16)
    grad_norm_two = contract_last(logit_low, router_cols)
    second_gain_part = jnp.sum(grad_norm_two * hat_two, axis=0)
    grad_rows = slot_back + norm_back(grad_norm_two, gain_two, hat_two, inv_two)
    moe_grad = scatter_col(grad_rows)
    grad_resid = grad_output + moe_grad
    grad_branch = grad_resid.astype(jnp.bfloat16)
    output_grad = contract_first(grad_branch, mixed_low).astype(jnp.bfloat16)
    grad_mixed = (
        jnp.dot(grad_branch, output_turned, preferred_element_type=jnp.float32)
        .astype(jnp.bfloat16)
        .astype(jnp.float32)
        .reshape(tok_rows, H, AEXP, DH)
    )
    grad_attended = jnp.sum(grad_mixed * output_gates[..., None], axis=2).astype(jnp.bfloat16)
    grad_output_gates = jnp.sum(grad_mixed * attended[:, :, None, :], axis=3)
    query_grads = []
    key_grads = []
    value_grads = []
    for head_idx in range(H):
        scores = head_scores(head_idx)
        probs_full = jnp.exp(scores - lse_list[head_idx])
        probs_low = probs_full.astype(jnp.bfloat16)
        grad_probs = jnp.einsum(
            "qd,kd->qk",
            grad_attended[:, head_idx],
            values_all[:, head_idx],
            preferred_element_type=jnp.float32,
        )
        grad_scores = (
            probs_full * (grad_probs - jnp.sum(probs_full * grad_probs, axis=1, keepdims=True))
        ).astype(jnp.bfloat16)
        query_grads.append(
            jnp.dot(grad_scores, keys_all[:, head_idx], preferred_element_type=jnp.float32)
        )
        key_grads.append(contract_first(grad_scores, query_rot[:, head_idx]))
        value_grads.append(contract_first(probs_low, grad_attended[:, head_idx]))
    grad_queries = jnp.stack(query_grads, axis=1)
    key_grads_all = jnp.stack(key_grads, axis=1)
    value_grads_all = jnp.stack(value_grads, axis=1)
    grad_key_rot = key_grads_all[:tok_rows]
    grad_values = value_grads_all[:tok_rows]
    for offset in range(1, key_span):
        back_keys, back_values = (
            shifted(
                key_grads_all[offset * tok_rows : (offset + 1) * tok_rows].astype(jnp.bfloat16),
                "col",
                -offset,
            ).astype(jnp.float32),
            shifted(
                value_grads_all[offset * tok_rows : (offset + 1) * tok_rows].astype(jnp.bfloat16),
                "col",
                -offset,
            ).astype(jnp.float32),
        )
        grad_key_rot = grad_key_rot + back_keys
        grad_values = grad_values + back_values
    grad_value_all = (
        (grad_values[:, :, None, :] * value_gates[..., None])
        .astype(jnp.bfloat16)
        .reshape(tok_rows, gated * DH)
    )
    grad_value_gates = jnp.sum(value_all * grad_values[:, :, None, :], axis=3)
    grad_query_raw = (
        unrotate(grad_queries * query_scale, cosine, sines)
        .astype(jnp.bfloat16)
        .reshape(tok_rows, H * DH)
    )
    grad_key_raw = (
        unrotate(grad_key_rot, cosine, sines).astype(jnp.bfloat16).reshape(tok_rows, H * DH)
    )
    grad_route = jnp.concatenate(
        [
            (grad_value_gates * chosen * value_sig * (1.0 - value_sig)).reshape(tok_rows, gated),
            (grad_output_gates * chosen * output_sig * (1.0 - output_sig)).reshape(tok_rows, gated),
        ],
        axis=1,
    ).astype(jnp.bfloat16)
    lead_back = padded(
        jnp.concatenate([grad_query_raw, grad_key_raw, grad_route], axis=1), 2 * H * DH + 128
    )
    value_grad = contract_first(block_input, grad_value_all).astype(jnp.bfloat16)
    grad_norm_one = contract_last(lead_back, lead_full)
    first_gain_part = jnp.sum(grad_norm_one * hat_one, axis=0)
    input_grad = (
        grad_resid
        + norm_back(grad_norm_one, gain_one, hat_one, inv_one)
        + contract_last(grad_value_all, value_full)
    )
    lead_cols = jnp.arange(2 * H * DH + 128, dtype=jnp.int32)[None, :]
    lead_grad = (
        contract_first(normed_low, lead_back)
        + jnp.where(lead_cols == extra_at, first_gain_part[:, None], 0.0)
        + jnp.where(lead_cols == extra_at + 1, second_gain_part[:, None], 0.0)
    ).astype(jnp.bfloat16)
    lead_sum, value_sum, output_turned_sum, up_sum, router_sum, down_sum = scatter_parts(
        [lead_grad, value_grad, output_grad, up_grad, router_grad, down_grad],
        [True, True, True, False, False, False],
        SCATTER_PLAN,
        2,
    )
    output_sum = output_turned_sum.T
    router_sum = router_sum[:, :local_experts]
    up_out = jnp.transpose(up_sum.reshape(-1, local_experts, hidden_local), (1, 0, 2))
    down_out = jnp.transpose(down_sum.reshape(-1, local_experts, hidden_local), (1, 2, 0))
    query_sum = lead_sum[:, : H * DH]
    key_sum = lead_sum[:, H * DH : 2 * H * DH]
    router_head_sum = lead_sum[:, 2 * H * DH : extra_at]
    first_sum = lead_sum[:, extra_at]
    second_sum = lead_sum[:, extra_at + 1]
    return (
        block_output,
        input_grad,
        first_sum,
        query_sum,
        key_sum,
        value_sum,
        router_head_sum,
        output_sum,
        second_sum,
        router_sum,
        up_out,
        down_out,
    )


def solution(mesh):
    return jax.shard_map(
        shards,
        mesh=mesh,
        in_specs=(
            P(("row", "col"), None),
            P(("row", "col"), None),
            P("row"),
            P(("row", "col"), None, None),
            P("row", None),
            P(("row", "col")),
            P(("row", "col"), None),
            P(("row", "col"), None),
            P(("row", "col"), None),
            P(("row", "col"), None),
            P(None, ("row", "col")),
            P(("row", "col")),
            P("row", "col"),
            P("col", "row", None),
            P("col", None, "row"),
        ),
        out_specs=(
            P(("row", "col"), None),
            P(("row", "col"), None),
            P(("row", "col")),
            P(("row", "col"), None),
            P(("row", "col"), None),
            P(("row", "col"), None),
            P(("row", "col"), None),
            P(None, ("row", "col")),
            P(("row", "col")),
            P("row", "col"),
            P("col", "row", None),
            P("col", None, "row"),
        ),
        check_vma=False,
    )
```

```python
import functools
import math

import jax
import jax.numpy as jnp
from jax import lax
from jax.experimental import pallas as pl
from jax.experimental.pallas import tpu as pltpu
from jax.sharding import PartitionSpec as P

H = 4
DH = 128
AEXP = 5
MAXLEN = 2048


EPS = 1e-05
MASKED = -1e30


def shifted(value, axis, steps):
    count = lax.axis_size(axis)
    leading, last = (max(0, -steps), min(count, count - steps))
    return lax.ppermute(value, axis, [(source, source + steps) for source in range(leading, last)])


def contract_last(left, right):
    return lax.dot_general(
        left, right, (((1,), (1,)), ((), ())), preferred_element_type=jnp.float32
    )


def contract_first(left, right):
    return lax.dot_general(
        left, right, (((0,), (0,)), ((), ())), preferred_element_type=jnp.float32
    )


GRID = (4, 2, 2)
MESH = pl.DeviceIdType.MESH
LEAD_GATHER = (
    (
        (0, 0, 384, (0, 1, 2)),
        (1, 0, 512, (2, 1, 0)),
        (1, 512, 768, (1, 0, 2)),
        (1, 1280, 640, (0, 2, 1)),
        (1, 1920, 640, (0, 1, 2)),
        (0, 384, 768, (0, 2, 1)),
    ),
    (
        (0, 0),
        (1, 0),
        (2, 0),
        (3, 0),
        (4, 0),
        (5, 0),
        (1, 1),
        (2, 1),
        (0, 1),
        (1, 2),
        (3, 1),
        (0, 2),
        (4, 1),
        (3, 2),
        (5, 1),
        (4, 2),
        (0, 3),
        (5, 2),
        (3, 3),
        (2, 2),
        (4, 3),
        (5, 3),
        (1, 3),
        (2, 3),
    ),
)
REST_GATHER = (
    (
        (0, 0, 1024, (0, 2, 1)),
        (0, 1024, 512, (0, 1, 2)),
        (2, 0, 896, (1, 0, 2)),
        (1, 0, 384, (0, 1, 2)),
        (0, 1536, 1024, (0, 2, 1)),
        (2, 896, 512, (1, 2, 0)),
        (1, 384, 1152, (0, 2, 1)),
        (1, 1536, 640, (0, 1, 2)),
        (2, 1408, 640, (0, 2, 1)),
    ),
    (
        (0, 0),
        (1, 0),
        (2, 0),
        (3, 0),
        (4, 0),
        (5, 0),
        (6, 0),
        (7, 0),
        (8, 0),
        (2, 1),
        (5, 1),
        (0, 1),
        (1, 1),
        (5, 2),
        (3, 1),
        (1, 2),
        (0, 2),
        (4, 1),
        (3, 2),
        (1, 3),
        (4, 2),
        (0, 3),
        (6, 1),
        (7, 1),
        (4, 3),
        (8, 1),
        (6, 2),
        (7, 2),
        (8, 2),
        (2, 2),
    ),
)
REST_SCATTER = (
    (
        (0, 0, 1536, (1, 2, 0)),
        (3, 0, 1024, (1, 2, 0)),
        (1, 0, 768, (1, 2, 0)),
        (2, 0, 128, (1, 2, 0)),
        (3, 1024, 640, (2, 0, 1)),
        (1, 768, 768, (2, 0, 1)),
        (1, 1536, 512, (0, 1, 2)),
        (0, 1536, 1024, (1, 2, 0)),
        (3, 1664, 384, (2, 1, 0)),
    ),
    (
        (1, 0),
        (2, 0),
        (3, 0),
        (4, 0),
        (5, 0),
        (6, 0),
        (8, 0),
        (0, 0),
        (7, 0),
        (4, 1),
        (6, 1),
        (1, 1),
        (5, 1),
        (4, 2),
        (8, 1),
        (2, 1),
        (3, 1),
        (1, 2),
        (5, 2),
        (2, 2),
        (0, 1),
        (3, 2),
        (0, 2),
        (7, 1),
        (6, 2),
        (7, 2),
        (8, 2),
    ),
)
LEAD_SCATTER = (
    (
        (0, 0, 512, (0, 2, 1)),
        (1, 0, 640, (1, 0, 2)),
        (1, 640, 896, (2, 1, 0)),
        (0, 512, 640, (1, 0, 2)),
        (1, 1536, 640, (2, 1, 0)),
        (1, 2176, 384, (2, 1, 0)),
    ),
    (
        (0, 0),
        (1, 0),
        (2, 0),
        (3, 0),
        (4, 0),
        (1, 1),
        (5, 0),
        (0, 1),
        (2, 1),
        (3, 1),
        (1, 2),
        (4, 1),
        (2, 2),
        (3, 2),
        (5, 1),
        (0, 2),
        (4, 2),
        (5, 2),
    ),
)


def by_grid():
    return lax.axis_size("row") == math.prod(GRID) and lax.axis_size("col") == 2


def places():
    row = lax.axis_index("row")
    return (row // 4, (row // 2) % 2, row % 2)


def row_of(place):
    return (place[0] * 2 + place[1]) * 2 + place[2]


def moved(place, dim, steps):
    there = list(place)
    there[dim] = lax.rem(place[dim] + steps, GRID[dim])
    return row_of(there)


def greet(place, core):
    barrier = pltpu.get_barrier_semaphore()
    partners = [(moved(place, dim, k), core) for dim in range(3) for k in range(1, GRID[dim])]
    partners.append((row_of(place), 1 - core))
    for row, col in partners:
        pl.semaphore_signal(barrier, inc=1, device_id={"row": row, "col": col}, device_id_type=MESH)
    pl.semaphore_wait(barrier, len(partners))


def push(source, target, send, recv, row, core):
    copy = pltpu.make_async_remote_copy(
        source, target, send, recv, device_id={"row": row, "col": core}, device_id_type=MESH
    )
    copy.start()
    return copy


def head_cols(head):
    return slice(head * DH, (head + 1) * DH)


def half_turned(values, cosine, sines):
    return values * cosine + pltpu.roll(values, DH // 2, 1) * sines


def masked_pair(queries, keys, others, limits, core):
    rows = queries.shape[0]
    query_at = core * rows + lax.broadcasted_iota(jnp.int32, (rows, rows), 0)
    key_at = lax.broadcasted_iota(jnp.int32, (rows, rows), 1)
    scores = []
    for block, start in ((keys, core * rows), (others, (1 - core) * rows)):
        place = start + key_at
        allowed = (place <= query_at) & (place < limits)
        scores.append(jnp.where(allowed, contract_last(queries, block), MASKED))
    return scores


def gather_run(chunks, events, shared, ins, outs, send, recv, local, place, core, tasks):
    owns = []
    for n in range(len(shared)):
        at = tuple(place) + ((core,) if shared[n] else ())
        owns.append(pltpu.make_async_copy(ins[n], outs[n].at[at], local.at[n]))
        owns[-1].start()
    sent, flying, left = ([], {}, list(tasks))
    early = sum(1 for _, phase in events if phase == 0)
    waited = False
    for step, (i, phase) in enumerate(events):
        if left and step >= early and (step - early) % 2 == 0:
            left.pop(0)()
        which, start, wide, order = chunks[i]
        if phase == 1 and not waited:
            for copy in owns:
                copy.wait()
            waited = True
        for copy in flying.pop(i, []):
            copy.wait_recv()
        held = order[:phase]
        at = [slice(None) if dim in held else place[dim] for dim in range(3)]
        at += [core] if shared[which] else []
        block = outs[which].at[tuple(at) + (slice(None), pl.ds(start, wide))]
        if phase == 3:
            flying[i] = [push(block, block, send.at[i, 5], recv.at[i, 5], row_of(place), 1 - core)]
        else:
            dim = order[phase]
            source = ins[which].at[:, pl.ds(start, wide)] if phase == 0 else block
            slot = (0, 3, 4)[dim]
            flying[i] = [
                push(
                    source,
                    block,
                    send.at[i, slot + k - 1],
                    recv.at[i, slot + k - 1],
                    moved(place, dim, k),
                    core,
                )
                for k in range(1, GRID[dim])
            ]
        sent += flying[i]
    for task in left:
        task()
    for copies in flying.values():
        for copy in copies:
            copy.wait_recv()
    for copy in sent:
        copy.wait_send()


def gather_kernel(chunks, events, shared, *refs):
    count = len(shared)
    place, core = (places(), lax.axis_index("col"))
    greet(place, core)
    gather_run(
        chunks, events, shared, refs[:count], refs[count : 2 * count], *refs[2 * count :], place, core, ()
    )


def attend_kernel(chunks, events, shared, *refs):
    count = len(shared)
    ins, refs = (refs[:count], refs[count:])
    lead, value_all, gates, cosine, sines, limits = refs[:6]
    outs, refs = (refs[6 : 6 + count], refs[6 + count :])
    query, key, value, key_other, value_other, attended, lse, mixed = refs[:8]
    send, recv, local, side_send, side_recv = refs[8:]
    place, core = (places(), lax.axis_index("col"))
    greet(place, core)
    side = []

    def make_keys():
        for head in range(H):
            at = head_cols(head)
            shift = slice(H * DH + head * DH, H * DH + (head + 1) * DH)
            key[:, at] = half_turned(lead[:, shift], cosine[...], sines[...]).astype(key.dtype)

    def make_values():
        for head in range(H):
            total = None
            for one in range(head * AEXP, (head + 1) * AEXP):
                term = value_all[:, head_cols(one)] * gates[:, one : one + 1]
                total = term if total is None else total + term
            value[:, head_cols(head)] = total.astype(value.dtype)

    def make_queries():
        row, col = (row_of(place), 1 - core)
        side.append(push(key, key_other, side_send.at[0], side_recv.at[0], row, col))
        side.append(push(value, value_other, side_send.at[1], side_recv.at[1], row, col))
        for head in range(H):
            at = head_cols(head)
            turned = half_turned(lead[:, at], cosine[...], sines[...]) * DH ** (-0.5)
            query[:, at] = turned.astype(query.dtype)

    def arrive():
        for copy in side:
            copy.wait()

    def attend(head):
        at = head_cols(head)
        near, far = masked_pair(query[:, at], key[:, at], key_other[:, at], limits[0:1, 0:1], core)
        top = jnp.maximum(
            jnp.max(near, axis=1, keepdims=True), jnp.max(far, axis=1, keepdims=True)
        )
        near, far = (jnp.exp(near - top), jnp.exp(far - top))
        total = jnp.sum(near, axis=1, keepdims=True) + jnp.sum(far, axis=1, keepdims=True)
        near, far = ((near / total).astype(jnp.bfloat16), (far / total).astype(jnp.bfloat16))
        out = jnp.dot(near, value[:, at], preferred_element_type=jnp.float32) + jnp.dot(
            far, value_other[:, at], preferred_element_type=jnp.float32
        )
        attended[:, at] = out
        lse[:, at] = jnp.broadcast_to(top + jnp.log(total), out.shape)
        for one in range(head * AEXP, (head + 1) * AEXP):
            gate = gates[:, H * AEXP + one : H * AEXP + one + 1]
            mixed[:, head_cols(one)] = (out * gate).astype(mixed.dtype)

    tasks = [make_keys, make_values, make_queries, arrive]
    tasks += [functools.partial(attend, head) for head in range(H)]
    gather_run(chunks, events, shared, ins, outs, send, recv, local, place, core, tasks)


def gather_call(kernel, parts, shared, plan, collective_id, more, made, scratch):
    chunks, events = plan
    count = len(parts)
    outs = pl.pallas_call(
        functools.partial(kernel, chunks, events, shared),
        out_shape=[
            jax.ShapeDtypeStruct(GRID + ((2,) if both else ()) + part.shape, part.dtype)
            for part, both in zip(parts, shared)
        ]
        + made,
        in_specs=[pl.BlockSpec(memory_space=pltpu.VMEM)] * (count + len(more)),
        out_specs=[pl.BlockSpec(memory_space=pl.ANY)] * count
        + [pl.BlockSpec(memory_space=pltpu.VMEM)] * len(made),
        scratch_shapes=[
            pltpu.SemaphoreType.DMA((len(chunks), 6)),
            pltpu.SemaphoreType.DMA((len(chunks), 6)),
            pltpu.SemaphoreType.DMA((count,)),
        ]
        + scratch,
        compiler_params=pltpu.CompilerParams(
            collective_id=collective_id, has_side_effects=True, vmem_limit_bytes=60 * 1024 * 1024
        ),
    )(*parts, *more)
    whole = [out.reshape(-1, part.shape[1]) for out, part in zip(outs, parts)]
    return (whole, outs[count:])


def gather_parts(parts, shared, plan, collective_id):
    if not by_grid():
        return [
            lax.all_gather(part, ("row", "col") if both else "row", axis=0, tiled=True)
            for part, both in zip(parts, shared)
        ]
    return gather_call(gather_kernel, parts, shared, plan, collective_id, [], [], [])[0]


def add_blocks(target, terms, lead, rows):
    steps = rows // 16

    def body(step, carry):
        block, part = (step // steps, (step % steps) * 16)
        at = []
        for size in lead[::-1]:
            at.insert(0, block % size)
            block = block // size
        at = tuple(at) + (pl.ds(pl.multiple_of(part, 16), 16),)
        total = terms[0][at].astype(jnp.float32)
        for term in terms[1:]:
            total = total + term[at].astype(jnp.float32)
        target[at] = total.astype(target.dtype)
        return carry

    lax.fori_loop(0, math.prod(lead) * steps, body, 0)


def scatter_run(chunks, events, shared, ins, outs, send, recv, local, slots, place, core, tasks):
    slots, rest = (list(slots), list(tasks))
    held = {}
    for i in range(len(chunks)):
        held[i] = [slots.pop(0) for _ in range(5 if shared[chunks[i][0]] else 4)]
    sent, flying, owns = ([], {}, {})

    for i in dict.fromkeys(i for i, _ in events):
        which, start, wide, order = chunks[i]
        cols = pl.ds(start, wide)
        if shared[which]:
            own = ins[which].at[:, :, :, core, :, cols]
            other = ins[which].at[:, :, :, 1 - core, :, cols]
            flying[i] = [
                push(other, held[i][1], send.at[i, 5], recv.at[i, 5], row_of(place), 1 - core)
            ]
            sent += flying[i]
        else:
            at = [slice(None)] * 3
            at[order[0]] = place[order[0]]
            own = ins[which].at[tuple(at) + (slice(None), cols)]
        owns[i] = pltpu.make_async_copy(own, held[i][0], local.at[i])
        owns[i].start()

    def source_of(i, phase):
        which, start, wide, order = chunks[i]
        if phase == 0:
            return held[i][1] if shared[which] else ins[which].at[:, :, :, :, pl.ds(start, wide)]
        return held[i][-3 + phase - 1].at[0]

    def landed(i, phase):
        which, start, wide, order = chunks[i]
        rows = outs[which].shape[0]
        for copy in flying.pop(i):
            copy.wait_recv()
        if phase < 0:
            owns[i].wait()
            add_blocks(held[i][1], [held[i][0], held[i][1]], list(GRID), rows)
            return
        dim = order[phase]
        came = held[i][-3 + phase]
        if phase == 0 and not shared[which]:
            owns[i].wait()
            own = held[i][0]
        else:
            left = [d for d in range(3) if d not in order[:phase]]
            own = source_of(i, phase).at[tuple(place[dim] if d == dim else slice(None) for d in left)]
        target = outs[which].at[:, pl.ds(start, wide)] if phase == 2 else came.at[0]
        terms = [own] + [came.at[k] for k in range(GRID[dim] - 1)]
        lead = [GRID[d] for d in range(3) if d not in order[: phase + 1]]
        add_blocks(target, terms, lead, rows)

    early = sum(1 for i, phase in events if phase == 0 and not shared[chunks[i][0]])
    for step, (i, phase) in enumerate(events):
        if rest and step >= early and (step - early) % 2 == 0:
            rest.pop(0)()
        which, start, wide, order = chunks[i]
        if phase > 0 or shared[which]:
            landed(i, phase - 1)
        dim = order[phase]
        left = [d for d in range(3) if d not in order[:phase]]
        slot = (0, 3, 4)[dim]
        flying[i] = []
        for k in range(1, GRID[dim]):
            there = lax.rem(place[dim] + k, GRID[dim])
            at = tuple(there if d == dim else slice(None) for d in left)
            flying[i].append(
                push(
                    source_of(i, phase).at[at],
                    held[i][-3 + phase].at[k - 1],
                    send.at[i, slot + k - 1],
                    recv.at[i, slot + k - 1],
                    moved(place, dim, k),
                    core,
                )
            )
        sent += flying[i]
    for task in rest:
        task()
    for i in list(flying):
        landed(i, 2)
    for copy in sent:
        copy.wait_send()


def scatter_kernel(chunks, events, shared, *refs):
    count = len(shared)
    ins, outs = (refs[:count], refs[count : 2 * count])
    send, recv, local = refs[2 * count : 2 * count + 3]
    place, core = (places(), lax.axis_index("col"))
    greet(place, core)
    slots = refs[2 * count + 3 :]
    scatter_run(chunks, events, shared, ins, outs, send, recv, local, slots, place, core, ())


def attend_back_kernel(chunks, events, shared, *refs):
    count = len(shared)
    ins, refs = (refs[:count], refs[count:])
    query, key, value, key_other, value_other, attended, lse, grad_mixed = refs[:8]
    value_all, gates, sigs, cosine, sines, limits = refs[8:14]
    outs, refs = (refs[14 : 14 + count], refs[14 + count :])
    lead_back, grad_value_all = refs[:2]
    send, recv, local, side_send, side_recv = refs[2:7]
    grad_key, grad_value, grad_gates, key_leave, value_leave, key_came, value_came = refs[7:14]
    slots = refs[14:]
    place, core = (places(), lax.axis_index("col"))
    greet(place, core)
    side = []
    gated = H * AEXP

    def put_gate(one, column):
        lanes = lax.broadcasted_iota(jnp.int32, grad_gates.shape, 1)
        grad_gates[...] = jnp.where(lanes == one, column, grad_gates[...])

    def attend_back(head):
        at = head_cols(head)
        if head == 0:
            grad_gates[...] = jnp.zeros_like(grad_gates)
        total = None
        for one in range(head * AEXP, (head + 1) * AEXP):
            gate = gates[:, gated + one : gated + one + 1]
            piece = grad_mixed[:, head_cols(one)].astype(jnp.float32)
            put_gate(gated + one, jnp.sum(piece * attended[:, at], axis=1, keepdims=True))
            total = piece * gate if total is None else total + piece * gate
        grad_out = total.astype(jnp.bfloat16)
        queries, keys, others = (query[:, at], key[:, at], key_other[:, at])
        near, far = masked_pair(queries, keys, others, limits[0:1, 0:1], core)
        level = lse[:, head * DH : head * DH + 1]
        near, far = (jnp.exp(near - level), jnp.exp(far - level))
        near_grad = contract_last(grad_out, value[:, at])
        far_grad = contract_last(grad_out, value_other[:, at])
        mean = jnp.sum(near * near_grad, axis=1, keepdims=True) + jnp.sum(
            far * far_grad, axis=1, keepdims=True
        )
        near_grad = (near * (near_grad - mean)).astype(jnp.bfloat16)
        far_grad = (far * (far_grad - mean)).astype(jnp.bfloat16)
        near, far = (near.astype(jnp.bfloat16), far.astype(jnp.bfloat16))
        grad_query = jnp.dot(near_grad, keys, preferred_element_type=jnp.float32) + jnp.dot(
            far_grad, others, preferred_element_type=jnp.float32
        )
        turned = half_turned(grad_query * DH ** (-0.5), cosine[...], -sines[...])
        lead_back[:, at] = turned.astype(lead_back.dtype)
        grad_key[:, at] = contract_first(near_grad, queries)
        grad_value[:, at] = contract_first(near, grad_out)
        key_leave[:, at] = contract_first(far_grad, queries).astype(key_leave.dtype)
        value_leave[:, at] = contract_first(far, grad_out).astype(value_leave.dtype)

    def leave():
        row, col = (row_of(place), 1 - core)
        side.append(push(key_leave, key_came, side_send.at[0], side_recv.at[0], row, col))
        side.append(push(value_leave, value_came, side_send.at[1], side_recv.at[1], row, col))

    def arrive():
        for copy in side:
            copy.wait()

    def finish(head):
        at = head_cols(head)
        turned = half_turned(
            grad_key[:, at] + key_came[:, at].astype(jnp.float32), cosine[...], -sines[...]
        )
        lead_back[:, H * DH + head * DH : H * DH + (head + 1) * DH] = turned.astype(lead_back.dtype)
        whole = grad_value[:, at] + value_came[:, at].astype(jnp.float32)
        for one in range(head * AEXP, (head + 1) * AEXP):
            grad_value_all[:, head_cols(one)] = (whole * gates[:, one : one + 1]).astype(
                grad_value_all.dtype
            )
            put_gate(one, jnp.sum(value_all[:, head_cols(one)] * whole, axis=1, keepdims=True))
        if head == H - 1:
            lead_back[:, 2 * H * DH :] = (
                grad_gates[...] * gates[...] * (1.0 - sigs[...])
            ).astype(lead_back.dtype)

    tasks = [functools.partial(attend_back, head) for head in range(H)]
    tasks += [leave, arrive] + [functools.partial(finish, head) for head in range(H)]
    scatter_run(chunks, events, shared, ins, outs, send, recv, local, slots, place, core, tasks)


def scatter_call(kernel, parts, shared, plan, collective_id, more, made, scratch):
    chunks, events = plan
    count = len(parts)
    views = []
    for part, both in zip(parts, shared):
        rows = part.shape[0] // (math.prod(GRID) * (2 if both else 1))
        views.append(part.reshape(GRID + ((2,) if both else ()) + (rows, part.shape[1])))
    slots = []
    for which, _, wide, order in chunks:
        rows = views[which].shape[-2]
        if shared[which]:
            slots += [pltpu.VMEM(GRID + (rows, wide), jnp.bfloat16)] * 2
        else:
            lead = tuple(GRID[dim] for dim in range(3) if dim != order[0])
            slots.append(pltpu.VMEM(lead + (rows, wide), jnp.bfloat16))
        for phase in range(3):
            lead = tuple(GRID[dim] for dim in range(3) if dim not in order[: phase + 1])
            slots.append(
                pltpu.VMEM((GRID[order[phase]] - 1,) + lead + (rows, wide), jnp.bfloat16)
            )
    outs = pl.pallas_call(
        functools.partial(kernel, chunks, events, shared),
        out_shape=[jax.ShapeDtypeStruct(view.shape[-2:], jnp.float32) for view in views] + made,
        in_specs=[pl.BlockSpec(memory_space=pl.ANY)] * count
        + [pl.BlockSpec(memory_space=pltpu.VMEM)] * len(more),
        out_specs=[pl.BlockSpec(memory_space=pltpu.VMEM)] * (count + len(made)),
        scratch_shapes=[
            pltpu.SemaphoreType.DMA((len(chunks), 6)),
            pltpu.SemaphoreType.DMA((len(chunks), 6)),
            pltpu.SemaphoreType.DMA((len(chunks),)),
        ]
        + scratch
        + slots,
        compiler_params=pltpu.CompilerParams(
            collective_id=collective_id, has_side_effects=True, vmem_limit_bytes=62 * 1024 * 1024
        ),
    )(*views, *more)
    return (outs[:count], outs[count:])


def scatter_parts(parts, shared, plan, collective_id):
    if not by_grid():
        return [
            lax.psum_scatter(
                part.astype(jnp.float32),
                ("row", "col") if both else "row",
                scatter_dimension=0,
                tiled=True,
            )
            for part, both in zip(parts, shared)
        ]
    return scatter_call(scatter_kernel, parts, shared, plan, collective_id, [], [], [])[0]


def sibling(value):
    return lax.ppermute(value, "col", [(0, 1), (1, 0)])


def gather_col(value):
    if lax.axis_size("col") != 2:
        return lax.all_gather(value, "col", axis=0, tiled=True)
    core = lax.axis_index("col")
    rows = value.shape[0]
    whole = jnp.zeros((2 * rows,) + value.shape[1:], value.dtype)
    whole = lax.dynamic_update_slice_in_dim(whole, value, core * rows, 0)
    return lax.dynamic_update_slice_in_dim(whole, sibling(value), (1 - core) * rows, 0)


def scatter_col(total):
    if lax.axis_size("col") != 2:
        return lax.psum_scatter(total, "col", scatter_dimension=0, tiled=True)
    core = lax.axis_index("col")
    rows = total.shape[0] // 2
    leaving = lax.dynamic_slice_in_dim(total, (1 - core) * rows, rows, 0).astype(jnp.bfloat16)
    mine = lax.dynamic_slice_in_dim(total, core * rows, rows, 0)
    return mine + sibling(leaving).astype(jnp.float32)


def padded(value, wide):
    return jnp.pad(value, ((0, 0), (0, wide - value.shape[1])))


def norm_parts(values, gain):
    average = jnp.mean(values, axis=-1, keepdims=True)
    centred = values - average
    inv_std = lax.rsqrt(jnp.mean(centred * centred, axis=-1, keepdims=True) + EPS)
    normed = centred * inv_std
    return (normed * gain, normed, inv_std)


def norm_back(grad_in, gain, normed, inv_std):
    grad_hat = grad_in * gain
    mean_one = jnp.mean(grad_hat, axis=-1, keepdims=True)
    mean_two = jnp.mean(grad_hat * normed, axis=-1, keepdims=True)
    return inv_std * (grad_hat - mean_one - normed * mean_two)


def rope_tables(positions, width):
    half_width = width // 2
    freq = jnp.exp(jnp.arange(half_width).astype(jnp.float32) * (-2.0 * math.log(10000.0) / width))
    angle = positions.astype(jnp.float32)[:, None] * freq[None, :]
    return (jnp.cos(angle), jnp.sin(angle))


def rotate(values, cosine, sines):
    half_width = values.shape[-1] // 2
    front_half = values[..., :half_width]
    back_half = values[..., half_width:]
    cos_part = cosine[:, None, :]
    sin_part = sines[:, None, :]
    return jnp.concatenate(
        [
            front_half * cos_part - back_half * sin_part,
            back_half * cos_part + front_half * sin_part,
        ],
        axis=-1,
    )


def unrotate(values, cosine, sines):
    half_width = values.shape[-1] // 2
    front_half = values[..., :half_width]
    back_half = values[..., half_width:]
    cos_part = cosine[:, None, :]
    sin_part = sines[:, None, :]
    return jnp.concatenate(
        [
            front_half * cos_part + back_half * sin_part,
            back_half * cos_part - front_half * sin_part,
        ],
        axis=-1,
    )


def shards(
    block_input,
    teacher,
    lengths,
    head_routes,
    expert_routes,
    first_gain,
    query_weight,
    key_weight,
    value_weight,
    head_router,
    output_weight,
    second_gain,
    expert_router,
    expert_up,
    expert_down,
):
    tok_rows = block_input.shape[0]
    width = block_input.shape[1]
    col_count = lax.axis_size("col")
    col_index = lax.axis_index("col")
    total_rows = tok_rows * lax.axis_size("row") * col_count
    group_size = tok_rows * col_count
    seq_length = min(MAXLEN, group_size)
    key_span = seq_length // tok_rows
    gated = H * AEXP
    local_experts = expert_up.shape[0]
    hidden_local = expert_up.shape[2]
    hidden = local_experts * hidden_local
    length_sum = jnp.sum(lengths)
    small_parts = [
        query_weight,
        key_weight,
        head_router,
        first_gain[:, None],
        second_gain[:, None],
    ]
    for digits in (length_sum // 64, length_sum % 64):
        small_parts.append(
            jnp.broadcast_to(digits.astype(jnp.bfloat16)[None, None], (first_gain.shape[0], 1))
        )
    lead_local = padded(jnp.concatenate(small_parts, axis=1), 2 * H * DH + 128)
    up_local = jnp.concatenate(
        [
            jnp.transpose(expert_up, (1, 0, 2)).reshape(-1, hidden),
            padded(expert_router, 128),
        ],
        axis=1,
    )
    down_local = jnp.transpose(expert_down, (2, 0, 1)).reshape(-1, hidden)
    lead_full, value_full = gather_parts(
        [lead_local, value_weight], [True, True], LEAD_GATHER, 1
    )
    rest_local = [output_weight.T, up_local, down_local]
    rest_shared = [True, False, False]
    paired = by_grid() and key_span == 2 and lengths.shape[0] == 1
    extra_at = 2 * H * DH + 2 * gated
    extra = lead_full[:, extra_at : extra_at + 4].astype(jnp.float32)
    gain_one = extra[:, 0]
    gain_two = extra[:, 1]
    stride = first_gain.shape[0] * col_count
    token_count = jnp.sum(extra[::stride, 2]) * 64.0 + jnp.sum(extra[::stride, 3])
    local_ids = jnp.arange(tok_rows, dtype=jnp.int32)
    group_ids = col_index * tok_rows + local_ids
    seq_pos = group_ids % seq_length
    seq_ids = group_ids // seq_length
    seq_slots = jnp.arange(lengths.shape[0], dtype=jnp.int32)
    tok_length = jnp.sum(
        jnp.where(seq_ids[:, None] == seq_slots[None, :], lengths[None, :], 0), axis=1
    )
    valid = (seq_pos < tok_length).astype(jnp.float32)
    inputs_full = block_input.astype(jnp.float32)
    normed_one, hat_one, inv_one = norm_parts(inputs_full, gain_one)
    normed_low = normed_one.astype(jnp.bfloat16)
    lead_raw = jnp.dot(normed_low, lead_full, preferred_element_type=jnp.float32)
    cosine, sines = rope_tables(seq_pos, DH)
    chosen = jnp.any(
        head_routes[:, :, :, None] == jnp.arange(AEXP, dtype=jnp.int32)[None, None, None, :], axis=2
    ).astype(jnp.float32)
    value_flat = jnp.dot(block_input, value_full, preferred_element_type=jnp.float32)
    if paired:
        sigs = jax.nn.sigmoid(lead_raw[:, 2 * H * DH :])
        picked = chosen.reshape(tok_rows, gated)
        both_gates = sigs * padded(jnp.concatenate([picked, picked], axis=1), 128)
        cos_wide = jnp.concatenate([cosine, cosine], axis=1)
        sin_wide = jnp.concatenate([-sines, sines], axis=1)
        limits = jnp.broadcast_to(lengths[:, None], (8, 128))
        low, full = (jnp.bfloat16, jnp.float32)
        made = [jax.ShapeDtypeStruct((tok_rows, H * DH), kind) for kind in [low] * 5 + [full] * 2]
        made.append(jax.ShapeDtypeStruct((tok_rows, gated * DH), low))
        (output_turned, up_wide, down_turned), kept = gather_call(
            attend_kernel,
            rest_local,
            rest_shared,
            REST_GATHER,
            2,
            [lead_raw, value_flat, both_gates, cos_wide, sin_wide, limits],
            made,
            [pltpu.SemaphoreType.DMA((2,))] * 2,
        )
        mixed_low = kept[7]
    else:
        output_turned, up_wide, down_turned = gather_parts(
            rest_local, rest_shared, REST_GATHER, 2
        )
        query_raw = lead_raw[:, : H * DH]
        key_raw = lead_raw[:, H * DH : 2 * H * DH]
        route_logits = lead_raw[:, 2 * H * DH : extra_at]
        query_scale = DH ** (-0.5)
        query_rot = (rotate(query_raw.reshape(tok_rows, H, DH), cosine, sines) * query_scale).astype(
            jnp.bfloat16
        )
        key_rot = rotate(key_raw.reshape(tok_rows, H, DH), cosine, sines).astype(jnp.bfloat16)
        value_sig = jax.nn.sigmoid(route_logits[:, :gated]).reshape(tok_rows, H, AEXP)
        output_sig = jax.nn.sigmoid(route_logits[:, gated:]).reshape(tok_rows, H, AEXP)
        value_gates = value_sig * chosen
        output_gates = output_sig * chosen
        value_all = value_flat.reshape(tok_rows, H, AEXP, DH)
        values_low = jnp.sum(value_all * value_gates[..., None], axis=2).astype(jnp.bfloat16)
        key_parts = [key_rot]
        value_parts = [values_low]
        id_parts = [group_ids]
        for offset in range(1, key_span):
            came_keys, came_values = shifted((key_rot, values_low), "col", offset)
            key_parts.append(came_keys)
            value_parts.append(came_values)
            id_parts.append(group_ids - offset * tok_rows)
        keys_all = jnp.concatenate(key_parts, axis=0)
        values_all = jnp.concatenate(value_parts, axis=0)
        key_ids = jnp.concatenate(id_parts, axis=0)
        allowed = (
            (key_ids[None, :] // seq_length == seq_ids[:, None])
            & (key_ids[None, :] <= group_ids[:, None])
            & (key_ids[None, :] % seq_length < tok_length[:, None])
        )

        def head_scores(head_idx):
            raw_scores = jnp.einsum(
                "qd,kd->qk",
                query_rot[:, head_idx],
                keys_all[:, head_idx],
                preferred_element_type=jnp.float32,
            )
            return jnp.where(allowed, raw_scores, MASKED)

        attended_list = []
        lse_list = []
        for head_idx in range(H):
            scores = head_scores(head_idx)
            row_top = jnp.max(scores, axis=1, keepdims=True)
            exponent = jnp.exp(scores - row_top)
            row_total = jnp.sum(exponent, axis=1, keepdims=True)
            probs_low = (exponent / row_total).astype(jnp.bfloat16)
            attended_list.append(
                jnp.dot(probs_low, values_all[:, head_idx], preferred_element_type=jnp.float32)
            )
            lse_list.append(row_top + jnp.log(row_total))
        attended = jnp.stack(attended_list, axis=1)
        mixed_low = (
            (attended[:, :, None, :] * output_gates[..., None])
            .astype(jnp.bfloat16)
            .reshape(tok_rows, gated * DH)
        )
    up_full = up_wide[:, :hidden]
    router_cols = up_wide[:, hidden : hidden + local_experts]
    resid = inputs_full + contract_last(mixed_low, output_turned)
    resid_low = resid.astype(jnp.bfloat16)
    group_in = gather_col(resid_low)
    normed_two, hat_two, inv_two = norm_parts(group_in.astype(jnp.float32), gain_two)
    normed_two_low = normed_two.astype(jnp.bfloat16)
    gates = jax.nn.sigmoid(jnp.dot(normed_two_low, router_cols, preferred_element_type=jnp.float32))
    expert_ids = col_index * local_experts + jnp.arange(local_experts, dtype=jnp.int32)
    member = jnp.any(expert_routes[:, :, None] == expert_ids[None, None, :], axis=1)
    used_gates = gates * member.astype(jnp.float32)

    def spread(columns):
        return jnp.repeat(columns, hidden_local, axis=1)

    inner = jnp.dot(group_in, up_full, preferred_element_type=jnp.float32)
    active = jnp.maximum(inner, 0.0).astype(jnp.bfloat16)
    gated_active = (active.astype(jnp.float32) * spread(used_gates)).astype(jnp.bfloat16)
    expert_sum = scatter_col(contract_last(gated_active, down_turned))
    output_full_rows = resid + expert_sum
    block_output = output_full_rows.astype(jnp.bfloat16)
    ratio = total_rows / token_count
    grad_output = ratio * (output_full_rows - teacher.astype(jnp.float32)) * valid[:, None]
    grad_output_low = grad_output.astype(jnp.bfloat16)
    group_grad = gather_col(grad_output_low)
    grad_hidden = jnp.dot(group_grad, down_turned, preferred_element_type=jnp.float32)
    gate_grad = jnp.sum(
        (active.astype(jnp.float32) * grad_hidden).reshape(group_size, local_experts, hidden_local),
        axis=2,
    )
    grad_inner = jnp.where(active > 0, grad_hidden * spread(used_gates), 0.0).astype(jnp.bfloat16)
    down_grad = contract_first(group_grad, gated_active).astype(jnp.bfloat16)
    up_grad = contract_first(group_in, grad_inner).astype(jnp.bfloat16)
    slot_back = contract_last(grad_inner, up_full)
    logit_low = (gate_grad * used_gates * (1.0 - gates)).astype(jnp.bfloat16)
    router_grad = contract_first(normed_two_low, padded(logit_low, 128)).astype(jnp.bfloat16)
    grad_norm_two = contract_last(logit_low, router_cols)
    second_gain_part = jnp.sum(grad_norm_two * hat_two, axis=0)
    grad_rows = slot_back + norm_back(grad_norm_two, gain_two, hat_two, inv_two)
    moe_grad = scatter_col(grad_rows)
    grad_resid = grad_output + moe_grad
    grad_branch = grad_resid.astype(jnp.bfloat16)
    output_grad = contract_first(grad_branch, mixed_low).astype(jnp.bfloat16)
    grad_mixed_low = jnp.dot(
        grad_branch, output_turned, preferred_element_type=jnp.float32
    ).astype(jnp.bfloat16)
    rest_grads = [output_grad, up_grad, router_grad, down_grad]
    rest_shared = [True, False, False, False]
    if paired:
        wide = (tok_rows, H * DH)
        sums, (lead_back, grad_value_all) = scatter_call(
            attend_back_kernel,
            rest_grads,
            rest_shared,
            REST_SCATTER,
            3,
            list(kept[:7])
            + [grad_mixed_low, value_flat, both_gates, sigs, cos_wide, sin_wide, limits],
            [
                jax.ShapeDtypeStruct((tok_rows, 2 * H * DH + 128), low),
                jax.ShapeDtypeStruct((tok_rows, gated * DH), low),
            ],
            [pltpu.SemaphoreType.DMA((2,))] * 2
            + [pltpu.VMEM(wide, full)] * 2
            + [pltpu.VMEM((tok_rows, 128), full)]
            + [pltpu.VMEM(wide, low)] * 4,
        )
    else:
        sums = scatter_parts(rest_grads, rest_shared, REST_SCATTER, 3)
        grad_mixed = grad_mixed_low.astype(jnp.float32).reshape(tok_rows, H, AEXP, DH)
        grad_attended = jnp.sum(grad_mixed * output_gates[..., None], axis=2).astype(jnp.bfloat16)
        grad_output_gates = jnp.sum(grad_mixed * attended[:, :, None, :], axis=3)
        query_grads = []
        key_grads = []
        value_grads = []
        for head_idx in range(H):
            scores = head_scores(head_idx)
            probs_full = jnp.exp(scores - lse_list[head_idx])
            probs_low = probs_full.astype(jnp.bfloat16)
            grad_probs = jnp.einsum(
                "qd,kd->qk",
                grad_attended[:, head_idx],
                values_all[:, head_idx],
                preferred_element_type=jnp.float32,
            )
            grad_scores = (
                probs_full * (grad_probs - jnp.sum(probs_full * grad_probs, axis=1, keepdims=True))
            ).astype(jnp.bfloat16)
            query_grads.append(
                jnp.dot(grad_scores, keys_all[:, head_idx], preferred_element_type=jnp.float32)
            )
            key_grads.append(contract_first(grad_scores, query_rot[:, head_idx]))
            value_grads.append(contract_first(probs_low, grad_attended[:, head_idx]))
        grad_queries = jnp.stack(query_grads, axis=1)
        key_grads_all = jnp.stack(key_grads, axis=1)
        value_grads_all = jnp.stack(value_grads, axis=1)
        grad_key_rot = key_grads_all[:tok_rows]
        grad_values = value_grads_all[:tok_rows]
        for offset in range(1, key_span):
            back_keys, back_values = (
                shifted(
                    key_grads_all[offset * tok_rows : (offset + 1) * tok_rows].astype(jnp.bfloat16),
                    "col",
                    -offset,
                ).astype(jnp.float32),
                shifted(
                    value_grads_all[offset * tok_rows : (offset + 1) * tok_rows].astype(jnp.bfloat16),
                    "col",
                    -offset,
                ).astype(jnp.float32),
            )
            grad_key_rot = grad_key_rot + back_keys
            grad_values = grad_values + back_values
        grad_value_all = (
            (grad_values[:, :, None, :] * value_gates[..., None])
            .astype(jnp.bfloat16)
            .reshape(tok_rows, gated * DH)
        )
        grad_value_gates = jnp.sum(value_all * grad_values[:, :, None, :], axis=3)
        grad_query_raw = (
            unrotate(grad_queries * query_scale, cosine, sines)
            .astype(jnp.bfloat16)
            .reshape(tok_rows, H * DH)
        )
        grad_key_raw = (
            unrotate(grad_key_rot, cosine, sines).astype(jnp.bfloat16).reshape(tok_rows, H * DH)
        )
        grad_route = jnp.concatenate(
            [
                (grad_value_gates * chosen * value_sig * (1.0 - value_sig)).reshape(tok_rows, gated),
                (grad_output_gates * chosen * output_sig * (1.0 - output_sig)).reshape(tok_rows, gated),
            ],
            axis=1,
        ).astype(jnp.bfloat16)
        lead_back = padded(
            jnp.concatenate([grad_query_raw, grad_key_raw, grad_route], axis=1), 2 * H * DH + 128
        )
    output_turned_sum, up_sum, router_sum, down_sum = sums
    value_grad = contract_first(block_input, grad_value_all).astype(jnp.bfloat16)
    grad_norm_one = contract_last(lead_back, lead_full)
    first_gain_part = jnp.sum(grad_norm_one * hat_one, axis=0)
    input_grad = (
        grad_resid
        + norm_back(grad_norm_one, gain_one, hat_one, inv_one)
        + contract_last(grad_value_all, value_full)
    )
    lead_cols = jnp.arange(2 * H * DH + 128, dtype=jnp.int32)[None, :]
    lead_grad = (
        contract_first(normed_low, lead_back)
        + jnp.where(lead_cols == extra_at, first_gain_part[:, None], 0.0)
        + jnp.where(lead_cols == extra_at + 1, second_gain_part[:, None], 0.0)
    ).astype(jnp.bfloat16)
    lead_sum, value_sum = scatter_parts([lead_grad, value_grad], [True, True], LEAD_SCATTER, 4)
    output_sum = output_turned_sum.T
    router_sum = router_sum[:, :local_experts]
    up_out = jnp.transpose(up_sum.reshape(-1, local_experts, hidden_local), (1, 0, 2))
    down_out = jnp.transpose(down_sum.reshape(-1, local_experts, hidden_local), (1, 2, 0))
    query_sum = lead_sum[:, : H * DH]
    key_sum = lead_sum[:, H * DH : 2 * H * DH]
    router_head_sum = lead_sum[:, 2 * H * DH : extra_at]
    first_sum = lead_sum[:, extra_at]
    second_sum = lead_sum[:, extra_at + 1]
    return (
        block_output,
        input_grad,
        first_sum,
        query_sum,
        key_sum,
        value_sum,
        router_head_sum,
        output_sum,
        second_sum,
        router_sum,
        up_out,
        down_out,
    )


def solution(mesh):
    return jax.shard_map(
        shards,
        mesh=mesh,
        in_specs=(
            P(("row", "col"), None),
            P(("row", "col"), None),
            P("row"),
            P(("row", "col"), None, None),
            P("row", None),
            P(("row", "col")),
            P(("row", "col"), None),
            P(("row", "col"), None),
            P(("row", "col"), None),
            P(("row", "col"), None),
            P(None, ("row", "col")),
            P(("row", "col")),
            P("row", "col"),
            P("col", "row", None),
            P("col", None, "row"),
        ),
        out_specs=(
            P(("row", "col"), None),
            P(("row", "col"), None),
            P(("row", "col")),
            P(("row", "col"), None),
            P(("row", "col"), None),
            P(("row", "col"), None),
            P(("row", "col"), None),
            P(None, ("row", "col")),
            P(("row", "col")),
            P("row", "col"),
            P("col", "row", None),
            P("col", None, "row"),
        ),
        check_vma=False,
    )
```

```python
import functools
import math

import jax
import jax.numpy as jnp
from jax import lax
from jax.experimental import pallas as pl
from jax.experimental.pallas import tpu as pltpu
from jax.sharding import PartitionSpec as P

H = 4
DH = 128
AEXP = 5
MAXLEN = 2048


EPS = 1e-05
MASKED = -1e30


def shifted(value, axis, steps):
    count = lax.axis_size(axis)
    leading, last = (max(0, -steps), min(count, count - steps))
    return lax.ppermute(value, axis, [(source, source + steps) for source in range(leading, last)])


def contract_last(left, right):
    return lax.dot_general(
        left, right, (((1,), (1,)), ((), ())), preferred_element_type=jnp.float32
    )


def contract_first(left, right):
    return lax.dot_general(
        left, right, (((0,), (0,)), ((), ())), preferred_element_type=jnp.float32
    )


GRID = (4, 2, 2)
MESH = pl.DeviceIdType.MESH
LEAD_GATHER = (
    (
        (0, 0, 384, (0, 1, 2)),
        (1, 0, 512, (2, 1, 0)),
        (1, 512, 768, (1, 0, 2)),
        (1, 1280, 640, (0, 2, 1)),
        (1, 1920, 640, (0, 1, 2)),
        (0, 384, 768, (0, 2, 1)),
    ),
    (
        (0, 0),
        (1, 0),
        (2, 0),
        (3, 0),
        (4, 0),
        (5, 0),
        (1, 1),
        (2, 1),
        (0, 1),
        (1, 2),
        (3, 1),
        (0, 2),
        (4, 1),
        (3, 2),
        (5, 1),
        (4, 2),
        (0, 3),
        (5, 2),
        (3, 3),
        (2, 2),
        (4, 3),
        (5, 3),
        (1, 3),
        (2, 3),
    ),
)
REST_GATHER = (
    (
        (0, 0, 1024, (0, 2, 1)),
        (0, 1024, 512, (0, 1, 2)),
        (2, 0, 896, (1, 0, 2)),
        (1, 0, 384, (0, 1, 2)),
        (0, 1536, 1024, (0, 2, 1)),
        (2, 896, 512, (1, 2, 0)),
        (1, 384, 1152, (0, 2, 1)),
        (1, 1536, 640, (0, 1, 2)),
        (2, 1408, 640, (0, 2, 1)),
    ),
    (
        (0, 0),
        (1, 0),
        (2, 0),
        (3, 0),
        (4, 0),
        (5, 0),
        (6, 0),
        (7, 0),
        (8, 0),
        (2, 1),
        (5, 1),
        (0, 1),
        (1, 1),
        (5, 2),
        (3, 1),
        (1, 2),
        (0, 2),
        (4, 1),
        (3, 2),
        (1, 3),
        (4, 2),
        (0, 3),
        (6, 1),
        (7, 1),
        (4, 3),
        (8, 1),
        (6, 2),
        (7, 2),
        (8, 2),
        (2, 2),
    ),
)
REST_SCATTER = (
    (
        (0, 0, 1536, (1, 2, 0)),
        (3, 0, 1024, (1, 2, 0)),
        (1, 0, 768, (1, 2, 0)),
        (2, 0, 128, (1, 2, 0)),
        (3, 1024, 640, (2, 0, 1)),
        (1, 768, 768, (2, 0, 1)),
        (1, 1536, 512, (0, 1, 2)),
        (0, 1536, 1024, (1, 2, 0)),
        (3, 1664, 384, (2, 1, 0)),
    ),
    (
        (1, 0),
        (2, 0),
        (3, 0),
        (4, 0),
        (5, 0),
        (6, 0),
        (8, 0),
        (0, 0),
        (7, 0),
        (4, 1),
        (6, 1),
        (1, 1),
        (5, 1),
        (4, 2),
        (8, 1),
        (2, 1),
        (3, 1),
        (1, 2),
        (5, 2),
        (2, 2),
        (0, 1),
        (3, 2),
        (0, 2),
        (7, 1),
        (6, 2),
        (7, 2),
        (8, 2),
    ),
)
LEAD_SCATTER = (
    (
        (0, 0, 512, (0, 2, 1)),
        (1, 0, 640, (1, 0, 2)),
        (1, 640, 896, (2, 1, 0)),
        (0, 512, 640, (1, 0, 2)),
        (1, 1536, 640, (2, 1, 0)),
        (1, 2176, 384, (2, 1, 0)),
    ),
    (
        (0, 0),
        (1, 0),
        (2, 0),
        (3, 0),
        (4, 0),
        (1, 1),
        (5, 0),
        (0, 1),
        (2, 1),
        (3, 1),
        (1, 2),
        (4, 1),
        (2, 2),
        (3, 2),
        (5, 1),
        (0, 2),
        (4, 2),
        (5, 2),
    ),
)


def by_grid():
    return lax.axis_size("row") == math.prod(GRID) and lax.axis_size("col") == 2


def places():
    row = lax.axis_index("row")
    return (row // 4, (row // 2) % 2, row % 2)


def row_of(place):
    return (place[0] * 2 + place[1]) * 2 + place[2]


def moved(place, dim, steps):
    there = list(place)
    there[dim] = lax.rem(place[dim] + steps, GRID[dim])
    return row_of(there)


def greet(place, core):
    barrier = pltpu.get_barrier_semaphore()
    partners = [(moved(place, dim, k), core) for dim in range(3) for k in range(1, GRID[dim])]
    partners.append((row_of(place), 1 - core))
    for row, col in partners:
        pl.semaphore_signal(barrier, inc=1, device_id={"row": row, "col": col}, device_id_type=MESH)
    pl.semaphore_wait(barrier, len(partners))


def push(source, target, send, recv, row, core):
    copy = pltpu.make_async_remote_copy(
        source, target, send, recv, device_id={"row": row, "col": core}, device_id_type=MESH
    )
    copy.start()
    return copy


def head_cols(head):
    return slice(head * DH, (head + 1) * DH)


def half_turned(values, cosine, sines):
    return values * cosine + pltpu.roll(values, DH // 2, 1) * sines


def masked_pair(queries, keys, others, limits, core):
    rows = queries.shape[0]
    query_at = core * rows + lax.broadcasted_iota(jnp.int32, (rows, rows), 0)
    key_at = lax.broadcasted_iota(jnp.int32, (rows, rows), 1)
    scores = []
    for block, start in ((keys, core * rows), (others, (1 - core) * rows)):
        place = start + key_at
        allowed = (place <= query_at) & (place < limits)
        scores.append(jnp.where(allowed, contract_last(queries, block), MASKED))
    return scores


def gather_run(chunks, events, shared, ins, outs, send, recv, local, place, core, tasks):
    owns = []
    for n in range(len(shared)):
        at = tuple(place) + ((core,) if shared[n] else ())
        owns.append(pltpu.make_async_copy(ins[n], outs[n].at[at], local.at[n]))
        owns[-1].start()
    sent, flying, left = ([], {}, list(tasks))
    early = sum(1 for _, phase in events if phase == 0)
    waited = False
    for step, (i, phase) in enumerate(events):
        if left and step >= early and (step - early) % 2 == 0:
            left.pop(0)()
        which, start, wide, order = chunks[i]
        if phase == 1 and not waited:
            for copy in owns:
                copy.wait()
            waited = True
        for copy in flying.pop(i, []):
            copy.wait_recv()
        held = order[:phase]
        at = [slice(None) if dim in held else place[dim] for dim in range(3)]
        at += [core] if shared[which] else []
        block = outs[which].at[tuple(at) + (slice(None), pl.ds(start, wide))]
        if phase == 3:
            flying[i] = [push(block, block, send.at[i, 5], recv.at[i, 5], row_of(place), 1 - core)]
        else:
            dim = order[phase]
            source = ins[which].at[:, pl.ds(start, wide)] if phase == 0 else block
            slot = (0, 3, 4)[dim]
            flying[i] = [
                push(
                    source,
                    block,
                    send.at[i, slot + k - 1],
                    recv.at[i, slot + k - 1],
                    moved(place, dim, k),
                    core,
                )
                for k in range(1, GRID[dim])
            ]
        sent += flying[i]
    for task in left:
        task()
    for copies in flying.values():
        for copy in copies:
            copy.wait_recv()
    for copy in sent:
        copy.wait_send()


def gather_kernel(chunks, events, shared, *refs):
    count = len(shared)
    place, core = (places(), lax.axis_index("col"))
    greet(place, core)
    gather_run(
        chunks, events, shared, refs[:count], refs[count : 2 * count], *refs[2 * count :], place, core, ()
    )


def attend_kernel(chunks, events, shared, *refs):
    count = len(shared)
    ins, refs = (refs[:count], refs[count:])
    lead, value_all, gates, cosine, sines, limits = refs[:6]
    outs, refs = (refs[6 : 6 + count], refs[6 + count :])
    query, key, value, key_other, value_other, attended, lse, mixed = refs[:8]
    send, recv, local, side_send, side_recv = refs[8:]
    place, core = (places(), lax.axis_index("col"))
    greet(place, core)
    side = []

    def make_keys():
        for head in range(H):
            at = head_cols(head)
            shift = slice(H * DH + head * DH, H * DH + (head + 1) * DH)
            key[:, at] = half_turned(lead[:, shift], cosine[...], sines[...]).astype(key.dtype)

    def make_values():
        for head in range(H):
            total = None
            for one in range(head * AEXP, (head + 1) * AEXP):
                term = value_all[:, head_cols(one)] * gates[:, one : one + 1]
                total = term if total is None else total + term
            value[:, head_cols(head)] = total.astype(value.dtype)

    def make_queries():
        row, col = (row_of(place), 1 - core)
        side.append(push(key, key_other, side_send.at[0], side_recv.at[0], row, col))
        side.append(push(value, value_other, side_send.at[1], side_recv.at[1], row, col))
        for head in range(H):
            at = head_cols(head)
            turned = half_turned(lead[:, at], cosine[...], sines[...]) * DH ** (-0.5)
            query[:, at] = turned.astype(query.dtype)

    def arrive():
        for copy in side:
            copy.wait()

    def attend(head):
        at = head_cols(head)
        near, far = masked_pair(query[:, at], key[:, at], key_other[:, at], limits[0:1, 0:1], core)
        top = jnp.maximum(
            jnp.max(near, axis=1, keepdims=True), jnp.max(far, axis=1, keepdims=True)
        )
        near, far = (jnp.exp(near - top), jnp.exp(far - top))
        total = jnp.sum(near, axis=1, keepdims=True) + jnp.sum(far, axis=1, keepdims=True)
        near, far = ((near / total).astype(jnp.bfloat16), (far / total).astype(jnp.bfloat16))
        out = jnp.dot(near, value[:, at], preferred_element_type=jnp.float32) + jnp.dot(
            far, value_other[:, at], preferred_element_type=jnp.float32
        )
        attended[:, at] = out
        lse[:, at] = jnp.broadcast_to(top + jnp.log(total), out.shape)
        for one in range(head * AEXP, (head + 1) * AEXP):
            gate = gates[:, H * AEXP + one : H * AEXP + one + 1]
            mixed[:, head_cols(one)] = (out * gate).astype(mixed.dtype)

    tasks = [make_keys, make_values, make_queries, arrive]
    tasks += [functools.partial(attend, head) for head in range(H)]
    gather_run(chunks, events, shared, ins, outs, send, recv, local, place, core, tasks)


def gather_call(kernel, parts, shared, plan, collective_id, more, made, scratch):
    chunks, events = plan
    count = len(parts)
    outs = pl.pallas_call(
        functools.partial(kernel, chunks, events, shared),
        out_shape=[
            jax.ShapeDtypeStruct(GRID + ((2,) if both else ()) + part.shape, part.dtype)
            for part, both in zip(parts, shared)
        ]
        + made,
        in_specs=[pl.BlockSpec(memory_space=pltpu.VMEM)] * (count + len(more)),
        out_specs=[pl.BlockSpec(memory_space=pl.ANY)] * count
        + [pl.BlockSpec(memory_space=pltpu.VMEM)] * len(made),
        scratch_shapes=[
            pltpu.SemaphoreType.DMA((len(chunks), 6)),
            pltpu.SemaphoreType.DMA((len(chunks), 6)),
            pltpu.SemaphoreType.DMA((count,)),
        ]
        + scratch,
        compiler_params=pltpu.CompilerParams(
            collective_id=collective_id, has_side_effects=True, vmem_limit_bytes=60 * 1024 * 1024
        ),
    )(*parts, *more)
    whole = [out.reshape(-1, part.shape[1]) for out, part in zip(outs, parts)]
    return (whole, outs[count:])


def gather_parts(parts, shared, plan, collective_id):
    if not by_grid():
        return [
            lax.all_gather(part, ("row", "col") if both else "row", axis=0, tiled=True)
            for part, both in zip(parts, shared)
        ]
    return gather_call(gather_kernel, parts, shared, plan, collective_id, [], [], [])[0]


def add_blocks(target, terms, lead, rows):
    steps = rows // 16

    def body(step, carry):
        block, part = (step // steps, (step % steps) * 16)
        at = []
        for size in lead[::-1]:
            at.insert(0, block % size)
            block = block // size
        at = tuple(at) + (pl.ds(pl.multiple_of(part, 16), 16),)
        total = terms[0][at].astype(jnp.float32)
        for term in terms[1:]:
            total = total + term[at].astype(jnp.float32)
        target[at] = total.astype(target.dtype)
        return carry

    lax.fori_loop(0, math.prod(lead) * steps, body, 0)


def scatter_run(chunks, events, shared, ins, outs, send, recv, local, slots, place, core, tasks):
    slots, rest = (list(slots), list(tasks))
    held = {}
    for i in range(len(chunks)):
        held[i] = [slots.pop(0) for _ in range(5 if shared[chunks[i][0]] else 4)]
    sent, flying, owns = ([], {}, {})

    for i in dict.fromkeys(i for i, _ in events):
        which, start, wide, order = chunks[i]
        cols = pl.ds(start, wide)
        if shared[which]:
            own = ins[which].at[:, :, :, core, :, cols]
            other = ins[which].at[:, :, :, 1 - core, :, cols]
            flying[i] = [
                push(other, held[i][1], send.at[i, 5], recv.at[i, 5], row_of(place), 1 - core)
            ]
            sent += flying[i]
        else:
            at = [slice(None)] * 3
            at[order[0]] = place[order[0]]
            own = ins[which].at[tuple(at) + (slice(None), cols)]
        owns[i] = pltpu.make_async_copy(own, held[i][0], local.at[i])
        owns[i].start()

    def source_of(i, phase):
        which, start, wide, order = chunks[i]
        if phase == 0:
            return held[i][1] if shared[which] else ins[which].at[:, :, :, :, pl.ds(start, wide)]
        return held[i][-3 + phase - 1].at[0]

    def landed(i, phase):
        which, start, wide, order = chunks[i]
        rows = outs[which].shape[0]
        for copy in flying.pop(i):
            copy.wait_recv()
        if phase < 0:
            owns[i].wait()
            add_blocks(held[i][1], [held[i][0], held[i][1]], list(GRID), rows)
            return
        dim = order[phase]
        came = held[i][-3 + phase]
        if phase == 0 and not shared[which]:
            owns[i].wait()
            own = held[i][0]
        else:
            left = [d for d in range(3) if d not in order[:phase]]
            own = source_of(i, phase).at[tuple(place[dim] if d == dim else slice(None) for d in left)]
        target = outs[which].at[:, pl.ds(start, wide)] if phase == 2 else came.at[0]
        terms = [own] + [came.at[k] for k in range(GRID[dim] - 1)]
        lead = [GRID[d] for d in range(3) if d not in order[: phase + 1]]
        add_blocks(target, terms, lead, rows)

    early = sum(1 for i, phase in events if phase == 0 and not shared[chunks[i][0]])
    for step, (i, phase) in enumerate(events):
        if rest and step >= early and (step - early) % 2 == 0:
            rest.pop(0)()
        which, start, wide, order = chunks[i]
        if phase > 0 or shared[which]:
            landed(i, phase - 1)
        dim = order[phase]
        left = [d for d in range(3) if d not in order[:phase]]
        slot = (0, 3, 4)[dim]
        flying[i] = []
        for k in range(1, GRID[dim]):
            there = lax.rem(place[dim] + k, GRID[dim])
            at = tuple(there if d == dim else slice(None) for d in left)
            flying[i].append(
                push(
                    source_of(i, phase).at[at],
                    held[i][-3 + phase].at[k - 1],
                    send.at[i, slot + k - 1],
                    recv.at[i, slot + k - 1],
                    moved(place, dim, k),
                    core,
                )
            )
        sent += flying[i]
    for task in rest:
        task()
    for i in list(flying):
        landed(i, 2)
    for copy in sent:
        copy.wait_send()


def scatter_kernel(chunks, events, shared, *refs):
    count = len(shared)
    ins, outs = (refs[:count], refs[count : 2 * count])
    send, recv, local = refs[2 * count : 2 * count + 3]
    place, core = (places(), lax.axis_index("col"))
    greet(place, core)
    slots = refs[2 * count + 3 :]
    scatter_run(chunks, events, shared, ins, outs, send, recv, local, slots, place, core, ())


def attend_back_kernel(chunks, events, shared, *refs):
    count = len(shared)
    ins, refs = (refs[:count], refs[count:])
    query, key, value, key_other, value_other, attended, lse, grad_mixed = refs[:8]
    value_all, gates, sigs, cosine, sines, limits = refs[8:14]
    outs, refs = (refs[14 : 14 + count], refs[14 + count :])
    lead_back, grad_value_all = refs[:2]
    send, recv, local, side_send, side_recv = refs[2:7]
    grad_key, grad_value, grad_gates, key_leave, value_leave, key_came, value_came = refs[7:14]
    slots = refs[14:]
    place, core = (places(), lax.axis_index("col"))
    greet(place, core)
    side = []
    gated = H * AEXP

    def put_gate(one, column):
        lanes = lax.broadcasted_iota(jnp.int32, grad_gates.shape, 1)
        grad_gates[...] = jnp.where(lanes == one, column, grad_gates[...])

    def attend_back(head):
        at = head_cols(head)
        if head == 0:
            grad_gates[...] = jnp.zeros_like(grad_gates)
        total = None
        for one in range(head * AEXP, (head + 1) * AEXP):
            gate = gates[:, gated + one : gated + one + 1]
            piece = grad_mixed[:, head_cols(one)].astype(jnp.float32)
            put_gate(gated + one, jnp.sum(piece * attended[:, at], axis=1, keepdims=True))
            total = piece * gate if total is None else total + piece * gate
        grad_out = total.astype(jnp.bfloat16)
        queries, keys, others = (query[:, at], key[:, at], key_other[:, at])
        near, far = masked_pair(queries, keys, others, limits[0:1, 0:1], core)
        level = lse[:, head * DH : head * DH + 1]
        near, far = (jnp.exp(near - level), jnp.exp(far - level))
        near_grad = contract_last(grad_out, value[:, at])
        far_grad = contract_last(grad_out, value_other[:, at])
        mean = jnp.sum(near * near_grad, axis=1, keepdims=True) + jnp.sum(
            far * far_grad, axis=1, keepdims=True
        )
        near_grad = (near * (near_grad - mean)).astype(jnp.bfloat16)
        far_grad = (far * (far_grad - mean)).astype(jnp.bfloat16)
        near, far = (near.astype(jnp.bfloat16), far.astype(jnp.bfloat16))
        grad_query = jnp.dot(near_grad, keys, preferred_element_type=jnp.float32) + jnp.dot(
            far_grad, others, preferred_element_type=jnp.float32
        )
        turned = half_turned(grad_query * DH ** (-0.5), cosine[...], -sines[...])
        lead_back[:, at] = turned.astype(lead_back.dtype)
        grad_key[:, at] = contract_first(near_grad, queries)
        grad_value[:, at] = contract_first(near, grad_out)
        key_leave[:, at] = contract_first(far_grad, queries).astype(key_leave.dtype)
        value_leave[:, at] = contract_first(far, grad_out).astype(value_leave.dtype)

    def leave():
        row, col = (row_of(place), 1 - core)
        side.append(push(key_leave, key_came, side_send.at[0], side_recv.at[0], row, col))
        side.append(push(value_leave, value_came, side_send.at[1], side_recv.at[1], row, col))

    def arrive():
        for copy in side:
            copy.wait()

    def finish(head):
        at = head_cols(head)
        turned = half_turned(
            grad_key[:, at] + key_came[:, at].astype(jnp.float32), cosine[...], -sines[...]
        )
        lead_back[:, H * DH + head * DH : H * DH + (head + 1) * DH] = turned.astype(lead_back.dtype)
        whole = grad_value[:, at] + value_came[:, at].astype(jnp.float32)
        for one in range(head * AEXP, (head + 1) * AEXP):
            grad_value_all[:, head_cols(one)] = (whole * gates[:, one : one + 1]).astype(
                grad_value_all.dtype
            )
            put_gate(one, jnp.sum(value_all[:, head_cols(one)] * whole, axis=1, keepdims=True))
        if head == H - 1:
            lead_back[:, 2 * H * DH :] = (
                grad_gates[...] * gates[...] * (1.0 - sigs[...])
            ).astype(lead_back.dtype)

    tasks = [functools.partial(attend_back, head) for head in range(H)]
    tasks += [leave, arrive] + [functools.partial(finish, head) for head in range(H)]
    scatter_run(chunks, events, shared, ins, outs, send, recv, local, slots, place, core, tasks)


def scatter_call(kernel, parts, shared, plan, collective_id, more, made, scratch):
    chunks, events = plan
    count = len(parts)
    views = []
    for part, both in zip(parts, shared):
        rows = part.shape[0] // (math.prod(GRID) * (2 if both else 1))
        views.append(part.reshape(GRID + ((2,) if both else ()) + (rows, part.shape[1])))
    slots = []
    for which, _, wide, order in chunks:
        rows = views[which].shape[-2]
        if shared[which]:
            slots += [pltpu.VMEM(GRID + (rows, wide), jnp.bfloat16)] * 2
        else:
            lead = tuple(GRID[dim] for dim in range(3) if dim != order[0])
            slots.append(pltpu.VMEM(lead + (rows, wide), jnp.bfloat16))
        for phase in range(3):
            lead = tuple(GRID[dim] for dim in range(3) if dim not in order[: phase + 1])
            slots.append(
                pltpu.VMEM((GRID[order[phase]] - 1,) + lead + (rows, wide), jnp.bfloat16)
            )
    outs = pl.pallas_call(
        functools.partial(kernel, chunks, events, shared),
        out_shape=[jax.ShapeDtypeStruct(view.shape[-2:], jnp.float32) for view in views] + made,
        in_specs=[pl.BlockSpec(memory_space=pl.ANY)] * count
        + [pl.BlockSpec(memory_space=pltpu.VMEM)] * len(more),
        out_specs=[pl.BlockSpec(memory_space=pltpu.VMEM)] * (count + len(made)),
        scratch_shapes=[
            pltpu.SemaphoreType.DMA((len(chunks), 6)),
            pltpu.SemaphoreType.DMA((len(chunks), 6)),
            pltpu.SemaphoreType.DMA((len(chunks),)),
        ]
        + scratch
        + slots,
        compiler_params=pltpu.CompilerParams(
            collective_id=collective_id, has_side_effects=True, vmem_limit_bytes=62 * 1024 * 1024
        ),
    )(*views, *more)
    return (outs[:count], outs[count:])


def scatter_parts(parts, shared, plan, collective_id):
    if not by_grid():
        return [
            lax.psum_scatter(
                part.astype(jnp.float32),
                ("row", "col") if both else "row",
                scatter_dimension=0,
                tiled=True,
            )
            for part, both in zip(parts, shared)
        ]
    return scatter_call(scatter_kernel, parts, shared, plan, collective_id, [], [], [])[0]


def sibling(value):
    return lax.ppermute(value, "col", [(0, 1), (1, 0)])


def gather_col(value):
    if lax.axis_size("col") != 2:
        return lax.all_gather(value, "col", axis=0, tiled=True)
    core = lax.axis_index("col")
    rows = value.shape[0]
    whole = jnp.zeros((2 * rows,) + value.shape[1:], value.dtype)
    whole = lax.dynamic_update_slice_in_dim(whole, value, core * rows, 0)
    return lax.dynamic_update_slice_in_dim(whole, sibling(value), (1 - core) * rows, 0)


def scatter_col(total):
    if lax.axis_size("col") != 2:
        return lax.psum_scatter(total, "col", scatter_dimension=0, tiled=True)
    core = lax.axis_index("col")
    rows = total.shape[0] // 2
    leaving = lax.dynamic_slice_in_dim(total, (1 - core) * rows, rows, 0).astype(jnp.bfloat16)
    mine = lax.dynamic_slice_in_dim(total, core * rows, rows, 0)
    return mine + sibling(leaving).astype(jnp.float32)


def padded(value, wide):
    return jnp.pad(value, ((0, 0), (0, wide - value.shape[1])))


def norm_parts(values, gain):
    average = jnp.mean(values, axis=-1, keepdims=True)
    centred = values - average
    inv_std = lax.rsqrt(jnp.mean(centred * centred, axis=-1, keepdims=True) + EPS)
    normed = centred * inv_std
    return (normed * gain, normed, inv_std)


def norm_back(grad_in, gain, normed, inv_std):
    grad_hat = grad_in * gain
    mean_one = jnp.mean(grad_hat, axis=-1, keepdims=True)
    mean_two = jnp.mean(grad_hat * normed, axis=-1, keepdims=True)
    return inv_std * (grad_hat - mean_one - normed * mean_two)


def rope_tables(positions, width):
    half_width = width // 2
    freq = jnp.exp(jnp.arange(half_width).astype(jnp.float32) * (-2.0 * math.log(10000.0) / width))
    angle = positions.astype(jnp.float32)[:, None] * freq[None, :]
    return (jnp.cos(angle), jnp.sin(angle))


def rotate(values, cosine, sines):
    half_width = values.shape[-1] // 2
    front_half = values[..., :half_width]
    back_half = values[..., half_width:]
    cos_part = cosine[:, None, :]
    sin_part = sines[:, None, :]
    return jnp.concatenate(
        [
            front_half * cos_part - back_half * sin_part,
            back_half * cos_part + front_half * sin_part,
        ],
        axis=-1,
    )


def unrotate(values, cosine, sines):
    half_width = values.shape[-1] // 2
    front_half = values[..., :half_width]
    back_half = values[..., half_width:]
    cos_part = cosine[:, None, :]
    sin_part = sines[:, None, :]
    return jnp.concatenate(
        [
            front_half * cos_part + back_half * sin_part,
            back_half * cos_part - front_half * sin_part,
        ],
        axis=-1,
    )


EXPERT_BLOCK = 512
ROW_BLOCK = 128


def gate_column(table, lane):
    lanes = lax.broadcasted_iota(jnp.int32, table.shape, 1)
    return jnp.sum(jnp.where(lanes == lane, table, 0.0), axis=1, keepdims=True)


def halves(core, rows):
    return (
        pl.ds(pl.multiple_of(core * rows, rows), rows),
        pl.ds(pl.multiple_of((1 - core) * rows, rows), rows),
    )


def hat_of(values):
    average = jnp.mean(values, axis=-1, keepdims=True)
    centred = values - average
    inv_std = lax.rsqrt(jnp.mean(centred * centred, axis=-1, keepdims=True) + EPS)
    return (centred * inv_std, inv_std)


def expert_kernel(
    own, other, gain, member, router, up, down, active, gated, normed, gates, mine, leaving, rows_in, total
):
    step, core = (pl.program_id(0), lax.axis_index("col"))
    here, there = halves(core, own.shape[0])
    hidden = 128

    @pl.when(step == 0)
    def _():
        rows_in[here] = own[...]
        rows_in[there] = other[...]

        def norm_block(block, carry):
            at = pl.ds(pl.multiple_of(block * ROW_BLOCK, ROW_BLOCK), ROW_BLOCK)
            hat, _ = hat_of(rows_in[at].astype(jnp.float32))
            normed[at] = (hat * gain[...]).astype(normed.dtype)
            return carry

        lax.fori_loop(0, rows_in.shape[0] // ROW_BLOCK, norm_block, 0)
        gates[...] = jax.nn.sigmoid(
            jnp.dot(normed[...], router[...], preferred_element_type=jnp.float32)
        )

    inner = jnp.dot(rows_in[...], up[...], preferred_element_type=jnp.float32)
    active[...] = jnp.maximum(inner, 0.0).astype(active.dtype)
    used = gates[...] * member[...]
    count = EXPERT_BLOCK // hidden
    for one in range(count):
        at = slice(one * hidden, (one + 1) * hidden)
        gate = gate_column(used, step * count + one)
        gated[:, at] = (active[:, at].astype(jnp.float32) * gate).astype(gated.dtype)
    part = contract_last(gated[...], down[...])

    @pl.when(step == 0)
    def _():
        total[...] = part

    @pl.when(step > 0)
    def _():
        total[...] += part

    @pl.when(step == pl.num_programs(0) - 1)
    def _():
        mine[...] = total[here]
        leaving[...] = total[there].astype(leaving.dtype)


def expert_back_kernel(
    own,
    other,
    grad_own,
    grad_other,
    gain,
    member,
    router,
    gates,
    normed,
    active,
    gated,
    up,
    down,
    down_grad,
    up_grad,
    router_grad,
    gain_grad,
    mine,
    leaving,
    rows_turned,
    grads,
    grads_turned,
    gate_grads,
    logits,
    total,
):
    step, core = (pl.program_id(0), lax.axis_index("col"))
    here, there = halves(core, own.shape[0])
    hidden = 128

    @pl.when(step == 0)
    def _():
        rows_turned[:, here] = own[...].T
        rows_turned[:, there] = other[...].T
        grads[here] = grad_own[...]
        grads[there] = grad_other[...]
        grads_turned[:, here] = grad_own[...].T
        grads_turned[:, there] = grad_other[...].T
        gate_grads[...] = jnp.zeros_like(gate_grads)

    grad_hidden = jnp.dot(grads[...], down[...], preferred_element_type=jnp.float32)
    used = gates[...] * member[...]
    lanes = lax.broadcasted_iota(jnp.int32, gate_grads.shape, 1)
    count = EXPERT_BLOCK // hidden
    pieces = []
    for one in range(count):
        at = slice(one * hidden, (one + 1) * hidden)
        lane = step * count + one
        act = active[:, at].astype(jnp.float32)
        piece = grad_hidden[:, at]
        column = jnp.sum(act * piece, axis=1, keepdims=True)
        gate_grads[...] = jnp.where(lanes == lane, column, gate_grads[...])
        pieces.append(jnp.where(act > 0, piece * gate_column(used, lane), 0.0).astype(jnp.bfloat16))
    grad_inner = jnp.concatenate(pieces, axis=1)
    down_grad[...] = jnp.dot(
        grads_turned[...], gated[...], preferred_element_type=jnp.float32
    ).astype(down_grad.dtype)
    up_grad[...] = jnp.dot(
        rows_turned[...], grad_inner, preferred_element_type=jnp.float32
    ).astype(up_grad.dtype)
    part = contract_last(grad_inner, up[...])

    @pl.when(step == 0)
    def _():
        total[...] = part

    @pl.when(step > 0)
    def _():
        total[...] += part

    @pl.when(step == pl.num_programs(0) - 1)
    def _():
        logits[...] = (gate_grads[...] * used * (1.0 - gates[...])).astype(logits.dtype)
        router_grad[...] = contract_first(normed[...], logits[...]).astype(router_grad.dtype)
        gain_grad[...] = jnp.zeros_like(gain_grad)

        def back_block(source, first):
            def body(block, carry):
                at = pl.ds(pl.multiple_of(block * ROW_BLOCK, ROW_BLOCK), ROW_BLOCK)
                whole = pl.ds(pl.multiple_of(first + block * ROW_BLOCK, ROW_BLOCK), ROW_BLOCK)
                hat, inv_std = hat_of(source[at].astype(jnp.float32))
                grad_norm = contract_last(logits[whole], router[...])
                gain_grad[...] += jnp.sum(grad_norm * hat, axis=0, keepdims=True)
                total[whole] += norm_back(grad_norm, gain[...], hat, inv_std)
                return carry

            lax.fori_loop(0, source.shape[0] // ROW_BLOCK, body, 0)

        back_block(own, core * own.shape[0])
        back_block(other, (1 - core) * own.shape[0])
        mine[...] = total[here]
        leaving[...] = total[there].astype(leaving.dtype)


def still(shape):
    return pl.BlockSpec(shape, lambda step: (0,) * len(shape))


def expert_calls(own, gain, member, up_wide, down_turned):
    rows, width = own.shape
    hidden = down_turned.shape[1]
    steps = hidden // EXPERT_BLOCK
    low, full = (jnp.bfloat16, jnp.float32)
    other = sibling(own)
    block = pl.BlockSpec((width, EXPERT_BLOCK), lambda step: (0, step))
    pairs = pl.BlockSpec((2 * rows, EXPERT_BLOCK), lambda step: (0, step))
    router = pl.BlockSpec((width, 128), lambda step: (0, hidden // 128))
    params = pltpu.CompilerParams(vmem_limit_bytes=60 * 1024 * 1024)
    active, gated, normed, gates, mine, leaving = pl.pallas_call(
        expert_kernel,
        grid=(steps,),
        out_shape=[
            jax.ShapeDtypeStruct((2 * rows, hidden), low),
            jax.ShapeDtypeStruct((2 * rows, hidden), low),
            jax.ShapeDtypeStruct((2 * rows, width), low),
            jax.ShapeDtypeStruct((2 * rows, 128), full),
            jax.ShapeDtypeStruct((rows, width), full),
            jax.ShapeDtypeStruct((rows, width), low),
        ],
        in_specs=[
            still((rows, width)),
            still((rows, width)),
            still((1, width)),
            still((2 * rows, 128)),
            router,
            block,
            block,
        ],
        out_specs=[
            pairs,
            pairs,
            still((2 * rows, width)),
            still((2 * rows, 128)),
            still((rows, width)),
            still((rows, width)),
        ],
        scratch_shapes=[pltpu.VMEM((2 * rows, width), low), pltpu.VMEM((2 * rows, width), full)],
        compiler_params=params,
    )(own, other, gain, member, up_wide, up_wide, down_turned)
    expert_sum = mine + sibling(leaving).astype(full)

    def back(grad_own):
        down_grad, up_grad, router_grad, gain_grad, mine, leaving = pl.pallas_call(
            expert_back_kernel,
            grid=(steps,),
            out_shape=[
                jax.ShapeDtypeStruct((width, hidden), low),
                jax.ShapeDtypeStruct((width, hidden), low),
                jax.ShapeDtypeStruct((width, 128), low),
                jax.ShapeDtypeStruct((1, width), full),
                jax.ShapeDtypeStruct((rows, width), full),
                jax.ShapeDtypeStruct((rows, width), low),
            ],
            in_specs=[still((rows, width))] * 4
            + [
                still((1, width)),
                still((2 * rows, 128)),
                router,
                still((2 * rows, 128)),
                still((2 * rows, width)),
                pairs,
                pairs,
                block,
                block,
            ],
            out_specs=[
                block,
                block,
                still((width, 128)),
                still((1, width)),
                still((rows, width)),
                still((rows, width)),
            ],
            scratch_shapes=[
                pltpu.VMEM((width, 2 * rows), low),
                pltpu.VMEM((2 * rows, width), low),
                pltpu.VMEM((width, 2 * rows), low),
                pltpu.VMEM((2 * rows, 128), full),
                pltpu.VMEM((2 * rows, 128), low),
                pltpu.VMEM((2 * rows, width), full),
            ],
            compiler_params=params,
        )(
            own,
            other,
            grad_own,
            sibling(grad_own),
            gain,
            member,
            up_wide,
            gates,
            normed,
            active,
            gated,
            up_wide,
            down_turned,
        )
        moe_grad = mine + sibling(leaving).astype(full)
        return (down_grad, up_grad, router_grad, gain_grad[0], moe_grad)

    return (expert_sum, back)


def shards(
    block_input,
    teacher,
    lengths,
    head_routes,
    expert_routes,
    first_gain,
    query_weight,
    key_weight,
    value_weight,
    head_router,
    output_weight,
    second_gain,
    expert_router,
    expert_up,
    expert_down,
):
    tok_rows = block_input.shape[0]
    width = block_input.shape[1]
    col_count = lax.axis_size("col")
    col_index = lax.axis_index("col")
    total_rows = tok_rows * lax.axis_size("row") * col_count
    group_size = tok_rows * col_count
    seq_length = min(MAXLEN, group_size)
    key_span = seq_length // tok_rows
    gated = H * AEXP
    local_experts = expert_up.shape[0]
    hidden_local = expert_up.shape[2]
    hidden = local_experts * hidden_local
    length_sum = jnp.sum(lengths)
    small_parts = [
        query_weight,
        key_weight,
        head_router,
        first_gain[:, None],
        second_gain[:, None],
    ]
    for digits in (length_sum // 64, length_sum % 64):
        small_parts.append(
            jnp.broadcast_to(digits.astype(jnp.bfloat16)[None, None], (first_gain.shape[0], 1))
        )
    lead_local = padded(jnp.concatenate(small_parts, axis=1), 2 * H * DH + 128)
    up_local = jnp.concatenate(
        [
            jnp.transpose(expert_up, (1, 0, 2)).reshape(-1, hidden),
            padded(expert_router, 128),
        ],
        axis=1,
    )
    down_local = jnp.transpose(expert_down, (2, 0, 1)).reshape(-1, hidden)
    lead_full, value_full = gather_parts(
        [lead_local, value_weight], [True, True], LEAD_GATHER, 1
    )
    rest_local = [output_weight.T, up_local, down_local]
    rest_shared = [True, False, False]
    paired = by_grid() and key_span == 2 and lengths.shape[0] == 1
    extra_at = 2 * H * DH + 2 * gated
    extra = lead_full[:, extra_at : extra_at + 4].astype(jnp.float32)
    gain_one = extra[:, 0]
    gain_two = extra[:, 1]
    stride = first_gain.shape[0] * col_count
    token_count = jnp.sum(extra[::stride, 2]) * 64.0 + jnp.sum(extra[::stride, 3])
    local_ids = jnp.arange(tok_rows, dtype=jnp.int32)
    group_ids = col_index * tok_rows + local_ids
    seq_pos = group_ids % seq_length
    seq_ids = group_ids // seq_length
    seq_slots = jnp.arange(lengths.shape[0], dtype=jnp.int32)
    tok_length = jnp.sum(
        jnp.where(seq_ids[:, None] == seq_slots[None, :], lengths[None, :], 0), axis=1
    )
    valid = (seq_pos < tok_length).astype(jnp.float32)
    inputs_full = block_input.astype(jnp.float32)
    normed_one, hat_one, inv_one = norm_parts(inputs_full, gain_one)
    normed_low = normed_one.astype(jnp.bfloat16)
    lead_raw = jnp.dot(normed_low, lead_full, preferred_element_type=jnp.float32)
    cosine, sines = rope_tables(seq_pos, DH)
    chosen = jnp.any(
        head_routes[:, :, :, None] == jnp.arange(AEXP, dtype=jnp.int32)[None, None, None, :], axis=2
    ).astype(jnp.float32)
    value_flat = jnp.dot(block_input, value_full, preferred_element_type=jnp.float32)
    if paired:
        sigs = jax.nn.sigmoid(lead_raw[:, 2 * H * DH :])
        picked = chosen.reshape(tok_rows, gated)
        both_gates = sigs * padded(jnp.concatenate([picked, picked], axis=1), 128)
        cos_wide = jnp.concatenate([cosine, cosine], axis=1)
        sin_wide = jnp.concatenate([-sines, sines], axis=1)
        limits = jnp.broadcast_to(lengths[:, None], (8, 128))
        low, full = (jnp.bfloat16, jnp.float32)
        made = [jax.ShapeDtypeStruct((tok_rows, H * DH), kind) for kind in [low] * 5 + [full] * 2]
        made.append(jax.ShapeDtypeStruct((tok_rows, gated * DH), low))
        (output_turned, up_wide, down_turned), kept = gather_call(
            attend_kernel,
            rest_local,
            rest_shared,
            REST_GATHER,
            2,
            [lead_raw, value_flat, both_gates, cos_wide, sin_wide, limits],
            made,
            [pltpu.SemaphoreType.DMA((2,))] * 2,
        )
        mixed_low = kept[7]
    else:
        output_turned, up_wide, down_turned = gather_parts(
            rest_local, rest_shared, REST_GATHER, 2
        )
        query_raw = lead_raw[:, : H * DH]
        key_raw = lead_raw[:, H * DH : 2 * H * DH]
        route_logits = lead_raw[:, 2 * H * DH : extra_at]
        query_scale = DH ** (-0.5)
        query_rot = (rotate(query_raw.reshape(tok_rows, H, DH), cosine, sines) * query_scale).astype(
            jnp.bfloat16
        )
        key_rot = rotate(key_raw.reshape(tok_rows, H, DH), cosine, sines).astype(jnp.bfloat16)
        value_sig = jax.nn.sigmoid(route_logits[:, :gated]).reshape(tok_rows, H, AEXP)
        output_sig = jax.nn.sigmoid(route_logits[:, gated:]).reshape(tok_rows, H, AEXP)
        value_gates = value_sig * chosen
        output_gates = output_sig * chosen
        value_all = value_flat.reshape(tok_rows, H, AEXP, DH)
        values_low = jnp.sum(value_all * value_gates[..., None], axis=2).astype(jnp.bfloat16)
        key_parts = [key_rot]
        value_parts = [values_low]
        id_parts = [group_ids]
        for offset in range(1, key_span):
            came_keys, came_values = shifted((key_rot, values_low), "col", offset)
            key_parts.append(came_keys)
            value_parts.append(came_values)
            id_parts.append(group_ids - offset * tok_rows)
        keys_all = jnp.concatenate(key_parts, axis=0)
        values_all = jnp.concatenate(value_parts, axis=0)
        key_ids = jnp.concatenate(id_parts, axis=0)
        allowed = (
            (key_ids[None, :] // seq_length == seq_ids[:, None])
            & (key_ids[None, :] <= group_ids[:, None])
            & (key_ids[None, :] % seq_length < tok_length[:, None])
        )

        def head_scores(head_idx):
            raw_scores = jnp.einsum(
                "qd,kd->qk",
                query_rot[:, head_idx],
                keys_all[:, head_idx],
                preferred_element_type=jnp.float32,
            )
            return jnp.where(allowed, raw_scores, MASKED)

        attended_list = []
        lse_list = []
        for head_idx in range(H):
            scores = head_scores(head_idx)
            row_top = jnp.max(scores, axis=1, keepdims=True)
            exponent = jnp.exp(scores - row_top)
            row_total = jnp.sum(exponent, axis=1, keepdims=True)
            probs_low = (exponent / row_total).astype(jnp.bfloat16)
            attended_list.append(
                jnp.dot(probs_low, values_all[:, head_idx], preferred_element_type=jnp.float32)
            )
            lse_list.append(row_top + jnp.log(row_total))
        attended = jnp.stack(attended_list, axis=1)
        mixed_low = (
            (attended[:, :, None, :] * output_gates[..., None])
            .astype(jnp.bfloat16)
            .reshape(tok_rows, gated * DH)
        )
    up_full = up_wide[:, :hidden]
    router_cols = up_wide[:, hidden : hidden + local_experts]
    resid = inputs_full + contract_last(mixed_low, output_turned)
    resid_low = resid.astype(jnp.bfloat16)
    expert_ids = col_index * local_experts + jnp.arange(local_experts, dtype=jnp.int32)
    member = jnp.any(expert_routes[:, :, None] == expert_ids[None, None, :], axis=1)
    if paired:
        expert_sum, expert_back = expert_calls(
            resid_low,
            gain_two[None, :],
            padded(member.astype(jnp.float32), 128),
            up_wide,
            down_turned,
        )
    else:
        group_in = gather_col(resid_low)
        normed_two, hat_two, inv_two = norm_parts(group_in.astype(jnp.float32), gain_two)
        normed_two_low = normed_two.astype(jnp.bfloat16)
        gates = jax.nn.sigmoid(jnp.dot(normed_two_low, router_cols, preferred_element_type=jnp.float32))
        used_gates = gates * member.astype(jnp.float32)

        def spread(columns):
            return jnp.repeat(columns, hidden_local, axis=1)

        inner = jnp.dot(group_in, up_full, preferred_element_type=jnp.float32)
        active = jnp.maximum(inner, 0.0).astype(jnp.bfloat16)
        gated_active = (active.astype(jnp.float32) * spread(used_gates)).astype(jnp.bfloat16)
        expert_sum = scatter_col(contract_last(gated_active, down_turned))
    output_full_rows = resid + expert_sum
    block_output = output_full_rows.astype(jnp.bfloat16)
    ratio = total_rows / token_count
    grad_output = ratio * (output_full_rows - teacher.astype(jnp.float32)) * valid[:, None]
    grad_output_low = grad_output.astype(jnp.bfloat16)
    if paired:
        down_grad, up_grad, router_grad, second_gain_part, moe_grad = expert_back(grad_output_low)
    else:
        group_grad = gather_col(grad_output_low)
        grad_hidden = jnp.dot(group_grad, down_turned, preferred_element_type=jnp.float32)
        gate_grad = jnp.sum(
            (active.astype(jnp.float32) * grad_hidden).reshape(group_size, local_experts, hidden_local),
            axis=2,
        )
        grad_inner = jnp.where(active > 0, grad_hidden * spread(used_gates), 0.0).astype(jnp.bfloat16)
        down_grad = contract_first(group_grad, gated_active).astype(jnp.bfloat16)
        up_grad = contract_first(group_in, grad_inner).astype(jnp.bfloat16)
        slot_back = contract_last(grad_inner, up_full)
        logit_low = (gate_grad * used_gates * (1.0 - gates)).astype(jnp.bfloat16)
        router_grad = contract_first(normed_two_low, padded(logit_low, 128)).astype(jnp.bfloat16)
        grad_norm_two = contract_last(logit_low, router_cols)
        second_gain_part = jnp.sum(grad_norm_two * hat_two, axis=0)
        grad_rows = slot_back + norm_back(grad_norm_two, gain_two, hat_two, inv_two)
        moe_grad = scatter_col(grad_rows)
    grad_resid = grad_output + moe_grad
    grad_branch = grad_resid.astype(jnp.bfloat16)
    output_grad = contract_first(grad_branch, mixed_low).astype(jnp.bfloat16)
    grad_mixed_low = jnp.dot(
        grad_branch, output_turned, preferred_element_type=jnp.float32
    ).astype(jnp.bfloat16)
    rest_grads = [output_grad, up_grad, router_grad, down_grad]
    rest_shared = [True, False, False, False]
    if paired:
        wide = (tok_rows, H * DH)
        sums, (lead_back, grad_value_all) = scatter_call(
            attend_back_kernel,
            rest_grads,
            rest_shared,
            REST_SCATTER,
            3,
            list(kept[:7])
            + [grad_mixed_low, value_flat, both_gates, sigs, cos_wide, sin_wide, limits],
            [
                jax.ShapeDtypeStruct((tok_rows, 2 * H * DH + 128), low),
                jax.ShapeDtypeStruct((tok_rows, gated * DH), low),
            ],
            [pltpu.SemaphoreType.DMA((2,))] * 2
            + [pltpu.VMEM(wide, full)] * 2
            + [pltpu.VMEM((tok_rows, 128), full)]
            + [pltpu.VMEM(wide, low)] * 4,
        )
    else:
        sums = scatter_parts(rest_grads, rest_shared, REST_SCATTER, 3)
        grad_mixed = grad_mixed_low.astype(jnp.float32).reshape(tok_rows, H, AEXP, DH)
        grad_attended = jnp.sum(grad_mixed * output_gates[..., None], axis=2).astype(jnp.bfloat16)
        grad_output_gates = jnp.sum(grad_mixed * attended[:, :, None, :], axis=3)
        query_grads = []
        key_grads = []
        value_grads = []
        for head_idx in range(H):
            scores = head_scores(head_idx)
            probs_full = jnp.exp(scores - lse_list[head_idx])
            probs_low = probs_full.astype(jnp.bfloat16)
            grad_probs = jnp.einsum(
                "qd,kd->qk",
                grad_attended[:, head_idx],
                values_all[:, head_idx],
                preferred_element_type=jnp.float32,
            )
            grad_scores = (
                probs_full * (grad_probs - jnp.sum(probs_full * grad_probs, axis=1, keepdims=True))
            ).astype(jnp.bfloat16)
            query_grads.append(
                jnp.dot(grad_scores, keys_all[:, head_idx], preferred_element_type=jnp.float32)
            )
            key_grads.append(contract_first(grad_scores, query_rot[:, head_idx]))
            value_grads.append(contract_first(probs_low, grad_attended[:, head_idx]))
        grad_queries = jnp.stack(query_grads, axis=1)
        key_grads_all = jnp.stack(key_grads, axis=1)
        value_grads_all = jnp.stack(value_grads, axis=1)
        grad_key_rot = key_grads_all[:tok_rows]
        grad_values = value_grads_all[:tok_rows]
        for offset in range(1, key_span):
            back_keys, back_values = (
                shifted(
                    key_grads_all[offset * tok_rows : (offset + 1) * tok_rows].astype(jnp.bfloat16),
                    "col",
                    -offset,
                ).astype(jnp.float32),
                shifted(
                    value_grads_all[offset * tok_rows : (offset + 1) * tok_rows].astype(jnp.bfloat16),
                    "col",
                    -offset,
                ).astype(jnp.float32),
            )
            grad_key_rot = grad_key_rot + back_keys
            grad_values = grad_values + back_values
        grad_value_all = (
            (grad_values[:, :, None, :] * value_gates[..., None])
            .astype(jnp.bfloat16)
            .reshape(tok_rows, gated * DH)
        )
        grad_value_gates = jnp.sum(value_all * grad_values[:, :, None, :], axis=3)
        grad_query_raw = (
            unrotate(grad_queries * query_scale, cosine, sines)
            .astype(jnp.bfloat16)
            .reshape(tok_rows, H * DH)
        )
        grad_key_raw = (
            unrotate(grad_key_rot, cosine, sines).astype(jnp.bfloat16).reshape(tok_rows, H * DH)
        )
        grad_route = jnp.concatenate(
            [
                (grad_value_gates * chosen * value_sig * (1.0 - value_sig)).reshape(tok_rows, gated),
                (grad_output_gates * chosen * output_sig * (1.0 - output_sig)).reshape(tok_rows, gated),
            ],
            axis=1,
        ).astype(jnp.bfloat16)
        lead_back = padded(
            jnp.concatenate([grad_query_raw, grad_key_raw, grad_route], axis=1), 2 * H * DH + 128
        )
    output_turned_sum, up_sum, router_sum, down_sum = sums
    value_grad = contract_first(block_input, grad_value_all).astype(jnp.bfloat16)
    grad_norm_one = contract_last(lead_back, lead_full)
    first_gain_part = jnp.sum(grad_norm_one * hat_one, axis=0)
    input_grad = (
        grad_resid
        + norm_back(grad_norm_one, gain_one, hat_one, inv_one)
        + contract_last(grad_value_all, value_full)
    )
    lead_cols = jnp.arange(2 * H * DH + 128, dtype=jnp.int32)[None, :]
    lead_grad = (
        contract_first(normed_low, lead_back)
        + jnp.where(lead_cols == extra_at, first_gain_part[:, None], 0.0)
        + jnp.where(lead_cols == extra_at + 1, second_gain_part[:, None], 0.0)
    ).astype(jnp.bfloat16)
    lead_sum, value_sum = scatter_parts([lead_grad, value_grad], [True, True], LEAD_SCATTER, 4)
    output_sum = output_turned_sum.T
    router_sum = router_sum[:, :local_experts]
    up_out = jnp.transpose(up_sum.reshape(-1, local_experts, hidden_local), (1, 0, 2))
    down_out = jnp.transpose(down_sum.reshape(-1, local_experts, hidden_local), (1, 2, 0))
    query_sum = lead_sum[:, : H * DH]
    key_sum = lead_sum[:, H * DH : 2 * H * DH]
    router_head_sum = lead_sum[:, 2 * H * DH : extra_at]
    first_sum = lead_sum[:, extra_at]
    second_sum = lead_sum[:, extra_at + 1]
    return (
        block_output,
        input_grad,
        first_sum,
        query_sum,
        key_sum,
        value_sum,
        router_head_sum,
        output_sum,
        second_sum,
        router_sum,
        up_out,
        down_out,
    )


def solution(mesh):
    return jax.shard_map(
        shards,
        mesh=mesh,
        in_specs=(
            P(("row", "col"), None),
            P(("row", "col"), None),
            P("row"),
            P(("row", "col"), None, None),
            P("row", None),
            P(("row", "col")),
            P(("row", "col"), None),
            P(("row", "col"), None),
            P(("row", "col"), None),
            P(("row", "col"), None),
            P(None, ("row", "col")),
            P(("row", "col")),
            P("row", "col"),
            P("col", "row", None),
            P("col", None, "row"),
        ),
        out_specs=(
            P(("row", "col"), None),
            P(("row", "col"), None),
            P(("row", "col")),
            P(("row", "col"), None),
            P(("row", "col"), None),
            P(("row", "col"), None),
            P(("row", "col"), None),
            P(None, ("row", "col")),
            P(("row", "col")),
            P("row", "col"),
            P("col", "row", None),
            P("col", None, "row"),
        ),
        check_vma=False,
    )
```

```python
import functools
import math

import jax
import jax.numpy as jnp
from jax import lax
from jax.experimental import pallas as pl
from jax.experimental.pallas import tpu as pltpu
from jax.sharding import PartitionSpec as P

H = 4
DH = 128
AEXP = 5
MAXLEN = 2048


EPS = 1e-05
MASKED = -1e30


def shifted(value, axis, steps):
    count = lax.axis_size(axis)
    leading, last = (max(0, -steps), min(count, count - steps))
    return lax.ppermute(value, axis, [(source, source + steps) for source in range(leading, last)])


def contract_last(left, right):
    return lax.dot_general(
        left, right, (((1,), (1,)), ((), ())), preferred_element_type=jnp.float32
    )


def contract_first(left, right):
    return lax.dot_general(
        left, right, (((0,), (0,)), ((), ())), preferred_element_type=jnp.float32
    )


GRID = (4, 2, 2)
MESH = pl.DeviceIdType.MESH
LEAD_GATHER = (
    (
        (0, 0, 384, (1, 2, 0)),
        (0, 384, 384, (2, 0, 1)),
        (0, 768, 384, (0, 1, 2)),
    ),
    (
        (0, 0),
        (1, 0),
        (2, 0),
        (0, 1),
        (1, 1),
        (2, 1),
        (0, 2),
        (2, 2),
        (1, 2),
        (2, 3),
        (1, 3),
        (0, 3),
    ),
)
REST_GATHER = (
    (
        (0, 0, 1152, (0, 2, 1)),
        (1, 0, 1792, (1, 0, 2)),
        (1, 1792, 768, (0, 1, 2)),
        (3, 0, 384, (0, 2, 1)),
        (3, 384, 1152, (0, 2, 1)),
        (0, 1152, 1408, (0, 1, 2)),
        (2, 0, 512, (2, 1, 0)),
        (2, 512, 512, (0, 2, 1)),
        (2, 1024, 1152, (0, 2, 1)),
        (3, 1536, 512, (1, 0, 2)),
    ),
    (
        (0, 0),
        (1, 0),
        (6, 0),
        (9, 0),
        (6, 1),
        (2, 0),
        (0, 1),
        (3, 0),
        (2, 1),
        (4, 0),
        (0, 2),
        (3, 1),
        (2, 2),
        (5, 0),
        (3, 2),
        (4, 1),
        (0, 3),
        (2, 3),
        (7, 0),
        (0, 4),
        (5, 1),
        (8, 0),
        (7, 1),
        (4, 2),
        (5, 2),
        (1, 1),
        (8, 1),
        (5, 3),
        (7, 2),
        (5, 4),
        (9, 1),
        (1, 2),
        (8, 2),
        (6, 2),
        (9, 2),
        (1, 3),
    ),
)
REST_SCATTER = (
    (
        (0, 0, 1536, (1, 2, 0)),
        (3, 0, 1024, (1, 2, 0)),
        (0, 1536, 1024, (1, 2, 0)),
        (1, 0, 384, (0, 1, 2)),
        (3, 1024, 640, (2, 0, 1)),
        (1, 384, 1024, (1, 2, 0)),
        (1, 1408, 640, (2, 0, 1)),
        (2, 0, 128, (2, 1, 0)),
        (3, 1664, 384, (2, 0, 1)),
    ),
    (
        (1, 0),
        (3, 0),
        (4, 0),
        (6, 0),
        (4, 1),
        (5, 0),
        (7, 0),
        (8, 0),
        (6, 1),
        (1, 1),
        (0, 0),
        (8, 1),
        (5, 1),
        (1, 2),
        (2, 0),
        (5, 2),
        (0, 1),
        (3, 1),
        (7, 1),
        (4, 2),
        (0, 2),
        (2, 1),
        (6, 2),
        (8, 2),
        (3, 2),
        (7, 2),
        (2, 2),
    ),
)
LEAD_SCATTER = (
    (
        (1, 0, 640, (1, 2, 0)),
        (1, 640, 640, (2, 1, 0)),
        (0, 0, 640, (0, 1, 2)),
        (1, 1280, 768, (1, 2, 0)),
        (0, 640, 512, (2, 1, 0)),
        (1, 2048, 512, (1, 2, 0)),
    ),
    (
        (0, 0),
        (1, 0),
        (2, 0),
        (3, 0),
        (0, 1),
        (4, 0),
        (1, 1),
        (0, 2),
        (5, 0),
        (3, 1),
        (1, 2),
        (4, 1),
        (3, 2),
        (2, 1),
        (5, 1),
        (4, 2),
        (2, 2),
        (5, 2),
    ),
)


def by_grid():
    return lax.axis_size("row") == math.prod(GRID) and lax.axis_size("col") == 2


def places():
    row = lax.axis_index("row")
    return (row // 4, (row // 2) % 2, row % 2)


def row_of(place):
    return (place[0] * 2 + place[1]) * 2 + place[2]


def moved(place, dim, steps):
    there = list(place)
    there[dim] = lax.rem(place[dim] + steps, GRID[dim])
    return row_of(there)


def greet(place, core):
    barrier = pltpu.get_barrier_semaphore()
    partners = [(moved(place, dim, k), core) for dim in range(3) for k in range(1, GRID[dim])]
    partners.append((row_of(place), 1 - core))
    for row, col in partners:
        pl.semaphore_signal(barrier, inc=1, device_id={"row": row, "col": col}, device_id_type=MESH)
    pl.semaphore_wait(barrier, len(partners))


def push(source, target, send, recv, row, core):
    copy = pltpu.make_async_remote_copy(
        source, target, send, recv, device_id={"row": row, "col": core}, device_id_type=MESH
    )
    copy.start()
    return copy


def head_cols(head):
    return slice(head * DH, (head + 1) * DH)


def half_turned(values, cosine, sines):
    return values * cosine + pltpu.roll(values, DH // 2, 1) * sines


def masked_pair(queries, keys, others, limits, core):
    rows = queries.shape[0]
    query_at = core * rows + lax.broadcasted_iota(jnp.int32, (rows, rows), 0)
    key_at = lax.broadcasted_iota(jnp.int32, (rows, rows), 1)
    scores = []
    for block, start in ((keys, core * rows), (others, (1 - core) * rows)):
        place = start + key_at
        allowed = (place <= query_at) & (place < limits)
        scores.append(jnp.where(allowed, contract_last(queries, block), MASKED))
    return scores


def gather_run(chunks, events, shared, ins, outs, send, recv, local, place, core, tasks, ready=None):
    owns = []
    for n in range(len(shared)):
        at = tuple(place) + ((core,) if shared[n] else ())
        owns.append(pltpu.make_async_copy(ins[n], outs[n].at[at], local.at[n]))
        owns[-1].start()
    sent, flying, left = ([], {}, list(tasks))
    waited, due = (False, sum(1 for _, phase in events if phase == 4))
    for step, (i, phase) in enumerate(events):
        if left and ready is not None and due == 0:
            left.pop(0)()
        which, start, wide, order = chunks[i]
        if phase == 4:
            for copy in flying.pop(i):
                copy.wait_recv()
            due -= 1
            if due == 0:
                ready()
            continue
        if phase == 1 and not waited:
            for copy in owns:
                copy.wait()
            waited = True
        for copy in flying.pop(i, []):
            copy.wait_recv()
        held = order[:phase]
        at = [slice(None) if dim in held else place[dim] for dim in range(3)]
        at += [core] if shared[which] else []
        block = outs[which].at[tuple(at) + (slice(None), pl.ds(start, wide))]
        if phase == 3:
            flying[i] = [push(block, block, send.at[i, 5], recv.at[i, 5], row_of(place), 1 - core)]
        else:
            dim = order[phase]
            source = ins[which].at[:, pl.ds(start, wide)] if phase == 0 else block
            slot = (0, 3, 4)[dim]
            flying[i] = [
                push(
                    source,
                    block,
                    send.at[i, slot + k - 1],
                    recv.at[i, slot + k - 1],
                    moved(place, dim, k),
                    core,
                )
                for k in range(1, GRID[dim])
            ]
        sent += flying[i]
    for task in left:
        task()
    for copies in flying.values():
        for copy in copies:
            copy.wait_recv()
    for copy in sent:
        copy.wait_send()


def gather_kernel(chunks, events, shared, *refs):
    count = len(shared)
    place, core = (places(), lax.axis_index("col"))
    greet(place, core)
    gather_run(
        chunks, events, shared, refs[:count], refs[count : 2 * count], *refs[2 * count :], place, core, ()
    )


def attend_kernel(chunks, events, shared, *refs):
    count = len(shared)
    ins, refs = (refs[:count], refs[count:])
    lead, rows_in, gates, cosine, sines, limits = refs[:6]
    outs, refs = (refs[6 : 6 + count], refs[6 + count :])
    query, key, value, key_other, value_other, attended, lse, mixed, value_all = refs[:9]
    send, recv, local, side_send, side_recv, weights, weights_sem = refs[9:]
    place, core = (places(), lax.axis_index("col"))
    greet(place, core)
    side, fetch = ([], [])

    def make_keys():
        for head in range(H):
            at = head_cols(head)
            shift = slice(H * DH + head * DH, H * DH + (head + 1) * DH)
            key[:, at] = half_turned(lead[:, shift], cosine[...], sines[...]).astype(key.dtype)

    def make_values():
        for head in range(H):
            total = None
            for one in range(head * AEXP, (head + 1) * AEXP):
                term = value_all[:, head_cols(one)] * gates[:, one : one + 1]
                total = term if total is None else total + term
            value[:, head_cols(head)] = total.astype(value.dtype)

    def ready():
        fetch.append(pltpu.make_async_copy(outs[0], weights, weights_sem))
        fetch[0].start()
        make_queries()
        fetch[0].wait()

    def project(block):
        at = slice(block * 512, (block + 1) * 512)
        part = weights[:, :, :, :, :, at].reshape(-1, 512)
        value_all[:, at] = jnp.dot(rows_in[...], part, preferred_element_type=jnp.float32)

    def offer():
        row, col = (row_of(place), 1 - core)
        side.append(push(key, key_other, side_send.at[0], side_recv.at[0], row, col))
        side.append(push(value, value_other, side_send.at[1], side_recv.at[1], row, col))

    def make_queries():
        make_keys()
        for head in range(H):
            at = head_cols(head)
            turned = half_turned(lead[:, at], cosine[...], sines[...]) * DH ** (-0.5)
            query[:, at] = turned.astype(query.dtype)

    def arrive():
        for copy in side:
            copy.wait()

    def attend(head):
        at = head_cols(head)
        near, far = masked_pair(query[:, at], key[:, at], key_other[:, at], limits[0:1, 0:1], core)
        top = jnp.maximum(
            jnp.max(near, axis=1, keepdims=True), jnp.max(far, axis=1, keepdims=True)
        )
        near, far = (jnp.exp(near - top), jnp.exp(far - top))
        total = jnp.sum(near, axis=1, keepdims=True) + jnp.sum(far, axis=1, keepdims=True)
        near, far = ((near / total).astype(jnp.bfloat16), (far / total).astype(jnp.bfloat16))
        out = jnp.dot(near, value[:, at], preferred_element_type=jnp.float32) + jnp.dot(
            far, value_other[:, at], preferred_element_type=jnp.float32
        )
        attended[:, at] = out
        lse[:, at] = jnp.broadcast_to(top + jnp.log(total), out.shape)
        for one in range(head * AEXP, (head + 1) * AEXP):
            gate = gates[:, H * AEXP + one : H * AEXP + one + 1]
            mixed[:, head_cols(one)] = (out * gate).astype(mixed.dtype)

    tasks = [functools.partial(project, block) for block in range(value_all.shape[1] // 512)]
    tasks += [make_values, offer, arrive]
    tasks += [functools.partial(attend, head) for head in range(H)]
    gather_run(
        chunks, events, shared, ins, outs, send, recv, local, place, core, tasks, ready
    )


def gather_call(kernel, parts, shared, plan, collective_id, more, made, scratch):
    chunks, events = plan
    count = len(parts)
    outs = pl.pallas_call(
        functools.partial(kernel, chunks, events, shared),
        out_shape=[
            jax.ShapeDtypeStruct(GRID + ((2,) if both else ()) + part.shape, part.dtype)
            for part, both in zip(parts, shared)
        ]
        + made,
        in_specs=[pl.BlockSpec(memory_space=pltpu.VMEM)] * (count + len(more)),
        out_specs=[pl.BlockSpec(memory_space=pl.ANY)] * count
        + [pl.BlockSpec(memory_space=pltpu.VMEM)] * len(made),
        scratch_shapes=[
            pltpu.SemaphoreType.DMA((len(chunks), 6)),
            pltpu.SemaphoreType.DMA((len(chunks), 6)),
            pltpu.SemaphoreType.DMA((count,)),
        ]
        + scratch,
        compiler_params=pltpu.CompilerParams(
            collective_id=collective_id, has_side_effects=True, vmem_limit_bytes=60 * 1024 * 1024
        ),
    )(*parts, *more)
    whole = [out.reshape(-1, part.shape[1]) for out, part in zip(outs, parts)]
    return (whole, outs[count:])


def gather_parts(parts, shared, plan, collective_id):
    if not by_grid():
        return [
            lax.all_gather(part, ("row", "col") if both else "row", axis=0, tiled=True)
            for part, both in zip(parts, shared)
        ]
    return gather_call(gather_kernel, parts, shared, plan, collective_id, [], [], [])[0]


def add_blocks(target, terms, lead, rows):
    steps = rows // 16

    def body(step, carry):
        block, part = (step // steps, (step % steps) * 16)
        at = []
        for size in lead[::-1]:
            at.insert(0, block % size)
            block = block // size
        at = tuple(at) + (pl.ds(pl.multiple_of(part, 16), 16),)
        total = terms[0][at].astype(jnp.float32)
        for term in terms[1:]:
            total = total + term[at].astype(jnp.float32)
        target[at] = total.astype(target.dtype)
        return carry

    lax.fori_loop(0, math.prod(lead) * steps, body, 0)


def scatter_run(chunks, events, shared, ins, outs, send, recv, local, slots, place, core, tasks):
    slots, rest = (list(slots), list(tasks))
    held = {}
    for i in range(len(chunks)):
        held[i] = [slots.pop(0) for _ in range(5 if shared[chunks[i][0]] else 4)]
    sent, flying, owns = ([], {}, {})

    for i in dict.fromkeys(i for i, _ in events):
        which, start, wide, order = chunks[i]
        cols = pl.ds(start, wide)
        if shared[which]:
            own = ins[which].at[:, :, :, core, :, cols]
            other = ins[which].at[:, :, :, 1 - core, :, cols]
            flying[i] = [
                push(other, held[i][1], send.at[i, 5], recv.at[i, 5], row_of(place), 1 - core)
            ]
            sent += flying[i]
        else:
            at = [slice(None)] * 3
            at[order[0]] = place[order[0]]
            own = ins[which].at[tuple(at) + (slice(None), cols)]
        owns[i] = pltpu.make_async_copy(own, held[i][0], local.at[i])
        owns[i].start()

    def source_of(i, phase):
        which, start, wide, order = chunks[i]
        if phase == 0:
            return held[i][1] if shared[which] else ins[which].at[:, :, :, :, pl.ds(start, wide)]
        return held[i][-3 + phase - 1].at[0]

    def landed(i, phase):
        which, start, wide, order = chunks[i]
        rows = outs[which].shape[0]
        for copy in flying.pop(i):
            copy.wait_recv()
        if phase < 0:
            owns[i].wait()
            add_blocks(held[i][1], [held[i][0], held[i][1]], list(GRID), rows)
            return
        dim = order[phase]
        came = held[i][-3 + phase]
        if phase == 0 and not shared[which]:
            owns[i].wait()
            own = held[i][0]
        else:
            left = [d for d in range(3) if d not in order[:phase]]
            own = source_of(i, phase).at[tuple(place[dim] if d == dim else slice(None) for d in left)]
        target = outs[which].at[:, pl.ds(start, wide)] if phase == 2 else came.at[0]
        terms = [own] + [came.at[k] for k in range(GRID[dim] - 1)]
        lead = [GRID[d] for d in range(3) if d not in order[: phase + 1]]
        add_blocks(target, terms, lead, rows)

    early = sum(1 for i, phase in events if phase == 0 and not shared[chunks[i][0]])
    early = min(early, len(events) - 2 * len(rest))
    for step, (i, phase) in enumerate(events):
        if rest and step >= early and (step - early) % 2 == 0:
            rest.pop(0)()
        which, start, wide, order = chunks[i]
        if phase > 0 or shared[which]:
            landed(i, phase - 1)
        dim = order[phase]
        left = [d for d in range(3) if d not in order[:phase]]
        slot = (0, 3, 4)[dim]
        flying[i] = []
        for k in range(1, GRID[dim]):
            there = lax.rem(place[dim] + k, GRID[dim])
            at = tuple(there if d == dim else slice(None) for d in left)
            flying[i].append(
                push(
                    source_of(i, phase).at[at],
                    held[i][-3 + phase].at[k - 1],
                    send.at[i, slot + k - 1],
                    recv.at[i, slot + k - 1],
                    moved(place, dim, k),
                    core,
                )
            )
        sent += flying[i]
    for task in rest:
        task()
    for i in list(flying):
        landed(i, 2)
    for copy in sent:
        copy.wait_send()


def scatter_kernel(chunks, events, shared, *refs):
    count = len(shared)
    ins, outs = (refs[:count], refs[count : 2 * count])
    send, recv, local = refs[2 * count : 2 * count + 3]
    place, core = (places(), lax.axis_index("col"))
    greet(place, core)
    slots = refs[2 * count + 3 :]
    scatter_run(chunks, events, shared, ins, outs, send, recv, local, slots, place, core, ())


def finish_kernel(chunks, events, shared, *refs):
    count = len(shared)
    ins, refs = (refs[:count], refs[count:])
    grad_value_all, weights, base = refs[:3]
    outs, refs = (refs[3 : 3 + count], refs[3 + count :])
    input_grad, send, recv, local = refs[:4]
    place, core = (places(), lax.axis_index("col"))
    greet(place, core)

    def block(part):
        at = slice(part * 256, (part + 1) * 256)
        input_grad[:, at] = base[:, at] + contract_last(grad_value_all[...], weights[at, :])

    tasks = [functools.partial(block, part) for part in range(base.shape[1] // 256)]
    scatter_run(chunks, events, shared, ins, outs, send, recv, local, refs[4:], place, core, tasks)


def attend_back_kernel(chunks, events, shared, *refs):
    count = len(shared)
    ins, refs = (refs[:count], refs[count:])
    query, key, value, key_other, value_other, attended, lse, grad_mixed = refs[:8]
    value_all, gates, sigs, cosine, sines, limits = refs[8:14]
    outs, refs = (refs[14 : 14 + count], refs[14 + count :])
    lead_back, grad_value_all = refs[:2]
    send, recv, local, side_send, side_recv = refs[2:7]
    grad_key, grad_value, grad_gates, key_leave, value_leave, key_came, value_came = refs[7:14]
    slots = refs[14:]
    place, core = (places(), lax.axis_index("col"))
    greet(place, core)
    side = []
    gated = H * AEXP

    def put_gate(one, column):
        lanes = lax.broadcasted_iota(jnp.int32, grad_gates.shape, 1)
        grad_gates[...] = jnp.where(lanes == one, column, grad_gates[...])

    def attend_back(head):
        at = head_cols(head)
        if head == 0:
            grad_gates[...] = jnp.zeros_like(grad_gates)
        total = None
        for one in range(head * AEXP, (head + 1) * AEXP):
            gate = gates[:, gated + one : gated + one + 1]
            piece = grad_mixed[:, head_cols(one)].astype(jnp.float32)
            put_gate(gated + one, jnp.sum(piece * attended[:, at], axis=1, keepdims=True))
            total = piece * gate if total is None else total + piece * gate
        grad_out = total.astype(jnp.bfloat16)
        queries, keys, others = (query[:, at], key[:, at], key_other[:, at])
        near, far = masked_pair(queries, keys, others, limits[0:1, 0:1], core)
        level = lse[:, head * DH : head * DH + 1]
        near, far = (jnp.exp(near - level), jnp.exp(far - level))
        near_grad = contract_last(grad_out, value[:, at])
        far_grad = contract_last(grad_out, value_other[:, at])
        mean = jnp.sum(near * near_grad, axis=1, keepdims=True) + jnp.sum(
            far * far_grad, axis=1, keepdims=True
        )
        near_grad = (near * (near_grad - mean)).astype(jnp.bfloat16)
        far_grad = (far * (far_grad - mean)).astype(jnp.bfloat16)
        near, far = (near.astype(jnp.bfloat16), far.astype(jnp.bfloat16))
        grad_query = jnp.dot(near_grad, keys, preferred_element_type=jnp.float32) + jnp.dot(
            far_grad, others, preferred_element_type=jnp.float32
        )
        turned = half_turned(grad_query * DH ** (-0.5), cosine[...], -sines[...])
        lead_back[:, at] = turned.astype(lead_back.dtype)
        grad_key[:, at] = contract_first(near_grad, queries)
        grad_value[:, at] = contract_first(near, grad_out)
        key_leave[:, at] = contract_first(far_grad, queries).astype(key_leave.dtype)
        value_leave[:, at] = contract_first(far, grad_out).astype(value_leave.dtype)

    def leave():
        row, col = (row_of(place), 1 - core)
        side.append(push(key_leave, key_came, side_send.at[0], side_recv.at[0], row, col))
        side.append(push(value_leave, value_came, side_send.at[1], side_recv.at[1], row, col))

    def arrive():
        for copy in side:
            copy.wait()

    def finish(head):
        at = head_cols(head)
        turned = half_turned(
            grad_key[:, at] + key_came[:, at].astype(jnp.float32), cosine[...], -sines[...]
        )
        lead_back[:, H * DH + head * DH : H * DH + (head + 1) * DH] = turned.astype(lead_back.dtype)
        whole = grad_value[:, at] + value_came[:, at].astype(jnp.float32)
        for one in range(head * AEXP, (head + 1) * AEXP):
            grad_value_all[:, head_cols(one)] = (whole * gates[:, one : one + 1]).astype(
                grad_value_all.dtype
            )
            put_gate(one, jnp.sum(value_all[:, head_cols(one)] * whole, axis=1, keepdims=True))
        if head == H - 1:
            lead_back[:, 2 * H * DH :] = (
                grad_gates[...] * gates[...] * (1.0 - sigs[...])
            ).astype(lead_back.dtype)

    tasks = [functools.partial(attend_back, head) for head in range(H)]
    tasks += [leave, arrive] + [functools.partial(finish, head) for head in range(H)]
    scatter_run(chunks, events, shared, ins, outs, send, recv, local, slots, place, core, tasks)


def scatter_call(kernel, parts, shared, plan, collective_id, more, made, scratch):
    chunks, events = plan
    count = len(parts)
    views = []
    for part, both in zip(parts, shared):
        rows = part.shape[0] // (math.prod(GRID) * (2 if both else 1))
        views.append(part.reshape(GRID + ((2,) if both else ()) + (rows, part.shape[1])))
    slots = []
    for which, _, wide, order in chunks:
        rows = views[which].shape[-2]
        if shared[which]:
            slots += [pltpu.VMEM(GRID + (rows, wide), jnp.bfloat16)] * 2
        else:
            lead = tuple(GRID[dim] for dim in range(3) if dim != order[0])
            slots.append(pltpu.VMEM(lead + (rows, wide), jnp.bfloat16))
        for phase in range(3):
            lead = tuple(GRID[dim] for dim in range(3) if dim not in order[: phase + 1])
            slots.append(
                pltpu.VMEM((GRID[order[phase]] - 1,) + lead + (rows, wide), jnp.bfloat16)
            )
    outs = pl.pallas_call(
        functools.partial(kernel, chunks, events, shared),
        out_shape=[jax.ShapeDtypeStruct(view.shape[-2:], jnp.float32) for view in views] + made,
        in_specs=[pl.BlockSpec(memory_space=pl.ANY)] * count
        + [pl.BlockSpec(memory_space=pltpu.VMEM)] * len(more),
        out_specs=[pl.BlockSpec(memory_space=pltpu.VMEM)] * (count + len(made)),
        scratch_shapes=[
            pltpu.SemaphoreType.DMA((len(chunks), 6)),
            pltpu.SemaphoreType.DMA((len(chunks), 6)),
            pltpu.SemaphoreType.DMA((len(chunks),)),
        ]
        + scratch
        + slots,
        compiler_params=pltpu.CompilerParams(
            collective_id=collective_id, has_side_effects=True, vmem_limit_bytes=62 * 1024 * 1024
        ),
    )(*views, *more)
    return (outs[:count], outs[count:])


def scatter_parts(parts, shared, plan, collective_id):
    if not by_grid():
        return [
            lax.psum_scatter(
                part.astype(jnp.float32),
                ("row", "col") if both else "row",
                scatter_dimension=0,
                tiled=True,
            )
            for part, both in zip(parts, shared)
        ]
    return scatter_call(scatter_kernel, parts, shared, plan, collective_id, [], [], [])[0]


def sibling(value):
    return lax.ppermute(value, "col", [(0, 1), (1, 0)])


def gather_col(value):
    if lax.axis_size("col") != 2:
        return lax.all_gather(value, "col", axis=0, tiled=True)
    core = lax.axis_index("col")
    rows = value.shape[0]
    whole = jnp.zeros((2 * rows,) + value.shape[1:], value.dtype)
    whole = lax.dynamic_update_slice_in_dim(whole, value, core * rows, 0)
    return lax.dynamic_update_slice_in_dim(whole, sibling(value), (1 - core) * rows, 0)


def scatter_col(total):
    if lax.axis_size("col") != 2:
        return lax.psum_scatter(total, "col", scatter_dimension=0, tiled=True)
    core = lax.axis_index("col")
    rows = total.shape[0] // 2
    leaving = lax.dynamic_slice_in_dim(total, (1 - core) * rows, rows, 0).astype(jnp.bfloat16)
    mine = lax.dynamic_slice_in_dim(total, core * rows, rows, 0)
    return mine + sibling(leaving).astype(jnp.float32)


def padded(value, wide):
    return jnp.pad(value, ((0, 0), (0, wide - value.shape[1])))


def norm_parts(values, gain):
    average = jnp.mean(values, axis=-1, keepdims=True)
    centred = values - average
    inv_std = lax.rsqrt(jnp.mean(centred * centred, axis=-1, keepdims=True) + EPS)
    normed = centred * inv_std
    return (normed * gain, normed, inv_std)


def norm_back(grad_in, gain, normed, inv_std):
    grad_hat = grad_in * gain
    mean_one = jnp.mean(grad_hat, axis=-1, keepdims=True)
    mean_two = jnp.mean(grad_hat * normed, axis=-1, keepdims=True)
    return inv_std * (grad_hat - mean_one - normed * mean_two)


def rope_tables(positions, width):
    half_width = width // 2
    freq = jnp.exp(jnp.arange(half_width).astype(jnp.float32) * (-2.0 * math.log(10000.0) / width))
    angle = positions.astype(jnp.float32)[:, None] * freq[None, :]
    return (jnp.cos(angle), jnp.sin(angle))


def rotate(values, cosine, sines):
    half_width = values.shape[-1] // 2
    front_half = values[..., :half_width]
    back_half = values[..., half_width:]
    cos_part = cosine[:, None, :]
    sin_part = sines[:, None, :]
    return jnp.concatenate(
        [
            front_half * cos_part - back_half * sin_part,
            back_half * cos_part + front_half * sin_part,
        ],
        axis=-1,
    )


def unrotate(values, cosine, sines):
    half_width = values.shape[-1] // 2
    front_half = values[..., :half_width]
    back_half = values[..., half_width:]
    cos_part = cosine[:, None, :]
    sin_part = sines[:, None, :]
    return jnp.concatenate(
        [
            front_half * cos_part + back_half * sin_part,
            back_half * cos_part - front_half * sin_part,
        ],
        axis=-1,
    )


EXPERT_BLOCK = 512
ROW_BLOCK = 128


def gate_column(table, lane):
    lanes = lax.broadcasted_iota(jnp.int32, table.shape, 1)
    return jnp.sum(jnp.where(lanes == lane, table, 0.0), axis=1, keepdims=True)


def halves(core, rows):
    return (
        pl.ds(pl.multiple_of(core * rows, rows), rows),
        pl.ds(pl.multiple_of((1 - core) * rows, rows), rows),
    )


def hat_of(values):
    average = jnp.mean(values, axis=-1, keepdims=True)
    centred = values - average
    inv_std = lax.rsqrt(jnp.mean(centred * centred, axis=-1, keepdims=True) + EPS)
    return (centred * inv_std, inv_std)


def expert_kernel(
    own, other, gain, member, router, up, down, active, gated, normed, gates, mine, leaving, rows_in, total
):
    step, core = (pl.program_id(0), lax.axis_index("col"))
    here, there = halves(core, own.shape[0])
    hidden = 128

    @pl.when(step == 0)
    def _():
        rows_in[here] = own[...]
        rows_in[there] = other[...]

        def norm_block(block, carry):
            at = pl.ds(pl.multiple_of(block * ROW_BLOCK, ROW_BLOCK), ROW_BLOCK)
            hat, _ = hat_of(rows_in[at].astype(jnp.float32))
            normed[at] = (hat * gain[...]).astype(normed.dtype)
            return carry

        lax.fori_loop(0, rows_in.shape[0] // ROW_BLOCK, norm_block, 0)
        gates[...] = jax.nn.sigmoid(
            jnp.dot(normed[...], router[...], preferred_element_type=jnp.float32)
        )

    inner = jnp.dot(rows_in[...], up[...], preferred_element_type=jnp.float32)
    active[...] = jnp.maximum(inner, 0.0).astype(active.dtype)
    used = gates[...] * member[...]
    count = EXPERT_BLOCK // hidden
    for one in range(count):
        at = slice(one * hidden, (one + 1) * hidden)
        gate = gate_column(used, step * count + one)
        gated[:, at] = (active[:, at].astype(jnp.float32) * gate).astype(gated.dtype)
    part = contract_last(gated[...], down[...])

    @pl.when(step == 0)
    def _():
        total[...] = part

    @pl.when(step > 0)
    def _():
        total[...] += part

    @pl.when(step == pl.num_programs(0) - 1)
    def _():
        mine[...] = total[here]
        leaving[...] = total[there].astype(leaving.dtype)


def expert_back_kernel(
    own,
    other,
    grad_own,
    grad_other,
    gain,
    member,
    router,
    gates,
    normed,
    active,
    gated,
    up,
    down,
    down_grad,
    up_grad,
    router_grad,
    gain_grad,
    mine,
    leaving,
    rows_turned,
    grads,
    grads_turned,
    gate_grads,
    logits,
    total,
):
    step, core = (pl.program_id(0), lax.axis_index("col"))
    here, there = halves(core, own.shape[0])
    hidden = 128

    @pl.when(step == 0)
    def _():
        rows_turned[:, here] = own[...].T
        rows_turned[:, there] = other[...].T
        grads[here] = grad_own[...]
        grads[there] = grad_other[...]
        grads_turned[:, here] = grad_own[...].T
        grads_turned[:, there] = grad_other[...].T
        gate_grads[...] = jnp.zeros_like(gate_grads)

    grad_hidden = jnp.dot(grads[...], down[...], preferred_element_type=jnp.float32)
    used = gates[...] * member[...]
    lanes = lax.broadcasted_iota(jnp.int32, gate_grads.shape, 1)
    count = EXPERT_BLOCK // hidden
    pieces = []
    for one in range(count):
        at = slice(one * hidden, (one + 1) * hidden)
        lane = step * count + one
        act = active[:, at].astype(jnp.float32)
        piece = grad_hidden[:, at]
        column = jnp.sum(act * piece, axis=1, keepdims=True)
        gate_grads[...] = jnp.where(lanes == lane, column, gate_grads[...])
        pieces.append(jnp.where(act > 0, piece * gate_column(used, lane), 0.0).astype(jnp.bfloat16))
    grad_inner = jnp.concatenate(pieces, axis=1)
    down_grad[...] = jnp.dot(
        grads_turned[...], gated[...], preferred_element_type=jnp.float32
    ).astype(down_grad.dtype)
    up_grad[...] = jnp.dot(
        rows_turned[...], grad_inner, preferred_element_type=jnp.float32
    ).astype(up_grad.dtype)
    part = contract_last(grad_inner, up[...])

    @pl.when(step == 0)
    def _():
        total[...] = part

    @pl.when(step > 0)
    def _():
        total[...] += part

    @pl.when(step == pl.num_programs(0) - 1)
    def _():
        logits[...] = (gate_grads[...] * used * (1.0 - gates[...])).astype(logits.dtype)
        router_grad[...] = contract_first(normed[...], logits[...]).astype(router_grad.dtype)
        gain_grad[...] = jnp.zeros_like(gain_grad)

        def back_block(source, first):
            def body(block, carry):
                at = pl.ds(pl.multiple_of(block * ROW_BLOCK, ROW_BLOCK), ROW_BLOCK)
                whole = pl.ds(pl.multiple_of(first + block * ROW_BLOCK, ROW_BLOCK), ROW_BLOCK)
                hat, inv_std = hat_of(source[at].astype(jnp.float32))
                grad_norm = contract_last(logits[whole], router[...])
                gain_grad[...] += jnp.sum(grad_norm * hat, axis=0, keepdims=True)
                total[whole] += norm_back(grad_norm, gain[...], hat, inv_std)
                return carry

            lax.fori_loop(0, source.shape[0] // ROW_BLOCK, body, 0)

        back_block(own, core * own.shape[0])
        back_block(other, (1 - core) * own.shape[0])
        mine[...] = total[here]
        leaving[...] = total[there].astype(leaving.dtype)


def still(shape):
    return pl.BlockSpec(shape, lambda step: (0,) * len(shape))


def expert_calls(own, gain, member, up_wide, down_turned):
    rows, width = own.shape
    hidden = down_turned.shape[1]
    steps = hidden // EXPERT_BLOCK
    low, full = (jnp.bfloat16, jnp.float32)
    other = sibling(own)
    block = pl.BlockSpec((width, EXPERT_BLOCK), lambda step: (0, step))
    pairs = pl.BlockSpec((2 * rows, EXPERT_BLOCK), lambda step: (0, step))
    router = pl.BlockSpec((width, 128), lambda step: (0, hidden // 128))
    params = pltpu.CompilerParams(vmem_limit_bytes=60 * 1024 * 1024)
    active, gated, normed, gates, mine, leaving = pl.pallas_call(
        expert_kernel,
        grid=(steps,),
        out_shape=[
            jax.ShapeDtypeStruct((2 * rows, hidden), low),
            jax.ShapeDtypeStruct((2 * rows, hidden), low),
            jax.ShapeDtypeStruct((2 * rows, width), low),
            jax.ShapeDtypeStruct((2 * rows, 128), full),
            jax.ShapeDtypeStruct((rows, width), full),
            jax.ShapeDtypeStruct((rows, width), low),
        ],
        in_specs=[
            still((rows, width)),
            still((rows, width)),
            still((1, width)),
            still((2 * rows, 128)),
            router,
            block,
            block,
        ],
        out_specs=[
            pairs,
            pairs,
            still((2 * rows, width)),
            still((2 * rows, 128)),
            still((rows, width)),
            still((rows, width)),
        ],
        scratch_shapes=[pltpu.VMEM((2 * rows, width), low), pltpu.VMEM((2 * rows, width), full)],
        compiler_params=params,
    )(own, other, gain, member, up_wide, up_wide, down_turned)
    expert_sum = mine + sibling(leaving).astype(full)

    def back(grad_own):
        down_grad, up_grad, router_grad, gain_grad, mine, leaving = pl.pallas_call(
            expert_back_kernel,
            grid=(steps,),
            out_shape=[
                jax.ShapeDtypeStruct((width, hidden), low),
                jax.ShapeDtypeStruct((width, hidden), low),
                jax.ShapeDtypeStruct((width, 128), low),
                jax.ShapeDtypeStruct((1, width), full),
                jax.ShapeDtypeStruct((rows, width), full),
                jax.ShapeDtypeStruct((rows, width), low),
            ],
            in_specs=[still((rows, width))] * 4
            + [
                still((1, width)),
                still((2 * rows, 128)),
                router,
                still((2 * rows, 128)),
                still((2 * rows, width)),
                pairs,
                pairs,
                block,
                block,
            ],
            out_specs=[
                block,
                block,
                still((width, 128)),
                still((1, width)),
                still((rows, width)),
                still((rows, width)),
            ],
            scratch_shapes=[
                pltpu.VMEM((width, 2 * rows), low),
                pltpu.VMEM((2 * rows, width), low),
                pltpu.VMEM((width, 2 * rows), low),
                pltpu.VMEM((2 * rows, 128), full),
                pltpu.VMEM((2 * rows, 128), low),
                pltpu.VMEM((2 * rows, width), full),
            ],
            compiler_params=params,
        )(
            own,
            other,
            grad_own,
            sibling(grad_own),
            gain,
            member,
            up_wide,
            gates,
            normed,
            active,
            gated,
            up_wide,
            down_turned,
        )
        moe_grad = mine + sibling(leaving).astype(full)
        return (down_grad, up_grad, router_grad, gain_grad[0], moe_grad)

    return (expert_sum, back)


def shards(
    block_input,
    teacher,
    lengths,
    head_routes,
    expert_routes,
    first_gain,
    query_weight,
    key_weight,
    value_weight,
    head_router,
    output_weight,
    second_gain,
    expert_router,
    expert_up,
    expert_down,
):
    tok_rows = block_input.shape[0]
    width = block_input.shape[1]
    col_count = lax.axis_size("col")
    col_index = lax.axis_index("col")
    total_rows = tok_rows * lax.axis_size("row") * col_count
    group_size = tok_rows * col_count
    seq_length = min(MAXLEN, group_size)
    key_span = seq_length // tok_rows
    gated = H * AEXP
    local_experts = expert_up.shape[0]
    hidden_local = expert_up.shape[2]
    hidden = local_experts * hidden_local
    length_sum = jnp.sum(lengths)
    small_parts = [
        query_weight,
        key_weight,
        head_router,
        first_gain[:, None],
        second_gain[:, None],
    ]
    for digits in (length_sum // 64, length_sum % 64):
        small_parts.append(
            jnp.broadcast_to(digits.astype(jnp.bfloat16)[None, None], (first_gain.shape[0], 1))
        )
    lead_local = padded(jnp.concatenate(small_parts, axis=1), 2 * H * DH + 128)
    up_local = jnp.concatenate(
        [
            jnp.transpose(expert_up, (1, 0, 2)).reshape(-1, hidden),
            padded(expert_router, 128),
        ],
        axis=1,
    )
    down_local = jnp.transpose(expert_down, (2, 0, 1)).reshape(-1, hidden)
    lead_full = gather_parts([lead_local], [True], LEAD_GATHER, 1)[0]
    rest_local = [value_weight, output_weight.T, up_local, down_local]
    rest_shared = [True, True, False, False]
    paired = by_grid() and key_span == 2 and lengths.shape[0] == 1
    extra_at = 2 * H * DH + 2 * gated
    extra = lead_full[:, extra_at : extra_at + 4].astype(jnp.float32)
    gain_one = extra[:, 0]
    gain_two = extra[:, 1]
    stride = first_gain.shape[0] * col_count
    token_count = jnp.sum(extra[::stride, 2]) * 64.0 + jnp.sum(extra[::stride, 3])
    local_ids = jnp.arange(tok_rows, dtype=jnp.int32)
    group_ids = col_index * tok_rows + local_ids
    seq_pos = group_ids % seq_length
    seq_ids = group_ids // seq_length
    seq_slots = jnp.arange(lengths.shape[0], dtype=jnp.int32)
    tok_length = jnp.sum(
        jnp.where(seq_ids[:, None] == seq_slots[None, :], lengths[None, :], 0), axis=1
    )
    valid = (seq_pos < tok_length).astype(jnp.float32)
    inputs_full = block_input.astype(jnp.float32)
    normed_one, hat_one, inv_one = norm_parts(inputs_full, gain_one)
    normed_low = normed_one.astype(jnp.bfloat16)
    lead_raw = jnp.dot(normed_low, lead_full, preferred_element_type=jnp.float32)
    cosine, sines = rope_tables(seq_pos, DH)
    chosen = jnp.any(
        head_routes[:, :, :, None] == jnp.arange(AEXP, dtype=jnp.int32)[None, None, None, :], axis=2
    ).astype(jnp.float32)
    if paired:
        sigs = jax.nn.sigmoid(lead_raw[:, 2 * H * DH :])
        picked = chosen.reshape(tok_rows, gated)
        both_gates = sigs * padded(jnp.concatenate([picked, picked], axis=1), 128)
        cos_wide = jnp.concatenate([cosine, cosine], axis=1)
        sin_wide = jnp.concatenate([-sines, sines], axis=1)
        limits = jnp.broadcast_to(lengths[:, None], (8, 128))
        low, full = (jnp.bfloat16, jnp.float32)
        made = [jax.ShapeDtypeStruct((tok_rows, H * DH), kind) for kind in [low] * 5 + [full] * 2]
        made += [jax.ShapeDtypeStruct((tok_rows, gated * DH), kind) for kind in (low, full)]
        (value_full, output_turned, up_wide, down_turned), kept = gather_call(
            attend_kernel,
            rest_local,
            rest_shared,
            REST_GATHER,
            2,
            [lead_raw, block_input, both_gates, cos_wide, sin_wide, limits],
            made,
            [pltpu.SemaphoreType.DMA((2,))] * 2
            + [pltpu.VMEM(GRID + (2,) + value_weight.shape, low), pltpu.SemaphoreType.DMA],
        )
        mixed_low, value_flat = kept[7:]
    else:
        value_full, output_turned, up_wide, down_turned = gather_parts(
            rest_local, rest_shared, REST_GATHER, 2
        )
        value_flat = jnp.dot(block_input, value_full, preferred_element_type=jnp.float32)
        query_raw = lead_raw[:, : H * DH]
        key_raw = lead_raw[:, H * DH : 2 * H * DH]
        route_logits = lead_raw[:, 2 * H * DH : extra_at]
        query_scale = DH ** (-0.5)
        query_rot = (rotate(query_raw.reshape(tok_rows, H, DH), cosine, sines) * query_scale).astype(
            jnp.bfloat16
        )
        key_rot = rotate(key_raw.reshape(tok_rows, H, DH), cosine, sines).astype(jnp.bfloat16)
        value_sig = jax.nn.sigmoid(route_logits[:, :gated]).reshape(tok_rows, H, AEXP)
        output_sig = jax.nn.sigmoid(route_logits[:, gated:]).reshape(tok_rows, H, AEXP)
        value_gates = value_sig * chosen
        output_gates = output_sig * chosen
        value_all = value_flat.reshape(tok_rows, H, AEXP, DH)
        values_low = jnp.sum(value_all * value_gates[..., None], axis=2).astype(jnp.bfloat16)
        key_parts = [key_rot]
        value_parts = [values_low]
        id_parts = [group_ids]
        for offset in range(1, key_span):
            came_keys, came_values = shifted((key_rot, values_low), "col", offset)
            key_parts.append(came_keys)
            value_parts.append(came_values)
            id_parts.append(group_ids - offset * tok_rows)
        keys_all = jnp.concatenate(key_parts, axis=0)
        values_all = jnp.concatenate(value_parts, axis=0)
        key_ids = jnp.concatenate(id_parts, axis=0)
        allowed = (
            (key_ids[None, :] // seq_length == seq_ids[:, None])
            & (key_ids[None, :] <= group_ids[:, None])
            & (key_ids[None, :] % seq_length < tok_length[:, None])
        )

        def head_scores(head_idx):
            raw_scores = jnp.einsum(
                "qd,kd->qk",
                query_rot[:, head_idx],
                keys_all[:, head_idx],
                preferred_element_type=jnp.float32,
            )
            return jnp.where(allowed, raw_scores, MASKED)

        attended_list = []
        lse_list = []
        for head_idx in range(H):
            scores = head_scores(head_idx)
            row_top = jnp.max(scores, axis=1, keepdims=True)
            exponent = jnp.exp(scores - row_top)
            row_total = jnp.sum(exponent, axis=1, keepdims=True)
            probs_low = (exponent / row_total).astype(jnp.bfloat16)
            attended_list.append(
                jnp.dot(probs_low, values_all[:, head_idx], preferred_element_type=jnp.float32)
            )
            lse_list.append(row_top + jnp.log(row_total))
        attended = jnp.stack(attended_list, axis=1)
        mixed_low = (
            (attended[:, :, None, :] * output_gates[..., None])
            .astype(jnp.bfloat16)
            .reshape(tok_rows, gated * DH)
        )
    up_full = up_wide[:, :hidden]
    router_cols = up_wide[:, hidden : hidden + local_experts]
    resid = inputs_full + contract_last(mixed_low, output_turned)
    resid_low = resid.astype(jnp.bfloat16)
    expert_ids = col_index * local_experts + jnp.arange(local_experts, dtype=jnp.int32)
    member = jnp.any(expert_routes[:, :, None] == expert_ids[None, None, :], axis=1)
    if paired:
        expert_sum, expert_back = expert_calls(
            resid_low,
            gain_two[None, :],
            padded(member.astype(jnp.float32), 128),
            up_wide,
            down_turned,
        )
    else:
        group_in = gather_col(resid_low)
        normed_two, hat_two, inv_two = norm_parts(group_in.astype(jnp.float32), gain_two)
        normed_two_low = normed_two.astype(jnp.bfloat16)
        gates = jax.nn.sigmoid(jnp.dot(normed_two_low, router_cols, preferred_element_type=jnp.float32))
        used_gates = gates * member.astype(jnp.float32)

        def spread(columns):
            return jnp.repeat(columns, hidden_local, axis=1)

        inner = jnp.dot(group_in, up_full, preferred_element_type=jnp.float32)
        active = jnp.maximum(inner, 0.0).astype(jnp.bfloat16)
        gated_active = (active.astype(jnp.float32) * spread(used_gates)).astype(jnp.bfloat16)
        expert_sum = scatter_col(contract_last(gated_active, down_turned))
    output_full_rows = resid + expert_sum
    block_output = output_full_rows.astype(jnp.bfloat16)
    ratio = total_rows / token_count
    grad_output = ratio * (output_full_rows - teacher.astype(jnp.float32)) * valid[:, None]
    grad_output_low = grad_output.astype(jnp.bfloat16)
    if paired:
        down_grad, up_grad, router_grad, second_gain_part, moe_grad = expert_back(grad_output_low)
    else:
        group_grad = gather_col(grad_output_low)
        grad_hidden = jnp.dot(group_grad, down_turned, preferred_element_type=jnp.float32)
        gate_grad = jnp.sum(
            (active.astype(jnp.float32) * grad_hidden).reshape(group_size, local_experts, hidden_local),
            axis=2,
        )
        grad_inner = jnp.where(active > 0, grad_hidden * spread(used_gates), 0.0).astype(jnp.bfloat16)
        down_grad = contract_first(group_grad, gated_active).astype(jnp.bfloat16)
        up_grad = contract_first(group_in, grad_inner).astype(jnp.bfloat16)
        slot_back = contract_last(grad_inner, up_full)
        logit_low = (gate_grad * used_gates * (1.0 - gates)).astype(jnp.bfloat16)
        router_grad = contract_first(normed_two_low, padded(logit_low, 128)).astype(jnp.bfloat16)
        grad_norm_two = contract_last(logit_low, router_cols)
        second_gain_part = jnp.sum(grad_norm_two * hat_two, axis=0)
        grad_rows = slot_back + norm_back(grad_norm_two, gain_two, hat_two, inv_two)
        moe_grad = scatter_col(grad_rows)
    grad_resid = grad_output + moe_grad
    grad_branch = grad_resid.astype(jnp.bfloat16)
    output_grad = contract_first(grad_branch, mixed_low).astype(jnp.bfloat16)
    grad_mixed_low = jnp.dot(
        grad_branch, output_turned, preferred_element_type=jnp.float32
    ).astype(jnp.bfloat16)
    rest_grads = [output_grad, up_grad, router_grad, down_grad]
    rest_shared = [True, False, False, False]
    if paired:
        wide = (tok_rows, H * DH)
        sums, (lead_back, grad_value_all) = scatter_call(
            attend_back_kernel,
            rest_grads,
            rest_shared,
            REST_SCATTER,
            3,
            list(kept[:7])
            + [grad_mixed_low, value_flat, both_gates, sigs, cos_wide, sin_wide, limits],
            [
                jax.ShapeDtypeStruct((tok_rows, 2 * H * DH + 128), low),
                jax.ShapeDtypeStruct((tok_rows, gated * DH), low),
            ],
            [pltpu.SemaphoreType.DMA((2,))] * 2
            + [pltpu.VMEM(wide, full)] * 2
            + [pltpu.VMEM((tok_rows, 128), full)]
            + [pltpu.VMEM(wide, low)] * 4,
        )
    else:
        sums = scatter_parts(rest_grads, rest_shared, REST_SCATTER, 3)
        grad_mixed = grad_mixed_low.astype(jnp.float32).reshape(tok_rows, H, AEXP, DH)
        grad_attended = jnp.sum(grad_mixed * output_gates[..., None], axis=2).astype(jnp.bfloat16)
        grad_output_gates = jnp.sum(grad_mixed * attended[:, :, None, :], axis=3)
        query_grads = []
        key_grads = []
        value_grads = []
        for head_idx in range(H):
            scores = head_scores(head_idx)
            probs_full = jnp.exp(scores - lse_list[head_idx])
            probs_low = probs_full.astype(jnp.bfloat16)
            grad_probs = jnp.einsum(
                "qd,kd->qk",
                grad_attended[:, head_idx],
                values_all[:, head_idx],
                preferred_element_type=jnp.float32,
            )
            grad_scores = (
                probs_full * (grad_probs - jnp.sum(probs_full * grad_probs, axis=1, keepdims=True))
            ).astype(jnp.bfloat16)
            query_grads.append(
                jnp.dot(grad_scores, keys_all[:, head_idx], preferred_element_type=jnp.float32)
            )
            key_grads.append(contract_first(grad_scores, query_rot[:, head_idx]))
            value_grads.append(contract_first(probs_low, grad_attended[:, head_idx]))
        grad_queries = jnp.stack(query_grads, axis=1)
        key_grads_all = jnp.stack(key_grads, axis=1)
        value_grads_all = jnp.stack(value_grads, axis=1)
        grad_key_rot = key_grads_all[:tok_rows]
        grad_values = value_grads_all[:tok_rows]
        for offset in range(1, key_span):
            back_keys, back_values = (
                shifted(
                    key_grads_all[offset * tok_rows : (offset + 1) * tok_rows].astype(jnp.bfloat16),
                    "col",
                    -offset,
                ).astype(jnp.float32),
                shifted(
                    value_grads_all[offset * tok_rows : (offset + 1) * tok_rows].astype(jnp.bfloat16),
                    "col",
                    -offset,
                ).astype(jnp.float32),
            )
            grad_key_rot = grad_key_rot + back_keys
            grad_values = grad_values + back_values
        grad_value_all = (
            (grad_values[:, :, None, :] * value_gates[..., None])
            .astype(jnp.bfloat16)
            .reshape(tok_rows, gated * DH)
        )
        grad_value_gates = jnp.sum(value_all * grad_values[:, :, None, :], axis=3)
        grad_query_raw = (
            unrotate(grad_queries * query_scale, cosine, sines)
            .astype(jnp.bfloat16)
            .reshape(tok_rows, H * DH)
        )
        grad_key_raw = (
            unrotate(grad_key_rot, cosine, sines).astype(jnp.bfloat16).reshape(tok_rows, H * DH)
        )
        grad_route = jnp.concatenate(
            [
                (grad_value_gates * chosen * value_sig * (1.0 - value_sig)).reshape(tok_rows, gated),
                (grad_output_gates * chosen * output_sig * (1.0 - output_sig)).reshape(tok_rows, gated),
            ],
            axis=1,
        ).astype(jnp.bfloat16)
        lead_back = padded(
            jnp.concatenate([grad_query_raw, grad_key_raw, grad_route], axis=1), 2 * H * DH + 128
        )
    output_turned_sum, up_sum, router_sum, down_sum = sums
    value_grad = contract_first(block_input, grad_value_all).astype(jnp.bfloat16)
    grad_norm_one = contract_last(lead_back, lead_full)
    first_gain_part = jnp.sum(grad_norm_one * hat_one, axis=0)
    grad_base = grad_resid + norm_back(grad_norm_one, gain_one, hat_one, inv_one)
    lead_cols = jnp.arange(2 * H * DH + 128, dtype=jnp.int32)[None, :]
    lead_grad = (
        contract_first(normed_low, lead_back)
        + jnp.where(lead_cols == extra_at, first_gain_part[:, None], 0.0)
        + jnp.where(lead_cols == extra_at + 1, second_gain_part[:, None], 0.0)
    ).astype(jnp.bfloat16)
    if paired:
        (lead_sum, value_sum), (input_grad,) = scatter_call(
            finish_kernel,
            [lead_grad, value_grad],
            [True, True],
            LEAD_SCATTER,
            4,
            [grad_value_all, value_full, grad_base],
            [jax.ShapeDtypeStruct(grad_base.shape, full)],
            [],
        )
    else:
        input_grad = grad_base + contract_last(grad_value_all, value_full)
        lead_sum, value_sum = scatter_parts([lead_grad, value_grad], [True, True], LEAD_SCATTER, 4)
    output_sum = output_turned_sum.T
    router_sum = router_sum[:, :local_experts]
    up_out = jnp.transpose(up_sum.reshape(-1, local_experts, hidden_local), (1, 0, 2))
    down_out = jnp.transpose(down_sum.reshape(-1, local_experts, hidden_local), (1, 2, 0))
    query_sum = lead_sum[:, : H * DH]
    key_sum = lead_sum[:, H * DH : 2 * H * DH]
    router_head_sum = lead_sum[:, 2 * H * DH : extra_at]
    first_sum = lead_sum[:, extra_at]
    second_sum = lead_sum[:, extra_at + 1]
    return (
        block_output,
        input_grad,
        first_sum,
        query_sum,
        key_sum,
        value_sum,
        router_head_sum,
        output_sum,
        second_sum,
        router_sum,
        up_out,
        down_out,
    )


def solution(mesh):
    return jax.shard_map(
        shards,
        mesh=mesh,
        in_specs=(
            P(("row", "col"), None),
            P(("row", "col"), None),
            P("row"),
            P(("row", "col"), None, None),
            P("row", None),
            P(("row", "col")),
            P(("row", "col"), None),
            P(("row", "col"), None),
            P(("row", "col"), None),
            P(("row", "col"), None),
            P(None, ("row", "col")),
            P(("row", "col")),
            P("row", "col"),
            P("col", "row", None),
            P("col", None, "row"),
        ),
        out_specs=(
            P(("row", "col"), None),
            P(("row", "col"), None),
            P(("row", "col")),
            P(("row", "col"), None),
            P(("row", "col"), None),
            P(("row", "col"), None),
            P(("row", "col"), None),
            P(None, ("row", "col")),
            P(("row", "col")),
            P("row", "col"),
            P("col", "row", None),
            P("col", None, "row"),
        ),
        check_vma=False,
    )
```
